32 devices in a mesh: ab: 2 (over y), cd: 16 (over z, x, core).
Axes of the slice: x: 2, y: 2, z: 4, core: 2. Of those that a mesh axis runs over, the one named last changes fastest.
Arguments:
- amplitudes: float32 [768, 16384], P('cd', 'ab'), may hold values from -1.25 to 1.25
- driver: float32 [768, 16384], P('cd', 'ab'), may hold values from -6 to 6
- ladder: bfloat16 [16384, 16384], P('ab', 'cd'), may hold values from -0.125 to 0.125
- block_mask: int32 [128, 128], P('ab', 'cd'), may hold values 0 or 1
- pair_list: int32 [768], replicated, may hold values from 0 to 1023, as said below
- occ_energy: float32 [32], replicated, may hold values from -2 to -0.5
- virt_energy: float32 [128], replicated, may hold values from 0.5 to 3
Outputs:
- new_amplitudes: float32 [768, 16384], P('cd', 'ab')
The draws below stay inside these ranges and needn't reach their ends.
Inputs may be any that keep to these rules, and one draw needn't show every extreme that they name: `pair_list`: the entries are distinct occupied pairs i * 32 + j. Rows come in aligned blocks of two: a pair with i != j shares its block with the pair (j, i); pairs with i == j stand two to a block. Pairs 0 and 1023 are always listed.
All inputs are finite; a program needn't handle non-finite values. No bound on the sum of `block_mask` on one device may be relied on, other than what follows from the above.
Results may differ from the reference program's by a relative error of at most 0.008.
Values may be sent and summed in bfloat16 or wider, within the bound.
A program may use at most 128 MiB of HBM per device.

```python
import jax
import jax.numpy as jnp
import numpy as np
from jax import lax

NV = 128
NOCC = 32
M_PAIRS = 768
BLK = 128
ITERS = 2
NP = 16384
N_AB = 2
N_CD = 16


def draw_pair_list(key, part):
    upper_i, upper_j = np.triu_indices(NOCC, 1)
    diag_even = np.arange(0, NOCC, 2)
    diag_odd = np.arange(1, NOCC, 2)
    lead = np.concatenate([upper_i * NOCC + upper_j, diag_even * NOCC + diag_even]).astype(np.int32)
    trail = np.concatenate([upper_j * NOCC + upper_i, diag_odd * NOCC + diag_odd]).astype(np.int32)
    units = lead.shape[0]
    forced = np.zeros((units,), np.int32)
    forced[units - NOCC // 2] = 1
    forced[units - 1] = 1
    lead_table = jnp.asarray(lead)
    trail_table = jnp.asarray(trail)
    scores = jax.random.randint(jax.random.fold_in(key, 11), (units,), 0, 1 << 16)
    scores = (scores + jnp.asarray(forced) * (1 << 17)) * units + jnp.arange(units, dtype=jnp.int32)
    chosen = lax_top(scores, M_PAIRS // 2)
    shuffle = jax.random.permutation(jax.random.fold_in(key, 12), M_PAIRS // 2)
    chosen = chosen[shuffle]
    turn = jax.random.randint(jax.random.fold_in(key, 13), (M_PAIRS // 2,), 0, 2)
    head = jnp.where(turn == 1, trail_table[chosen], lead_table[chosen])
    tail = jnp.where(turn == 1, lead_table[chosen], trail_table[chosen])
    return jnp.stack([head, tail], axis=1).reshape(M_PAIRS).astype(jnp.int32)


def lax_top(scores, count):
    values, indices = jax.lax.top_k(scores, count)
    return indices.astype(jnp.int32)


def touch_ends(entries, key, smallest, largest):
    extent = entries.shape
    index_at = [jax.random.randint(jax.random.fold_in(key, axis), (), 0, extent[axis]) for axis in range(len(extent))]
    entries = entries.at[tuple(index_at)].set(smallest)
    longest = extent.index(max(extent))
    index_at[longest] = (index_at[longest] + 1) % extent[longest]
    return entries.at[tuple(index_at)].set(largest)


def shard_levels(stream_key, dims, cuts, smallest, high):
    gain = 1.0
    for dim, blocks in cuts:
        heights = jax.random.uniform(jax.random.fold_in(jax.random.fold_in(stream_key, 6), dim), (blocks,), jnp.float32, smallest / len(cuts), high / len(cuts))
        gain = gain * jnp.repeat(jnp.exp(heights), dims[dim] // blocks).reshape((-1,) + (1,) * (len(dims) - 1 - dim))
    return gain


def gaussian(key, extent, deviation, reach, cuts=(), held_as=jnp.bfloat16):
    values = deviation * jax.random.normal(key, extent, jnp.float32)
    if cuts:
        values = values * shard_levels(key, extent, cuts, -0.22, 0.18)
    return jnp.clip(values, -reach, reach).astype(held_as)


def setup_inputs(seed: int = 0) -> dict:
    seeds = jax.random.split(jax.random.key(seed), 8)
    amplitudes = gaussian(seeds[0], (M_PAIRS, NP), 0.2, 1.25, ((0, 16), (1, 2)), jnp.float32)
    driver = gaussian(seeds[1], (M_PAIRS, NP), 1.0, 6.0, ((0, 16), (1, 2)), jnp.float32)
    ladder = gaussian(seeds[2], (NP, NP), (NP // 8) ** -0.5, 0.125, ((0, 2), (1, 16)))
    block_mask = touch_ends((jax.random.randint(seeds[3], (NP // BLK, NP // BLK), 0, 100) < 37).astype(jnp.int32), jax.random.fold_in(seeds[3], 1), 0, 1)
    pair_list = draw_pair_list(jax.random.fold_in(seeds[7], 71), 0)
    occ_energy = jnp.clip(jax.random.uniform(seeds[5], (NOCC,), jnp.float32, -2.0, -0.5), -2.0, -0.5)
    virt_energy = jnp.clip(jax.random.uniform(seeds[6], (NV,), jnp.float32, 0.5, 3.0), 0.5, 3.0)
    return {"amplitudes": amplitudes, "driver": driver, "ladder": ladder, "block_mask": block_mask, "pair_list": pair_list, "occ_energy": occ_energy, "virt_energy": virt_energy}


def pair_maps():
    tile = NV // N_AB
    pairs = jnp.arange(NP, dtype=jnp.int32)
    big_a = pairs // (tile * NV)
    big_b = (pairs // (tile * tile)) % N_AB
    inner_a = (pairs // tile) % tile
    inner_b = pairs % tile
    first = big_a * tile + inner_a
    second = big_b * tile + inner_b
    mirror = big_b * (tile * NV) + big_a * (tile * tile) + inner_b * tile + inner_a
    in_block = NP // N_CD
    piece = NP // (N_AB * N_CD)
    slot = pairs // in_block
    source = (pairs % in_block) // piece
    rest = pairs % piece
    position = source * (NP // N_AB) + slot * piece + rest
    return first, second, mirror, position


def reference(amplitudes, driver, ladder, block_mask, pair_list, occ_energy, virt_energy):
    first, second, mirror, position = pair_maps()
    occ_i = pair_list // NOCC
    occ_j = pair_list % NOCC
    denominator = (virt_energy[first] + virt_energy[second])[None, :] - (occ_energy[occ_i] + occ_energy[occ_j])[:, None]
    inverse = jnp.zeros((NOCC * NOCC,), jnp.int32).at[pair_list].set(jnp.arange(M_PAIRS, dtype=jnp.int32))
    mirror_row = inverse[occ_j * NOCC + occ_i]
    out_block = NP // N_AB
    in_block = NP // N_CD
    ladder_rows = ladder.reshape(N_AB, out_block, NP)
    mask_rows = block_mask.reshape(N_AB, out_block // BLK, NP // BLK)
    state = amplitudes
    for step in range(ITERS):
        low = state.astype(jnp.bfloat16)[:, position].astype(jnp.float32)

        def block_product(operands):
            rows_here, mask_here = operands
            masked = rows_here.astype(jnp.float32).reshape(out_block // BLK, BLK, NP // BLK, BLK)
            masked = masked * mask_here.astype(jnp.float32)[:, None, :, None]
            masked = masked.reshape(out_block, NP)

            def one_block(carry, index):
                start = index * in_block
                left = lax.dynamic_slice_in_dim(low, start, in_block, 1)
                right = lax.dynamic_slice_in_dim(masked, start, in_block, 1)
                part = jnp.dot(left, right.T, precision=lax.Precision.HIGHEST)
                return carry + part.astype(jnp.bfloat16).astype(jnp.float32), None

            zeros = jnp.zeros((M_PAIRS, out_block), jnp.float32)
            total, unused = lax.scan(one_block, zeros, jnp.arange(N_CD, dtype=jnp.int32))
            return total

        blocks = lax.map(block_product, (ladder_rows, mask_rows))
        ladder_term = jnp.transpose(blocks, (1, 0, 2)).reshape(M_PAIRS, NP)
        symmetric = ladder_term + ladder_term[mirror_row][:, mirror]
        state = (driver + symmetric) / denominator
    return state
```

```python
import functools

import jax
import jax.numpy as jnp
from jax import lax
from jax.experimental import pallas as pl
from jax.experimental.pallas import tpu as pltpu
from jax.sharding import PartitionSpec as P

NV = 128
NOCC = 32
BLK = 128
ITERS = 2
STRIP = 16
MESH = pl.DeviceIdType.MESH
NT = (((1,), (1,)), ((), ()))


def flip_tiles(tiles, tile_width):
    row_count, tile_count = tiles.shape[:2]
    turned = jnp.swapaxes(tiles.reshape(row_count, tile_count, tile_width, tile_width), 2, 3)
    return turned.reshape(row_count, tile_count * tile_width * tile_width)


def bit_of(index, bit):
    return lax.rem(index // (1 << bit), 2)


def flip_bit(index, bit):
    return index + (1 - 2 * bit_of(index, bit)) * (1 << bit)


def ladder_kernel(
    bits, chunks, diag_chunks, width,
    low_ref, swap_ref, straight_ref, mirrored_ref, out_ref,
    straight, mirrored, *rest,
):
    held = rest[: bits + 1]
    load_sem, mirror_sem, send_sem, recv_sem = rest[bits + 1 :]
    ab = lax.axis_index("ab")
    cd = lax.axis_index("cd")
    rows = out_ref.shape[0]
    own = [bit_of(cd, bit) for bit in range(bits)]
    partner = [(ab, flip_bit(cd, bit)) for bit in range(bits)]

    def at(stage, chunk, which):
        lead = (slice(None),) * (bits - 1 - stage)
        return held[stage].at[(chunk,) + lead + (which,)]

    def copy(stage, chunk):
        return pltpu.make_async_remote_copy(
            src_ref=at(stage, chunk, 1 - own[stage]),
            dst_ref=held[stage + 1].at[chunk],
            send_sem=send_sem.at[stage, chunk],
            recv_sem=recv_sem.at[stage, chunk],
            device_id=partner[stage],
            device_id_type=MESH,
        )

    def load_straight(chunk):
        start = pl.multiple_of(chunk * width, width)
        return pltpu.make_async_copy(
            straight_ref.at[pl.ds(start, width)], straight.at[chunk], load_sem.at[chunk]
        )

    def load_mirrored(chunk):
        start = pl.multiple_of(chunk * width, width)
        return pltpu.make_async_copy(
            mirrored_ref.at[pl.ds(start, width)], mirrored.at[chunk], mirror_sem.at[chunk]
        )

    @pl.loop(0, diag_chunks)
    def _(chunk):
        load_straight(chunk).start()
        load_mirrored(chunk).start()

    @pl.loop(diag_chunks, chunks)
    def _(chunk):
        load_straight(chunk).start()

    barrier = pltpu.get_barrier_semaphore()
    for device in partner:
        pl.semaphore_signal(barrier, inc=1, device_id=device, device_id_type=MESH)
    pl.semaphore_wait(barrier, bits)

    def put(chunk, product):
        value = product.astype(jnp.bfloat16)
        for block in range(1 << bits):
            index = tuple((block >> (bits - 1 - axis)) & 1 for axis in range(bits))
            held[0][(chunk,) + index] = value[block * rows : (block + 1) * rows]

    @pl.loop(0, chunks + 2 * bits)
    def _(step):
        @pl.when(step < diag_chunks)
        def _():
            load_straight(step).wait()
            load_mirrored(step).wait()
            total = lax.dot_general(
                low_ref[...], straight[step], NT, preferred_element_type=jnp.float32
            )
            total += lax.dot_general(
                swap_ref[...], mirrored[step], NT, preferred_element_type=jnp.float32
            )
            put(step, total)
            copy(0, step).start()

        @pl.when((step >= diag_chunks) & (step < chunks))
        def _():
            load_straight(step).wait()
            put(
                step,
                lax.dot_general(
                    low_ref[...], straight[step], NT, preferred_element_type=jnp.float32
                ),
            )
            copy(0, step).start()

        for stage in range(bits):
            chunk = step - (2 * stage + 1)

            @pl.when((chunk >= 0) & (chunk < chunks))
            def _():
                copy(stage, chunk).wait_recv()
                mine = at(stage, chunk, own[stage])[...].astype(jnp.float32)
                total = held[stage + 1][chunk].astype(jnp.float32) + mine
                if stage < bits - 1:
                    held[stage + 1][chunk] = total.astype(jnp.bfloat16)
                    copy(stage + 1, chunk).start()
                else:
                    out_ref[:, pl.ds(pl.multiple_of(chunk * width, width), width)] = total

    @pl.loop(0, chunks)
    def _(chunk):
        for stage in range(bits):
            copy(stage, chunk).wait_send()


def ladder_sums(low, swapped, straight, mirrored, rows, width):
    count = low.shape[0] // rows
    bits = count.bit_length() - 1
    depth = low.shape[1]
    chunks = straight.shape[0] // width
    diag_chunks = mirrored.shape[0] // width
    held = [
        pltpu.VMEM((chunks,) + (2,) * (bits - stage) + (rows, width), jnp.bfloat16)
        for stage in range(bits + 1)
    ]
    return pl.pallas_call(
        functools.partial(ladder_kernel, bits, chunks, diag_chunks, width),
        out_shape=jax.ShapeDtypeStruct((rows, chunks * width), jnp.float32),
        in_specs=[pl.BlockSpec(memory_space=pltpu.VMEM)] * 2
        + [pl.BlockSpec(memory_space=pl.ANY)] * 2,
        out_specs=pl.BlockSpec(memory_space=pltpu.VMEM),
        scratch_shapes=[
            pltpu.VMEM((chunks, width, depth), jnp.bfloat16),
            pltpu.VMEM((diag_chunks, width, depth), jnp.bfloat16),
            *held,
            pltpu.SemaphoreType.DMA((chunks,)),
            pltpu.SemaphoreType.DMA((diag_chunks,)),
            pltpu.SemaphoreType.DMA((bits, chunks)),
            pltpu.SemaphoreType.DMA((bits, chunks)),
        ],
        compiler_params=pltpu.CompilerParams(
            collective_id=0, has_side_effects=True, vmem_limit_bytes=58 * 2**20
        ),
    )(low, swapped, straight, mirrored)


def body(amplitudes, driver, ladder, block_mask, pair_list, occ_energy, virt_energy):
    ab_count = lax.axis_size("ab")
    ab_index = lax.axis_index("ab")
    cd_index = lax.axis_index("cd")
    rows_dev, cols_dev = amplitudes.shape
    out_rows, in_cols = ladder.shape
    tile_width = NV // ab_count
    tile_area = tile_width * tile_width
    strip = min(STRIP, tile_width)
    strips = tile_width // strip
    diag_cols = sum(strip * (tile_width - s * strip) for s in range(strips))
    width = min(512, tile_area)

    weights = ladder.reshape(out_rows // BLK, BLK, in_cols // BLK, BLK)
    weights = (weights * block_mask.astype(jnp.bfloat16)[:, None, :, None]).reshape(
        ab_count, tile_width, tile_width, in_cols
    )
    diag_tile = lax.dynamic_index_in_dim(weights, ab_index, 0, keepdims=False)

    def pack(tile):
        return jnp.concatenate(
            [
                tile[s * strip : (s + 1) * strip, s * strip :].reshape(-1, in_cols)
                for s in range(strips)
            ]
        )

    others = [
        lax.dynamic_index_in_dim(
            weights, lax.rem(ab_index + j, ab_count), 0, keepdims=False
        ).reshape(tile_area, in_cols)
        for j in range(1, ab_count)
    ]
    straight = jnp.concatenate([pack(diag_tile)] + others)
    mirrored = pack(jnp.swapaxes(diag_tile, 0, 1))

    pairs_local = ab_index * cols_dev + jnp.arange(cols_dev, dtype=jnp.int32)
    big_a = pairs_local // (tile_width * NV)
    big_b = pairs_local // tile_area % ab_count
    first = big_a * tile_width + pairs_local // tile_width % tile_width
    second = big_b * tile_width + pairs_local % tile_width
    virt_index = jnp.arange(NV, dtype=jnp.int32)
    picks = (first[:, None] == virt_index).astype(jnp.float32) + (
        second[:, None] == virt_index
    ).astype(jnp.float32)
    col_energy = jnp.dot(picks, virt_energy, precision=lax.Precision.HIGHEST)
    row_pairs = lax.dynamic_slice_in_dim(pair_list, cd_index * rows_dev, rows_dev)
    occ_index = jnp.arange(NOCC, dtype=jnp.int32)
    occ_picks = (row_pairs[:, None] // NOCC == occ_index).astype(jnp.float32)
    occ_picks = occ_picks + (row_pairs[:, None] % NOCC == occ_index).astype(jnp.float32)
    row_energy = jnp.dot(occ_picks, occ_energy, precision=lax.Precision.HIGHEST)
    denominator = col_energy[None, :] - row_energy[:, None]

    def swap_matrix(listed):
        diagonal = listed // NOCC == listed % NOCC
        index = jnp.arange(listed.shape[0], dtype=jnp.int32)
        mirror_row = jnp.where(diagonal, index, index ^ 1)
        return (mirror_row[:, None] == index).astype(jnp.bfloat16)

    row_swap = swap_matrix(row_pairs)
    all_swap = swap_matrix(pair_list)

    def spread(packed):
        pieces, start = [], 0
        for s in range(strips):
            wide = tile_width - s * strip
            piece = packed[:, start : start + strip * wide].reshape(rows_dev, strip, wide)
            start += strip * wide
            piece = jnp.concatenate([0.5 * piece[:, :, :strip], piece[:, :, strip:]], axis=2)
            pieces.append(jnp.pad(piece, ((0, 0), (0, 0), (s * strip, 0))))
        return jnp.concatenate(pieces, axis=1).reshape(rows_dev, tile_area)

    state = amplitudes
    for step in range(ITERS):
        rounded = state.astype(jnp.bfloat16)
        regrouped = lax.all_to_all(rounded, "cd", split_axis=1, concat_axis=0, tiled=True)
        low = lax.all_gather(regrouped, "ab", axis=1, tiled=True)
        swapped_low = jnp.dot(all_swap, low, preferred_element_type=jnp.float32)
        sums = ladder_sums(
            low, swapped_low.astype(jnp.bfloat16), straight, mirrored, rows_dev, width
        )
        parts = [spread(sums[:, :diag_cols])]
        for j in range(1, ab_count):
            start = diag_cols + (j - 1) * tile_area
            parts.append(sums[:, start : start + tile_area])
        placed = jnp.concatenate(parts, axis=1)
        received = jnp.roll(placed.reshape(rows_dev, ab_count, tile_area), ab_index, axis=1)
        received = received.reshape(rows_dev, cols_dev)
        swapped = jnp.dot(
            row_swap, received.astype(jnp.bfloat16), preferred_element_type=jnp.float32
        )
        tiles = lax.all_to_all(
            swapped.astype(jnp.bfloat16).reshape(rows_dev, ab_count, tile_area),
            "ab",
            split_axis=1,
            concat_axis=1,
            tiled=True,
        )
        symmetric = received + flip_tiles(tiles, tile_width).astype(jnp.float32)
        state = (driver + symmetric) / denominator
    return state


def solution(mesh):
    placed = (P("cd", "ab"), P("cd", "ab"), P("ab", "cd"), P("ab", "cd"), P(), P(), P())
    return jax.shard_map(body, mesh=mesh, in_specs=placed, out_specs=P("cd", "ab"), check_vma=False)
```

```python
import functools

import jax
import jax.numpy as jnp
from jax import lax
from jax.experimental import pallas as pl
from jax.experimental.pallas import tpu as pltpu
from jax.sharding import PartitionSpec as P

NV = 128
NOCC = 32
BLK = 128
ITERS = 2
STRIP = 16
MESH = pl.DeviceIdType.MESH
NT = (((1,), (1,)), ((), ()))


def flip_tiles(tiles, tile_width):
    row_count, tile_count = tiles.shape[:2]
    turned = jnp.swapaxes(tiles.reshape(row_count, tile_count, tile_width, tile_width), 2, 3)
    return turned.reshape(row_count, tile_count * tile_width * tile_width)


def bit_of(index, bit):
    return lax.rem(index // (1 << bit), 2)


def flip_bit(index, bit):
    return index + (1 - 2 * bit_of(index, bit)) * (1 << bit)


def ladder_kernel(
    bits, chunks, diag_chunks, width,
    low_ref, swap_ref, straight_ref, mirrored_ref, out_ref,
    straight, mirrored, *rest,
):
    held = rest[: bits + 1]
    load_sem, mirror_sem, send_sem, recv_sem = rest[bits + 1 :]
    ab = lax.axis_index("ab")
    cd = lax.axis_index("cd")
    rows = out_ref.shape[0]
    own = [bit_of(cd, bit) for bit in range(bits)]
    partner = [(ab, flip_bit(cd, bit)) for bit in range(bits)]

    def at(stage, chunk, which):
        lead = (slice(None),) * (bits - 1 - stage)
        return held[stage].at[(chunk,) + lead + (which,)]

    def copy(stage, chunk):
        return pltpu.make_async_remote_copy(
            src_ref=at(stage, chunk, 1 - own[stage]),
            dst_ref=held[stage + 1].at[chunk],
            send_sem=send_sem.at[stage, chunk],
            recv_sem=recv_sem.at[stage, chunk],
            device_id=partner[stage],
            device_id_type=MESH,
        )

    def load_straight(chunk):
        start = pl.multiple_of(chunk * width, width)
        return pltpu.make_async_copy(
            straight_ref.at[pl.ds(start, width)], straight.at[chunk], load_sem.at[chunk]
        )

    def load_mirrored(chunk):
        start = pl.multiple_of(chunk * width, width)
        return pltpu.make_async_copy(
            mirrored_ref.at[pl.ds(start, width)], mirrored.at[chunk], mirror_sem.at[chunk]
        )

    @pl.loop(0, diag_chunks)
    def _(chunk):
        load_straight(chunk).start()
        load_mirrored(chunk).start()

    @pl.loop(diag_chunks, chunks)
    def _(chunk):
        load_straight(chunk).start()

    barrier = pltpu.get_barrier_semaphore()
    for device in partner:
        pl.semaphore_signal(barrier, inc=1, device_id=device, device_id_type=MESH)
    pl.semaphore_wait(barrier, bits)

    def put(chunk, product):
        value = product.astype(jnp.bfloat16)
        for block in range(1 << bits):
            index = tuple((block >> (bits - 1 - axis)) & 1 for axis in range(bits))
            held[0][(chunk,) + index] = value[block * rows : (block + 1) * rows]

    @pl.loop(0, chunks + 2 * bits)
    def _(step):
        @pl.when(step < diag_chunks)
        def _():
            load_straight(step).wait()
            load_mirrored(step).wait()
            total = lax.dot_general(
                low_ref[...], straight[step], NT, preferred_element_type=jnp.float32
            )
            total += lax.dot_general(
                swap_ref[...], mirrored[step], NT, preferred_element_type=jnp.float32
            )
            put(step, total)
            copy(0, step).start()

        @pl.when((step >= diag_chunks) & (step < chunks))
        def _():
            load_straight(step).wait()
            put(
                step,
                lax.dot_general(
                    low_ref[...], straight[step], NT, preferred_element_type=jnp.float32
                ),
            )
            copy(0, step).start()

        for stage in range(bits):
            chunk = step - (2 * stage + 1)

            @pl.when((chunk >= 0) & (chunk < chunks))
            def _():
                copy(stage, chunk).wait_recv()
                mine = at(stage, chunk, own[stage])[...].astype(jnp.float32)
                total = held[stage + 1][chunk].astype(jnp.float32) + mine
                if stage < bits - 1:
                    held[stage + 1][chunk] = total.astype(jnp.bfloat16)
                    copy(stage + 1, chunk).start()
                else:
                    out_ref[:, pl.ds(pl.multiple_of(chunk * width, width), width)] = total

    @pl.loop(0, chunks)
    def _(chunk):
        for stage in range(bits):
            copy(stage, chunk).wait_send()


def ladder_sums(low, swapped, straight, mirrored, rows, width):
    count = low.shape[0] // rows
    bits = count.bit_length() - 1
    depth = low.shape[1]
    chunks = straight.shape[0] // width
    diag_chunks = mirrored.shape[0] // width
    held = [
        pltpu.VMEM((chunks,) + (2,) * (bits - stage) + (rows, width), jnp.bfloat16)
        for stage in range(bits + 1)
    ]
    return pl.pallas_call(
        functools.partial(ladder_kernel, bits, chunks, diag_chunks, width),
        out_shape=jax.ShapeDtypeStruct((rows, chunks * width), jnp.float32),
        in_specs=[pl.BlockSpec(memory_space=pltpu.VMEM)] * 2
        + [pl.BlockSpec(memory_space=pl.ANY)] * 2,
        out_specs=pl.BlockSpec(memory_space=pltpu.VMEM),
        scratch_shapes=[
            pltpu.VMEM((chunks, width, depth), jnp.bfloat16),
            pltpu.VMEM((diag_chunks, width, depth), jnp.bfloat16),
            *held,
            pltpu.SemaphoreType.DMA((chunks,)),
            pltpu.SemaphoreType.DMA((diag_chunks,)),
            pltpu.SemaphoreType.DMA((bits, chunks)),
            pltpu.SemaphoreType.DMA((bits, chunks)),
        ],
        compiler_params=pltpu.CompilerParams(
            collective_id=0, has_side_effects=True, vmem_limit_bytes=58 * 2**20
        ),
    )(low, swapped, straight, mirrored)


def iteration_kernel(
    bits, width, strip, rows, half,
    state_ref, diagonal_ref, weight_ref, turned_ref, sums_ref, other_ref,
    low, straight, mirrored, outer, part, part_y, *rest,
):
    held = (part,) + rest[:bits]
    final, landed = rest[bits : bits + 2]
    (
        load_sem, self_sem, a_send, a_recv, b_send, b_recv,
        core_send, core_recv, y_send, y_recv, send_sem, recv_sem, last_send, last_recv,
    ) = rest[bits + 2 :]
    ab = lax.axis_index("ab")
    cd = lax.axis_index("cd")
    count = 1 << bits
    tile_width = weight_ref.shape[1]
    depth = weight_ref.shape[3]
    piece = depth // 2
    keeps = outer.shape[0] // (2 * width)
    diags = keeps + 1
    products = 3 * keeps + 1
    finals = diags + keeps
    own = [bit_of(cd, bit) for bit in range(bits)]
    partner = [(ab, flip_bit(cd, bit)) for bit in range(bits)]
    across = (1 - ab, cd)

    def remote(src, dst, send, recv, device):
        return pltpu.make_async_remote_copy(
            src_ref=src, dst_ref=dst, send_sem=send, recv_sem=recv,
            device_id=device, device_id_type=MESH,
        )

    for s in range(tile_width // strip):
        wide = tile_width - s * strip
        base = sum(strip * (tile_width - r * strip) for r in range(s))

        @pl.loop(0, strip)
        def _(x):
            rows_to = pl.ds(pl.multiple_of(base + x * wide, strip), wide)
            rows_from = pl.ds(s * strip, wide)
            pltpu.make_async_copy(
                weight_ref.at[ab, s * strip + x, rows_from], straight.at[rows_to], load_sem.at[0]
            ).start()
            pltpu.make_async_copy(
                turned_ref.at[ab, s * strip + x, rows_from], mirrored.at[rows_to], load_sem.at[1]
            ).start()

    @pl.loop(0, tile_width)
    def _(x):
        side = lax.rem(x // half + ab, 2)
        kept = pl.ds(pl.multiple_of(side * half, half), half)
        sent = pl.ds(pl.multiple_of((1 - side) * half, half), half)
        to = pl.multiple_of(x * half, half)
        pltpu.make_async_copy(
            weight_ref.at[1 - ab, x, kept], outer.at[pl.ds(to, half)], load_sem.at[2]
        ).start()
        pltpu.make_async_copy(
            turned_ref.at[1 - ab, x, sent],
            outer.at[pl.ds(to + tile_width * half, half)],
            load_sem.at[2],
        ).start()

    barrier = pltpu.get_barrier_semaphore()

    @pl.loop(1, count)
    def _(j):
        pl.semaphore_signal(
            barrier, inc=1, device_id=(ab, lax.rem(cd + j, count)), device_id_type=MESH
        )

    pl.semaphore_signal(barrier, inc=1, device_id=across, device_id_type=MESH)
    pl.semaphore_wait(barrier, count)

    def rows_of(source):
        return pl.ds(pl.multiple_of(source * rows, rows), rows)

    def cols_of(side):
        return pl.ds(pl.multiple_of(side * piece, piece), piece)

    def scatter(target, source):
        return remote(
            state_ref.at[:, pl.ds(pl.multiple_of(target * piece, piece), piece)],
            low.at[0, rows_of(source), cols_of(ab)],
            a_send.at[target], a_recv.at[source], (ab, target),
        )

    def forward(source, side):
        block = low.at[0, rows_of(source), cols_of(side)]
        return remote(block, block, b_send.at[source], b_recv.at[source], across)

    stay = pltpu.make_async_copy(
        state_ref.at[:, pl.ds(pl.multiple_of(cd * piece, piece), piece)],
        low.at[0, rows_of(cd), cols_of(ab)],
        self_sem,
    )
    stay.start()

    @pl.loop(0, count)
    def _(i):
        j = lax.rem(i + count // 2, count)

        @pl.when(j != 0)
        def _():
            scatter(lax.rem(cd + j, count), cd).start()

    stay.wait()
    forward(cd, ab).start()

    @pl.loop(0, count)
    def _(i):
        j = lax.rem(i + count // 2, count)

        @pl.when(j != 0)
        def _():
            source = lax.rem(cd + count - j, count)
            scatter(cd, source).wait_recv()
            forward(source, ab).start()

    pltpu.make_async_copy(straight, straight, load_sem.at[0]).wait()
    pltpu.make_async_copy(mirrored, mirrored, load_sem.at[1]).wait()
    pltpu.make_async_copy(outer, outer, load_sem.at[2]).wait()

    @pl.loop(0, count)
    def _(i):
        j = lax.rem(i + count // 2, count)
        source = lax.rem(cd + count - j, count)
        forward(source, 1 - ab).wait_recv()

    odd = lax.rem(lax.broadcasted_iota(jnp.int32, (rows, 128), 0), 2) == 1

    @pl.loop(0, count)
    def _(source):
        at = rows_of(source)
        same = diagonal_ref[at, :] != 0
        for lane in range(0, depth, 128):
            value = low[0, at, lane : lane + 128].astype(jnp.float32)
            other = jnp.where(odd, pltpu.roll(value, 1, 0), pltpu.roll(value, rows - 1, 0))
            low[1, at, lane : lane + 128] = jnp.where(same, value, other).astype(jnp.bfloat16)

    def at(stage, index, which):
        lead = (slice(None),) * (bits - 1 - stage)
        return held[stage].at[(index,) + lead + (which,)]

    def place(q):
        turn = q // 2
        diag = jnp.where(turn == keeps, 3 * keeps, 3 * turn + 1)
        return jnp.where(lax.rem(q, 2) == 0, diag, 3 * turn + 2)

    def core_copy(u):
        return remote(
            at(0, u, 1 - own[0]), held[1].at[u], core_send.at[u], core_recv.at[u], partner[0]
        )

    def y_copy(j):
        return remote(held[1].at[3 * j], part_y.at[j], y_send.at[j], y_recv.at[j], across)

    def stage_copy(stage, q):
        source = at(1, place(q), 1 - own[1]) if stage == 1 else at(stage, q, 1 - own[stage])
        return remote(
            source, held[stage + 1].at[q],
            send_sem.at[stage - 1, q], recv_sem.at[stage - 1, q], partner[stage],
        )

    def last_copy(j):
        return remote(final.at[j], landed.at[j], last_send.at[j], last_recv.at[j], across)

    def put(u, product):
        value = product.astype(jnp.bfloat16)
        for block in range(count):
            index = tuple((block >> (bits - 1 - axis)) & 1 for axis in range(bits))
            part[(u,) + index] = value[block * rows : (block + 1) * rows]

    def rows_at(start):
        return pl.ds(pl.multiple_of(start, width), width)

    def dot(left, right):
        return lax.dot_general(left, right, NT, preferred_element_type=jnp.float32)

    y_lag = 7
    lags = [5 + 2 * s for s in range(bits - 1)]

    @pl.loop(0, 2 * (finals - 1) + lags[-1] + 1)
    def _(step):
        turn = step // 3
        kind = lax.rem(step, 3)
        is_diag = ((kind == 1) & (step < 3 * keeps)) | (step == 3 * keeps)

        @pl.when(is_diag)
        def _():
            total = dot(low[0], straight[rows_at(turn * width)])
            put(step, total + dot(low[1], mirrored[rows_at(turn * width)]))
            core_copy(step).start()

        @pl.when((kind != 1) & (step < 3 * keeps))
        def _():
            sent = 1 - kind // 2
            put(step, dot(low[sent], outer[rows_at((sent * keeps + turn) * width)]))
            core_copy(step).start()

        u = step - 1

        @pl.when((u >= 0) & (u < products))
        def _():
            core_copy(u).wait_recv()
            held[1][u] = held[1][u] + at(0, u, own[0])[...]
            u_kind = lax.rem(u, 3)

            @pl.when((u_kind == 1) | (u == 3 * keeps))
            def _():
                stage_copy(1, 2 * (u // 3)).start()

            @pl.when((u_kind == 0) & (u < 3 * keeps))
            def _():
                y_copy(u // 3).start()

        v = step - y_lag

        @pl.when((v >= 0) & (lax.rem(v + 3, 3) == 0) & (v < 3 * keeps))
        def _():
            y_copy(v // 3).wait_recv()
            held[1][v + 2] = held[1][v + 2] + part_y[v // 3]
            stage_copy(1, 2 * (v // 3) + 1).start()

        for stage in range(1, bits):
            w = step - lags[stage - 1]
            q = w // 2

            @pl.when((w >= 0) & (lax.rem(w + 2, 2) == 0) & (q < finals))
            def _():
                stage_copy(stage, q).wait_recv()
                index = place(q) if stage == 1 else q
                mine = at(stage, index, own[stage])[...]
                if stage < bits - 1:
                    held[stage + 1][q] = held[stage + 1][q] + mine
                    stage_copy(stage + 1, q).start()
                else:
                    total = held[stage + 1][q].astype(jnp.float32) + mine.astype(jnp.float32)
                    kept = lax.rem(q, 2) == 1
                    start = jnp.where(kept, diags + q // 2, q // 2) * width
                    sums_ref[:, rows_at(start)] = total

                    @pl.when(kept)
                    def _():
                        final[q // 2] = total.astype(jnp.bfloat16)
                        last_copy(q // 2).start()

    for j in range(keeps):
        last_copy(j).wait_recv()
        other_ref[:, j * width : (j + 1) * width] = landed[j]

    @pl.loop(0, count)
    def _(i):
        @pl.when(i != cd)
        def _():
            scatter(i, cd).wait_send()

        forward(i, ab).wait_send()

    @pl.loop(0, products)
    def _(u):
        core_copy(u).wait_send()

    @pl.loop(0, keeps)
    def _(j):
        y_copy(j).wait_send()
        last_copy(j).wait_send()

    @pl.loop(0, finals)
    def _(q):
        for stage in range(1, bits):
            stage_copy(stage, q).wait_send()


def iteration_sums(state, diagonal, weights, turned, width, strip):
    rows = state.shape[0]
    count = diagonal.shape[0] // rows
    bits = count.bit_length() - 1
    tile_width, depth = weights.shape[1], weights.shape[3]
    half = tile_width // 2
    diag_cols = sum(
        strip * (tile_width - s * strip) for s in range(tile_width // strip)
    )
    keeps = tile_width * half // width
    products, finals = 3 * keeps + 1, 2 * keeps + 1
    dma = pltpu.SemaphoreType.DMA
    block = (rows, width)
    return pl.pallas_call(
        functools.partial(iteration_kernel, bits, width, strip, rows, half),
        out_shape=(
            jax.ShapeDtypeStruct((rows, finals * width), jnp.float32),
            jax.ShapeDtypeStruct((rows, keeps * width), jnp.bfloat16),
        ),
        in_specs=[pl.BlockSpec(memory_space=pltpu.VMEM)] * 2
        + [pl.BlockSpec(memory_space=pl.ANY)] * 2,
        out_specs=[pl.BlockSpec(memory_space=pltpu.VMEM)] * 2,
        scratch_shapes=[
            pltpu.VMEM((2, count * rows, depth), jnp.bfloat16),
            pltpu.VMEM((diag_cols, depth), jnp.bfloat16),
            pltpu.VMEM((diag_cols, depth), jnp.bfloat16),
            pltpu.VMEM((2 * tile_width * half, depth), jnp.bfloat16),
            pltpu.VMEM((products,) + (2,) * bits + block, jnp.bfloat16),
            pltpu.VMEM((keeps,) + (2,) * (bits - 1) + block, jnp.bfloat16),
            pltpu.VMEM((products,) + (2,) * (bits - 1) + block, jnp.bfloat16),
            *[
                pltpu.VMEM((finals,) + (2,) * (bits - 1 - s) + block, jnp.bfloat16)
                for s in range(1, bits)
            ],
            pltpu.VMEM((keeps,) + block, jnp.bfloat16),
            pltpu.VMEM((keeps,) + block, jnp.bfloat16),
            dma((3,)), dma,
            dma((count,)), dma((count,)), dma((count,)), dma((count,)),
            dma((products,)), dma((products,)), dma((keeps,)), dma((keeps,)),
            dma((bits - 1, finals)), dma((bits - 1, finals)), dma((keeps,)), dma((keeps,)),
        ],
        compiler_params=pltpu.CompilerParams(
            collective_id=1, has_side_effects=True, vmem_limit_bytes=60 * 2**20
        ),
    )(state, diagonal, weights, turned)


def body(amplitudes, driver, ladder, block_mask, pair_list, occ_energy, virt_energy):
    ab_count = lax.axis_size("ab")
    ab_index = lax.axis_index("ab")
    cd_index = lax.axis_index("cd")
    rows_dev, cols_dev = amplitudes.shape
    out_rows, in_cols = ladder.shape
    tile_width = NV // ab_count
    tile_area = tile_width * tile_width
    strip = min(STRIP, tile_width)
    strips = tile_width // strip
    diag_cols = sum(strip * (tile_width - s * strip) for s in range(strips))
    width = min(512, tile_area)

    weights = ladder.reshape(out_rows // BLK, BLK, in_cols // BLK, BLK)
    weights = (weights * block_mask.astype(jnp.bfloat16)[:, None, :, None]).reshape(
        ab_count, tile_width, tile_width, in_cols
    )
    paired = (
        ab_count == 2
        and tile_area % (2 * width) == 0
        and diag_cols == (tile_area // 2 // width + 1) * width
    )
    turned = jnp.swapaxes(weights, 1, 2)
    diag_tile = lax.dynamic_index_in_dim(weights, ab_index, 0, keepdims=False)

    def pack(tile):
        return jnp.concatenate(
            [
                tile[s * strip : (s + 1) * strip, s * strip :].reshape(-1, in_cols)
                for s in range(strips)
            ]
        )

    others = [
        lax.dynamic_index_in_dim(
            weights, lax.rem(ab_index + j, ab_count), 0, keepdims=False
        ).reshape(tile_area, in_cols)
        for j in range(1, ab_count)
    ]
    straight = jnp.concatenate([pack(diag_tile)] + others)
    mirrored = pack(jnp.swapaxes(diag_tile, 0, 1))

    pairs_local = ab_index * cols_dev + jnp.arange(cols_dev, dtype=jnp.int32)
    big_a = pairs_local // (tile_width * NV)
    big_b = pairs_local // tile_area % ab_count
    first = big_a * tile_width + pairs_local // tile_width % tile_width
    second = big_b * tile_width + pairs_local % tile_width
    virt_index = jnp.arange(NV, dtype=jnp.int32)
    picks = (first[:, None] == virt_index).astype(jnp.float32) + (
        second[:, None] == virt_index
    ).astype(jnp.float32)
    col_energy = jnp.dot(picks, virt_energy, precision=lax.Precision.HIGHEST)
    row_pairs = lax.dynamic_slice_in_dim(pair_list, cd_index * rows_dev, rows_dev)
    occ_index = jnp.arange(NOCC, dtype=jnp.int32)
    occ_picks = (row_pairs[:, None] // NOCC == occ_index).astype(jnp.float32)
    occ_picks = occ_picks + (row_pairs[:, None] % NOCC == occ_index).astype(jnp.float32)
    row_energy = jnp.dot(occ_picks, occ_energy, precision=lax.Precision.HIGHEST)
    denominator = col_energy[None, :] - row_energy[:, None]

    def swap_matrix(listed):
        diagonal = listed // NOCC == listed % NOCC
        index = jnp.arange(listed.shape[0], dtype=jnp.int32)
        mirror_row = jnp.where(diagonal, index, index ^ 1)
        return (mirror_row[:, None] == index).astype(jnp.bfloat16)

    row_swap = swap_matrix(row_pairs)
    all_swap = swap_matrix(pair_list)

    def spread(packed):
        pieces, start = [], 0
        for s in range(strips):
            wide = tile_width - s * strip
            piece = packed[:, start : start + strip * wide].reshape(rows_dev, strip, wide)
            start += strip * wide
            piece = jnp.concatenate([0.5 * piece[:, :, :strip], piece[:, :, strip:]], axis=2)
            pieces.append(jnp.pad(piece, ((0, 0), (0, 0), (s * strip, 0))))
        return jnp.concatenate(pieces, axis=1).reshape(rows_dev, tile_area)

    diag_rows = (pair_list // NOCC == pair_list % NOCC).astype(jnp.float32)
    diag_rows = jnp.broadcast_to(diag_rows[:, None], (pair_list.shape[0], 128))
    odd_row = (jnp.arange(rows_dev) % 2 == 1)[:, None]
    same_row = (row_pairs // NOCC == row_pairs % NOCC)[:, None]

    def swap_rows(value):
        above = jnp.concatenate([value[-1:], value[:-1]])
        below = jnp.concatenate([value[1:], value[:1]])
        return jnp.where(same_row, value, jnp.where(odd_row, above, below))

    def symmetric_tiles(sums, other):
        half = tile_width // 2
        diag = spread(sums[:, :diag_cols])
        diag = diag + flip_tiles(swap_rows(diag)[:, None, :], tile_width)
        kept = sums[:, diag_cols:].reshape(rows_dev, 2, half, half)
        came = swap_rows(other).reshape(rows_dev, 2, half, half).swapaxes(2, 3)
        came = jnp.where(ab_index == 1, came, came[:, ::-1]).astype(jnp.float32)
        first_half = jnp.concatenate(
            [
                jnp.where(ab_index == 0, kept[:, 0], came[:, 0]),
                jnp.where(ab_index == 0, came[:, 0], kept[:, 0]),
            ],
            axis=2,
        )
        second_half = jnp.concatenate(
            [
                jnp.where(ab_index == 0, came[:, 1], kept[:, 1]),
                jnp.where(ab_index == 0, kept[:, 1], came[:, 1]),
            ],
            axis=2,
        )
        off = jnp.concatenate([first_half, second_half], axis=1).reshape(rows_dev, tile_area)
        return jnp.concatenate(
            [jnp.where(ab_index == 0, diag, off), jnp.where(ab_index == 0, off, diag)], axis=1
        )

    state = amplitudes
    for step in range(ITERS):
        rounded = state.astype(jnp.bfloat16)
        if paired:
            sums, other = iteration_sums(rounded, diag_rows, weights, turned, width, strip)
            state = (driver + symmetric_tiles(sums, other)) / denominator
            continue
        regrouped = lax.all_to_all(rounded, "cd", split_axis=1, concat_axis=0, tiled=True)
        low = lax.all_gather(regrouped, "ab", axis=1, tiled=True)
        swapped_low = jnp.dot(all_swap, low, preferred_element_type=jnp.float32)
        sums = ladder_sums(
            low, swapped_low.astype(jnp.bfloat16), straight, mirrored, rows_dev, width
        )
        parts = [spread(sums[:, :diag_cols])]
        for j in range(1, ab_count):
            start = diag_cols + (j - 1) * tile_area
            parts.append(sums[:, start : start + tile_area])
        placed = jnp.concatenate(parts, axis=1)
        received = jnp.roll(placed.reshape(rows_dev, ab_count, tile_area), ab_index, axis=1)
        received = received.reshape(rows_dev, cols_dev)
        swapped = jnp.dot(
            row_swap, received.astype(jnp.bfloat16), preferred_element_type=jnp.float32
        )
        tiles = lax.all_to_all(
            swapped.astype(jnp.bfloat16).reshape(rows_dev, ab_count, tile_area),
            "ab",
            split_axis=1,
            concat_axis=1,
            tiled=True,
        )
        symmetric = received + flip_tiles(tiles, tile_width).astype(jnp.float32)
        state = (driver + symmetric) / denominator
    return state


def solution(mesh):
    placed = (P("cd", "ab"), P("cd", "ab"), P("ab", "cd"), P("ab", "cd"), P(), P(), P())
    return jax.shard_map(body, mesh=mesh, in_specs=placed, out_specs=P("cd", "ab"), check_vma=False)
```

```python
import functools

import jax
import jax.numpy as jnp
from jax import lax
from jax.experimental import pallas as pl
from jax.experimental.pallas import tpu as pltpu
from jax.sharding import PartitionSpec as P

NV = 128
NOCC = 32
BLK = 128
ITERS = 2
STRIP = 16
MESH = pl.DeviceIdType.MESH
NT = (((1,), (1,)), ((), ()))


def flip_tiles(tiles, tile_width):
    row_count, tile_count = tiles.shape[:2]
    turned = jnp.swapaxes(tiles.reshape(row_count, tile_count, tile_width, tile_width), 2, 3)
    return turned.reshape(row_count, tile_count * tile_width * tile_width)


def bit_of(index, bit):
    return lax.rem(index // (1 << bit), 2)


def flip_bit(index, bit):
    return index + (1 - 2 * bit_of(index, bit)) * (1 << bit)


def ladder_kernel(
    bits, chunks, diag_chunks, width,
    low_ref, swap_ref, straight_ref, mirrored_ref, out_ref,
    straight, mirrored, *rest,
):
    held = rest[: bits + 1]
    load_sem, mirror_sem, send_sem, recv_sem = rest[bits + 1 :]
    ab = lax.axis_index("ab")
    cd = lax.axis_index("cd")
    rows = out_ref.shape[0]
    own = [bit_of(cd, bit) for bit in range(bits)]
    partner = [(ab, flip_bit(cd, bit)) for bit in range(bits)]

    def at(stage, chunk, which):
        lead = (slice(None),) * (bits - 1 - stage)
        return held[stage].at[(chunk,) + lead + (which,)]

    def copy(stage, chunk):
        return pltpu.make_async_remote_copy(
            src_ref=at(stage, chunk, 1 - own[stage]),
            dst_ref=held[stage + 1].at[chunk],
            send_sem=send_sem.at[stage, chunk],
            recv_sem=recv_sem.at[stage, chunk],
            device_id=partner[stage],
            device_id_type=MESH,
        )

    def load_straight(chunk):
        start = pl.multiple_of(chunk * width, width)
        return pltpu.make_async_copy(
            straight_ref.at[pl.ds(start, width)], straight.at[chunk], load_sem.at[chunk]
        )

    def load_mirrored(chunk):
        start = pl.multiple_of(chunk * width, width)
        return pltpu.make_async_copy(
            mirrored_ref.at[pl.ds(start, width)], mirrored.at[chunk], mirror_sem.at[chunk]
        )

    @pl.loop(0, diag_chunks)
    def _(chunk):
        load_straight(chunk).start()
        load_mirrored(chunk).start()

    @pl.loop(diag_chunks, chunks)
    def _(chunk):
        load_straight(chunk).start()

    barrier = pltpu.get_barrier_semaphore()
    for device in partner:
        pl.semaphore_signal(barrier, inc=1, device_id=device, device_id_type=MESH)
    pl.semaphore_wait(barrier, bits)

    def put(chunk, product):
        value = product.astype(jnp.bfloat16)
        for block in range(1 << bits):
            index = tuple((block >> (bits - 1 - axis)) & 1 for axis in range(bits))
            held[0][(chunk,) + index] = value[block * rows : (block + 1) * rows]

    @pl.loop(0, chunks + 2 * bits)
    def _(step):
        @pl.when(step < diag_chunks)
        def _():
            load_straight(step).wait()
            load_mirrored(step).wait()
            total = lax.dot_general(
                low_ref[...], straight[step], NT, preferred_element_type=jnp.float32
            )
            total += lax.dot_general(
                swap_ref[...], mirrored[step], NT, preferred_element_type=jnp.float32
            )
            put(step, total)
            copy(0, step).start()

        @pl.when((step >= diag_chunks) & (step < chunks))
        def _():
            load_straight(step).wait()
            put(
                step,
                lax.dot_general(
                    low_ref[...], straight[step], NT, preferred_element_type=jnp.float32
                ),
            )
            copy(0, step).start()

        for stage in range(bits):
            chunk = step - (2 * stage + 1)

            @pl.when((chunk >= 0) & (chunk < chunks))
            def _():
                copy(stage, chunk).wait_recv()
                mine = at(stage, chunk, own[stage])[...].astype(jnp.float32)
                total = held[stage + 1][chunk].astype(jnp.float32) + mine
                if stage < bits - 1:
                    held[stage + 1][chunk] = total.astype(jnp.bfloat16)
                    copy(stage + 1, chunk).start()
                else:
                    out_ref[:, pl.ds(pl.multiple_of(chunk * width, width), width)] = total

    @pl.loop(0, chunks)
    def _(chunk):
        for stage in range(bits):
            copy(stage, chunk).wait_send()


def ladder_sums(low, swapped, straight, mirrored, rows, width):
    count = low.shape[0] // rows
    bits = count.bit_length() - 1
    depth = low.shape[1]
    chunks = straight.shape[0] // width
    diag_chunks = mirrored.shape[0] // width
    held = [
        pltpu.VMEM((chunks,) + (2,) * (bits - stage) + (rows, width), jnp.bfloat16)
        for stage in range(bits + 1)
    ]
    return pl.pallas_call(
        functools.partial(ladder_kernel, bits, chunks, diag_chunks, width),
        out_shape=jax.ShapeDtypeStruct((rows, chunks * width), jnp.float32),
        in_specs=[pl.BlockSpec(memory_space=pltpu.VMEM)] * 2
        + [pl.BlockSpec(memory_space=pl.ANY)] * 2,
        out_specs=pl.BlockSpec(memory_space=pltpu.VMEM),
        scratch_shapes=[
            pltpu.VMEM((chunks, width, depth), jnp.bfloat16),
            pltpu.VMEM((diag_chunks, width, depth), jnp.bfloat16),
            *held,
            pltpu.SemaphoreType.DMA((chunks,)),
            pltpu.SemaphoreType.DMA((diag_chunks,)),
            pltpu.SemaphoreType.DMA((bits, chunks)),
            pltpu.SemaphoreType.DMA((bits, chunks)),
        ],
        compiler_params=pltpu.CompilerParams(
            collective_id=0, has_side_effects=True, vmem_limit_bytes=58 * 2**20
        ),
    )(low, swapped, straight, mirrored)


def iteration_kernel(
    bits, width, rows,
    state_ref, diagonal_ref, mask_ref, weight_ref, sums_ref, other_ref,
    low, straight, mirrored, outer, part, part_y, *rest,
):
    held = (part,) + rest[:bits]
    final, landed = rest[bits : bits + 2]
    (
        load_sem, self_sem, a_send, a_recv, b_send, b_recv,
        core_send, core_recv, y_send, y_recv, send_sem, recv_sem, last_send, last_recv,
    ) = rest[bits + 2 :]
    ab = lax.axis_index("ab")
    cd = lax.axis_index("cd")
    count = 1 << bits
    side = straight.shape[1]
    strips = weight_ref.shape[1] // side
    depth = weight_ref.shape[3]
    piece = depth // 2
    keeps = strips
    span = width // (side * side)
    diags = keeps + 1
    products = 3 * keeps + 1
    finals = diags + keeps
    own = [bit_of(cd, bit) for bit in range(bits)]
    partner = [(ab, flip_bit(cd, bit)) for bit in range(bits)]
    across = (1 - ab, cd)

    def remote(src, dst, send, recv, device):
        return pltpu.make_async_remote_copy(
            src_ref=src, dst_ref=dst, send_sem=send, recv_sem=recv,
            device_id=device, device_id_type=MESH,
        )

    def block_of(tile, x, y):
        return weight_ref.at[
            tile,
            pl.ds(pl.multiple_of(x * side, side), side),
            pl.ds(pl.multiple_of(y * side, side), side),
        ]

    def upper(p):
        starts = [sum(strips - r for r in range(s)) for s in range(strips)]
        x = sum((p >= start).astype(jnp.int32) for start in starts[1:])
        start = sum(
            jnp.where(x == s, starts[s], 0) for s in range(strips)
        )
        return x, p - start + x

    def kept_y(p, which):
        return span * lax.rem(p // (span * span) + which, 2) + lax.rem(p, span)

    @pl.loop(0, diags * span)
    def _(p):
        x, y = upper(p)
        pltpu.make_async_copy(block_of(ab, x, y), straight.at[p], load_sem.at[0]).start()
        pltpu.make_async_copy(block_of(ab, y, x), mirrored.at[p], load_sem.at[1]).start()

    @pl.loop(0, keeps * span)
    def _(p):
        pltpu.make_async_copy(
            block_of(1 - ab, p // span, kept_y(p, ab)), outer.at[0, p], load_sem.at[2]
        ).start()
        pltpu.make_async_copy(
            block_of(1 - ab, kept_y(p, 1 - ab), p // span), outer.at[1, p], load_sem.at[3]
        ).start()

    def masked(block, tile, x):
        pairs = side // 2
        mask = mask_ref[tile, pl.ds(pl.multiple_of(x * pairs, pairs), pairs)]
        value = block.reshape(pairs, 2, side, depth) * mask[:, None]
        return value.reshape(side * side, depth)

    area = side * side
    row_at = lax.broadcasted_iota(jnp.int32, (area, area), 0)
    col_at = lax.broadcasted_iota(jnp.int32, (area, area), 1)
    turn_rows = (row_at == lax.rem(col_at, side) * side + col_at // side).astype(jnp.bfloat16)

    def turned(value):
        product = jnp.dot(turn_rows, value, preferred_element_type=jnp.float32)
        return product.astype(jnp.bfloat16).reshape(side, side, depth)

    def prepare_diag(p):
        x, y = upper(p)
        straight[p] = masked(straight[p], ab, x).reshape(side, side, depth)
        mirrored[p] = turned(masked(mirrored[p], ab, y))

    def prepare_outer(p):
        outer[0, p] = masked(outer[0, p], 1 - ab, p // span).reshape(side, side, depth)
        outer[1, p] = turned(masked(outer[1, p], 1 - ab, kept_y(p, 1 - ab)))

    barrier = pltpu.get_barrier_semaphore()

    @pl.loop(1, count)
    def _(j):
        pl.semaphore_signal(
            barrier, inc=1, device_id=(ab, lax.rem(cd + j, count)), device_id_type=MESH
        )

    pl.semaphore_signal(barrier, inc=1, device_id=across, device_id_type=MESH)
    pl.semaphore_wait(barrier, count)

    def rows_of(source):
        return pl.ds(pl.multiple_of(source * rows, rows), rows)

    def cols_of(side):
        return pl.ds(pl.multiple_of(side * piece, piece), piece)

    def scatter(target, source):
        return remote(
            state_ref.at[:, pl.ds(pl.multiple_of(target * piece, piece), piece)],
            low.at[0, rows_of(source), cols_of(ab)],
            a_send.at[target], a_recv.at[source], (ab, target),
        )

    def forward(source, side):
        block = low.at[0, rows_of(source), cols_of(side)]
        return remote(block, block, b_send.at[source], b_recv.at[source], across)

    stay = pltpu.make_async_copy(
        state_ref.at[:, pl.ds(pl.multiple_of(cd * piece, piece), piece)],
        low.at[0, rows_of(cd), cols_of(ab)],
        self_sem,
    )
    stay.start()

    @pl.loop(0, count)
    def _(i):
        j = lax.rem(i + count // 2, count)

        @pl.when(j != 0)
        def _():
            scatter(lax.rem(cd + j, count), cd).start()

    stay.wait()
    forward(cd, ab).start()

    @pl.loop(0, count)
    def _(i):
        j = lax.rem(i + count // 2, count)

        @pl.when(j != 0)
        def _():
            source = lax.rem(cd + count - j, count)
            scatter(cd, source).wait_recv()
            forward(source, ab).start()

        @pl.when(i == 0)
        def _():
            pltpu.make_async_copy(straight, straight, load_sem.at[0]).wait()
            pltpu.make_async_copy(mirrored, mirrored, load_sem.at[1]).wait()

        @pl.when(i < diags * span)
        def _():
            prepare_diag(i)

        late = i - (count - keeps * span)

        @pl.when(late == 0)
        def _():
            pltpu.make_async_copy(outer.at[0], outer.at[0], load_sem.at[2]).wait()
            pltpu.make_async_copy(outer.at[1], outer.at[1], load_sem.at[3]).wait()

        @pl.when(late >= 0)
        def _():
            prepare_outer(late)

    @pl.loop(0, count)
    def _(i):
        j = lax.rem(i + count // 2, count)
        source = lax.rem(cd + count - j, count)
        forward(source, 1 - ab).wait_recv()

    odd = lax.rem(lax.broadcasted_iota(jnp.int32, (rows, 128), 0), 2) == 1

    @pl.loop(0, count)
    def _(source):
        at = rows_of(source)
        same = diagonal_ref[at, :] != 0
        for lane in range(0, depth, 128):
            value = low[0, at, lane : lane + 128].astype(jnp.float32)
            other = jnp.where(odd, pltpu.roll(value, 1, 0), pltpu.roll(value, rows - 1, 0))
            low[1, at, lane : lane + 128] = jnp.where(same, value, other).astype(jnp.bfloat16)

    def at(stage, index, which):
        lead = (slice(None),) * (bits - 1 - stage)
        return held[stage].at[(index,) + lead + (which,)]

    def place(q):
        turn = q // 2
        diag = jnp.where(turn == keeps, 3 * keeps, 3 * turn + 1)
        return jnp.where(lax.rem(q, 2) == 0, diag, 3 * turn + 2)

    def core_copy(u):
        return remote(
            at(0, u, 1 - own[0]), held[1].at[u], core_send.at[u], core_recv.at[u], partner[0]
        )

    def y_copy(j):
        return remote(held[1].at[3 * j], part_y.at[j], y_send.at[j], y_recv.at[j], across)

    def stage_copy(stage, q):
        source = at(1, place(q), 1 - own[1]) if stage == 1 else at(stage, q, 1 - own[stage])
        return remote(
            source, held[stage + 1].at[q],
            send_sem.at[stage - 1, q], recv_sem.at[stage - 1, q], partner[stage],
        )

    def last_copy(j):
        return remote(final.at[j], landed.at[j], last_send.at[j], last_recv.at[j], across)

    def put(u, product):
        value = product.astype(jnp.bfloat16)
        for block in range(count):
            index = tuple((block >> (bits - 1 - axis)) & 1 for axis in range(bits))
            part[(u,) + index] = value[block * rows : (block + 1) * rows]

    def rows_at(start):
        return pl.ds(pl.multiple_of(start, width), width)

    def blocks_at(turn):
        return pl.ds(turn * span, span)

    def dot(left, right):
        return lax.dot_general(left, right, NT, preferred_element_type=jnp.float32)

    y_lag = 7
    lags = [5 + 2 * s for s in range(bits - 1)]

    @pl.loop(0, 2 * (finals - 1) + lags[-1] + 1)
    def _(step):
        turn = step // 3
        kind = lax.rem(step, 3)
        is_diag = ((kind == 1) & (step < 3 * keeps)) | (step == 3 * keeps)

        @pl.when(is_diag)
        def _():
            total = dot(low[0], straight[blocks_at(turn)].reshape(width, depth))
            put(step, total + dot(low[1], mirrored[blocks_at(turn)].reshape(width, depth)))
            core_copy(step).start()

        @pl.when((kind != 1) & (step < 3 * keeps))
        def _():
            sent = 1 - kind // 2
            put(step, dot(low[sent], outer[sent, blocks_at(turn)].reshape(width, depth)))
            core_copy(step).start()

        u = step - 1

        @pl.when((u >= 0) & (u < products))
        def _():
            core_copy(u).wait_recv()
            held[1][u] = held[1][u] + at(0, u, own[0])[...]
            u_kind = lax.rem(u, 3)

            @pl.when((u_kind == 1) | (u == 3 * keeps))
            def _():
                stage_copy(1, 2 * (u // 3)).start()

            @pl.when((u_kind == 0) & (u < 3 * keeps))
            def _():
                y_copy(u // 3).start()

        v = step - y_lag

        @pl.when((v >= 0) & (lax.rem(v + 3, 3) == 0) & (v < 3 * keeps))
        def _():
            y_copy(v // 3).wait_recv()
            held[1][v + 2] = held[1][v + 2] + part_y[v // 3]
            stage_copy(1, 2 * (v // 3) + 1).start()

        for stage in range(1, bits):
            w = step - lags[stage - 1]
            q = w // 2

            @pl.when((w >= 0) & (lax.rem(w + 2, 2) == 0) & (q < finals))
            def _():
                stage_copy(stage, q).wait_recv()
                index = place(q) if stage == 1 else q
                mine = at(stage, index, own[stage])[...]
                if stage < bits - 1:
                    held[stage + 1][q] = held[stage + 1][q] + mine
                    stage_copy(stage + 1, q).start()
                else:
                    total = held[stage + 1][q].astype(jnp.float32) + mine.astype(jnp.float32)
                    kept = lax.rem(q, 2) == 1
                    start = jnp.where(kept, diags + q // 2, q // 2) * width
                    sums_ref[:, rows_at(start)] = total

                    @pl.when(kept)
                    def _():
                        final[q // 2] = total.astype(jnp.bfloat16)
                        last_copy(q // 2).start()

    for j in range(keeps):
        last_copy(j).wait_recv()
        other_ref[:, j * width : (j + 1) * width] = landed[j]

    @pl.loop(0, count)
    def _(i):
        @pl.when(i != cd)
        def _():
            scatter(i, cd).wait_send()

        forward(i, ab).wait_send()

    @pl.loop(0, products)
    def _(u):
        core_copy(u).wait_send()

    @pl.loop(0, keeps)
    def _(j):
        y_copy(j).wait_send()
        last_copy(j).wait_send()

    @pl.loop(0, finals)
    def _(q):
        for stage in range(1, bits):
            stage_copy(stage, q).wait_send()


def iteration_sums(state, diagonal, mask, weights, width):
    rows = state.shape[0]
    count = diagonal.shape[0] // rows
    bits = count.bit_length() - 1
    tile_width, depth = weights.shape[1], weights.shape[3]
    keeps = tile_width // STRIP
    diags = keeps + 1
    span = width // (STRIP * STRIP)
    products, finals = 3 * keeps + 1, 2 * keeps + 1
    dma = pltpu.SemaphoreType.DMA
    block = (rows, width)
    square = (STRIP, STRIP, depth)
    return pl.pallas_call(
        functools.partial(iteration_kernel, bits, width, rows),
        out_shape=(
            jax.ShapeDtypeStruct((rows, finals * width), jnp.float32),
            jax.ShapeDtypeStruct((rows, keeps * width), jnp.bfloat16),
        ),
        in_specs=[pl.BlockSpec(memory_space=pltpu.VMEM)] * 3
        + [pl.BlockSpec(memory_space=pl.ANY)],
        out_specs=[pl.BlockSpec(memory_space=pltpu.VMEM)] * 2,
        scratch_shapes=[
            pltpu.VMEM((2, count * rows, depth), jnp.bfloat16),
            pltpu.VMEM((diags * span,) + square, jnp.bfloat16),
            pltpu.VMEM((diags * span,) + square, jnp.bfloat16),
            pltpu.VMEM((2, keeps * span) + square, jnp.bfloat16),
            pltpu.VMEM((products,) + (2,) * bits + block, jnp.bfloat16),
            pltpu.VMEM((keeps,) + (2,) * (bits - 1) + block, jnp.bfloat16),
            pltpu.VMEM((products,) + (2,) * (bits - 1) + block, jnp.bfloat16),
            *[
                pltpu.VMEM((finals,) + (2,) * (bits - 1 - s) + block, jnp.bfloat16)
                for s in range(1, bits)
            ],
            pltpu.VMEM((keeps,) + block, jnp.bfloat16),
            pltpu.VMEM((keeps,) + block, jnp.bfloat16),
            dma((4,)), dma,
            dma((count,)), dma((count,)), dma((count,)), dma((count,)),
            dma((products,)), dma((products,)), dma((keeps,)), dma((keeps,)),
            dma((bits - 1, finals)), dma((bits - 1, finals)), dma((keeps,)), dma((keeps,)),
        ],
        compiler_params=pltpu.CompilerParams(
            collective_id=1, has_side_effects=True, vmem_limit_bytes=60 * 2**20
        ),
    )(state, diagonal, mask, weights)


def update_kernel(
    strips, side, span,
    sums_ref, other_ref, driver_ref, cols_ref, rows_ref, same_ref, next_ref,
):
    ab = lax.axis_index("ab")
    rows = driver_ref.shape[0]
    area = side * side
    wide = strips * area
    tile_area = strips * wide
    uppers = [(x, y) for x in range(strips) for y in range(x, strips)]

    def iotas(size):
        return (lax.broadcasted_iota(jnp.int32, (size, size), axis) for axis in (0, 1))

    start, end = iotas(area)
    turn = (start == lax.rem(end, side) * side + end // side).astype(jnp.bfloat16)
    start, end = iotas(wide)
    block, inner = lax.rem(end, strips * side) // side, lax.rem(end, side)
    ordered = start == block * area + end // (strips * side) * side + inner
    ordered = ordered.astype(jnp.bfloat16)
    odd = lax.rem(lax.broadcasted_iota(jnp.int32, (rows, area), 0), 2) == 1
    same = jnp.broadcast_to(same_ref[:, 0:1], (rows, area)) != 0

    def swap(value):
        return jnp.where(
            same, value, jnp.where(odd, pltpu.roll(value, 1, 0), pltpu.roll(value, rows - 1, 0))
        )

    def sums_of(index):
        return sums_ref[:, index * area : (index + 1) * area]

    def exact_dot(value, right):
        high = value.astype(jnp.bfloat16)
        rest = (value - high.astype(jnp.float32)).astype(jnp.bfloat16)
        return jnp.dot(high, right, preferred_element_type=jnp.float32) + jnp.dot(
            rest, right, preferred_element_type=jnp.float32
        )

    lower = [swap(sums_of(p)) for p, (x, y) in enumerate(uppers) if x < y]
    turned = exact_dot(jnp.concatenate(lower), turn)
    diag, taken = {}, 0
    for p, (x, y) in enumerate(uppers):
        diag[x, y] = sums_of(p)
        if x < y:
            diag[y, x] = turned[taken * rows : (taken + 1) * rows]
            taken += 1
    came = [
        swap(other_ref[:, p * area : (p + 1) * area].astype(jnp.float32))
        for p in range(strips * span)
    ]
    came = jnp.dot(
        jnp.concatenate(came).astype(jnp.bfloat16), turn, preferred_element_type=jnp.float32
    )
    even = ab == 0
    off = {}
    for x in range(strips):
        for y in range(strips):
            kept = sums_of(len(uppers) + x * span + y % span)
            p = y * span + x % span
            sent = came[p * rows : (p + 1) * rows]
            if x // span == y // span:
                off[x, y] = jnp.where(even, kept, sent)
            else:
                off[x, y] = jnp.where(even, sent, kept)
    for tile, blocks in ((ab, diag), (1 - ab, off)):
        for x in range(strips):
            line = jnp.concatenate([blocks[x, y] for y in range(strips)], axis=1)
            symmetric = exact_dot(line, ordered)
            at = pl.ds(pl.multiple_of(tile * tile_area + x * wide, wide), wide)
            below = cols_ref[:, at] - rows_ref[:, 0:1]
            next_ref[:, at] = ((driver_ref[:, at] + symmetric) / below).astype(next_ref.dtype)


def update(sums, other, driver, col_energy, row_energy, same, tile_width, width, dtype):
    strips = tile_width // STRIP
    span = width // (STRIP * STRIP)
    return pl.pallas_call(
        functools.partial(update_kernel, strips, STRIP, span),
        out_shape=jax.ShapeDtypeStruct(driver.shape, dtype),
        in_specs=[pl.BlockSpec(memory_space=pltpu.VMEM)] * 6,
        out_specs=pl.BlockSpec(memory_space=pltpu.VMEM),
        compiler_params=pltpu.CompilerParams(vmem_limit_bytes=48 * 2**20),
    )(sums, other, driver, col_energy, row_energy, same)


def body(amplitudes, driver, ladder, block_mask, pair_list, occ_energy, virt_energy):
    ab_count = lax.axis_size("ab")
    ab_index = lax.axis_index("ab")
    cd_index = lax.axis_index("cd")
    rows_dev, cols_dev = amplitudes.shape
    out_rows, in_cols = ladder.shape
    tile_width = NV // ab_count
    tile_area = tile_width * tile_width
    strip = min(STRIP, tile_width)
    strips = tile_width // strip
    diag_cols = sum(strip * (tile_width - s * strip) for s in range(strips))
    width = min(512, tile_area)

    paired = (
        ab_count == 2
        and tile_width % (2 * STRIP) == 0
        and width == 2 * STRIP * STRIP
        and diag_cols == (strips + 1) * width
        and lax.axis_size("cd") >= 2 * (strips + 1)
        and lax.axis_size("cd").bit_count() == 1
    )
    weights = ladder.reshape(out_rows // BLK, BLK, in_cols // BLK, BLK)
    weights = (weights * block_mask.astype(jnp.bfloat16)[:, None, :, None]).reshape(
        ab_count, tile_width, tile_width, in_cols
    )
    diag_tile = lax.dynamic_index_in_dim(weights, ab_index, 0, keepdims=False)

    def pack(tile):
        return jnp.concatenate(
            [
                tile[s * strip : (s + 1) * strip, s * strip :].reshape(-1, in_cols)
                for s in range(strips)
            ]
        )

    others = [
        lax.dynamic_index_in_dim(
            weights, lax.rem(ab_index + j, ab_count), 0, keepdims=False
        ).reshape(tile_area, in_cols)
        for j in range(1, ab_count)
    ]
    straight = jnp.concatenate([pack(diag_tile)] + others)
    mirrored = pack(jnp.swapaxes(diag_tile, 0, 1))

    pairs_local = ab_index * cols_dev + jnp.arange(cols_dev, dtype=jnp.int32)
    big_a = pairs_local // (tile_width * NV)
    big_b = pairs_local // tile_area % ab_count
    first = big_a * tile_width + pairs_local // tile_width % tile_width
    second = big_b * tile_width + pairs_local % tile_width
    virt_index = jnp.arange(NV, dtype=jnp.int32)
    picks = (first[:, None] == virt_index).astype(jnp.float32) + (
        second[:, None] == virt_index
    ).astype(jnp.float32)
    col_energy = jnp.dot(picks, virt_energy, precision=lax.Precision.HIGHEST)
    row_pairs = lax.dynamic_slice_in_dim(pair_list, cd_index * rows_dev, rows_dev)
    occ_index = jnp.arange(NOCC, dtype=jnp.int32)
    occ_picks = (row_pairs[:, None] // NOCC == occ_index).astype(jnp.float32)
    occ_picks = occ_picks + (row_pairs[:, None] % NOCC == occ_index).astype(jnp.float32)
    row_energy = jnp.dot(occ_picks, occ_energy, precision=lax.Precision.HIGHEST)
    denominator = col_energy[None, :] - row_energy[:, None]

    def swap_matrix(listed):
        diagonal = listed // NOCC == listed % NOCC
        index = jnp.arange(listed.shape[0], dtype=jnp.int32)
        mirror_row = jnp.where(diagonal, index, index ^ 1)
        return (mirror_row[:, None] == index).astype(jnp.bfloat16)

    row_swap = swap_matrix(row_pairs)
    all_swap = swap_matrix(pair_list)

    def spread(packed):
        pieces, start = [], 0
        for s in range(strips):
            wide = tile_width - s * strip
            piece = packed[:, start : start + strip * wide].reshape(rows_dev, strip, wide)
            start += strip * wide
            piece = jnp.concatenate([0.5 * piece[:, :, :strip], piece[:, :, strip:]], axis=2)
            pieces.append(jnp.pad(piece, ((0, 0), (0, 0), (s * strip, 0))))
        return jnp.concatenate(pieces, axis=1).reshape(rows_dev, tile_area)

    diag_rows = (pair_list // NOCC == pair_list % NOCC).astype(jnp.float32)
    diag_rows = jnp.broadcast_to(diag_rows[:, None], (pair_list.shape[0], 128))
    row_same = (row_pairs // NOCC == row_pairs % NOCC).astype(jnp.float32)

    def lanes(values):
        return jnp.broadcast_to(values[:, None], (values.shape[0], 128))

    if paired:
        masks = block_mask.astype(jnp.bfloat16).reshape(ab_count, tile_area // BLK, 1, -1, 1)
        masks = jnp.broadcast_to(
            masks, (ab_count, tile_area // BLK, STRIP, in_cols // BLK, BLK)
        ).reshape(ab_count, tile_area // BLK, STRIP, in_cols)
        tiles_in = ladder.reshape(ab_count, tile_width, tile_width, in_cols)
        state = amplitudes.astype(jnp.bfloat16)
        for step in range(ITERS):
            sums, other = iteration_sums(state, diag_rows, masks, tiles_in, width)
            state = update(
                sums, other, driver, col_energy[None, :], lanes(row_energy), lanes(row_same),
                tile_width, width, jnp.bfloat16 if step < ITERS - 1 else jnp.float32,
            )
        return state

    state = amplitudes
    for step in range(ITERS):
        rounded = state.astype(jnp.bfloat16)
        regrouped = lax.all_to_all(rounded, "cd", split_axis=1, concat_axis=0, tiled=True)
        low = lax.all_gather(regrouped, "ab", axis=1, tiled=True)
        swapped_low = jnp.dot(all_swap, low, preferred_element_type=jnp.float32)
        sums = ladder_sums(
            low, swapped_low.astype(jnp.bfloat16), straight, mirrored, rows_dev, width
        )
        parts = [spread(sums[:, :diag_cols])]
        for j in range(1, ab_count):
            start = diag_cols + (j - 1) * tile_area
            parts.append(sums[:, start : start + tile_area])
        placed = jnp.concatenate(parts, axis=1)
        received = jnp.roll(placed.reshape(rows_dev, ab_count, tile_area), ab_index, axis=1)
        received = received.reshape(rows_dev, cols_dev)
        swapped = jnp.dot(
            row_swap, received.astype(jnp.bfloat16), preferred_element_type=jnp.float32
        )
        tiles = lax.all_to_all(
            swapped.astype(jnp.bfloat16).reshape(rows_dev, ab_count, tile_area),
            "ab",
            split_axis=1,
            concat_axis=1,
            tiled=True,
        )
        symmetric = received + flip_tiles(tiles, tile_width).astype(jnp.float32)
        state = (driver + symmetric) / denominator
    return state


def solution(mesh):
    placed = (P("cd", "ab"), P("cd", "ab"), P("ab", "cd"), P("ab", "cd"), P(), P(), P())
    return jax.shard_map(body, mesh=mesh, in_specs=placed, out_specs=P("cd", "ab"), check_vma=False)
```

```python
import functools

import jax
import jax.numpy as jnp
from jax import lax
from jax.experimental import pallas as pl
from jax.experimental.pallas import tpu as pltpu
from jax.sharding import PartitionSpec as P

NV = 128
NOCC = 32
BLK = 128
ITERS = 2
STRIP = 16
MESH = pl.DeviceIdType.MESH
NT = (((1,), (1,)), ((), ()))


def flip_tiles(tiles, tile_width):
    row_count, tile_count = tiles.shape[:2]
    turned = jnp.swapaxes(tiles.reshape(row_count, tile_count, tile_width, tile_width), 2, 3)
    return turned.reshape(row_count, tile_count * tile_width * tile_width)


def bit_of(index, bit):
    return lax.rem(index // (1 << bit), 2)


def flip_bit(index, bit):
    return index + (1 - 2 * bit_of(index, bit)) * (1 << bit)


def ladder_kernel(
    bits, chunks, diag_chunks, width,
    low_ref, swap_ref, straight_ref, mirrored_ref, out_ref,
    straight, mirrored, *rest,
):
    held = rest[: bits + 1]
    load_sem, mirror_sem, send_sem, recv_sem = rest[bits + 1 :]
    ab = lax.axis_index("ab")
    cd = lax.axis_index("cd")
    rows = out_ref.shape[0]
    own = [bit_of(cd, bit) for bit in range(bits)]
    partner = [(ab, flip_bit(cd, bit)) for bit in range(bits)]

    def at(stage, chunk, which):
        lead = (slice(None),) * (bits - 1 - stage)
        return held[stage].at[(chunk,) + lead + (which,)]

    def copy(stage, chunk):
        return pltpu.make_async_remote_copy(
            src_ref=at(stage, chunk, 1 - own[stage]),
            dst_ref=held[stage + 1].at[chunk],
            send_sem=send_sem.at[stage, chunk],
            recv_sem=recv_sem.at[stage, chunk],
            device_id=partner[stage],
            device_id_type=MESH,
        )

    def load_straight(chunk):
        start = pl.multiple_of(chunk * width, width)
        return pltpu.make_async_copy(
            straight_ref.at[pl.ds(start, width)], straight.at[chunk], load_sem.at[chunk]
        )

    def load_mirrored(chunk):
        start = pl.multiple_of(chunk * width, width)
        return pltpu.make_async_copy(
            mirrored_ref.at[pl.ds(start, width)], mirrored.at[chunk], mirror_sem.at[chunk]
        )

    @pl.loop(0, diag_chunks)
    def _(chunk):
        load_straight(chunk).start()
        load_mirrored(chunk).start()

    @pl.loop(diag_chunks, chunks)
    def _(chunk):
        load_straight(chunk).start()

    barrier = pltpu.get_barrier_semaphore()
    for device in partner:
        pl.semaphore_signal(barrier, inc=1, device_id=device, device_id_type=MESH)
    pl.semaphore_wait(barrier, bits)

    def put(chunk, product):
        value = product.astype(jnp.bfloat16)
        for block in range(1 << bits):
            index = tuple((block >> (bits - 1 - axis)) & 1 for axis in range(bits))
            held[0][(chunk,) + index] = value[block * rows : (block + 1) * rows]

    @pl.loop(0, chunks + 2 * bits)
    def _(step):
        @pl.when(step < diag_chunks)
        def _():
            load_straight(step).wait()
            load_mirrored(step).wait()
            total = lax.dot_general(
                low_ref[...], straight[step], NT, preferred_element_type=jnp.float32
            )
            total += lax.dot_general(
                swap_ref[...], mirrored[step], NT, preferred_element_type=jnp.float32
            )
            put(step, total)
            copy(0, step).start()

        @pl.when((step >= diag_chunks) & (step < chunks))
        def _():
            load_straight(step).wait()
            put(
                step,
                lax.dot_general(
                    low_ref[...], straight[step], NT, preferred_element_type=jnp.float32
                ),
            )
            copy(0, step).start()

        for stage in range(bits):
            chunk = step - (2 * stage + 1)

            @pl.when((chunk >= 0) & (chunk < chunks))
            def _():
                copy(stage, chunk).wait_recv()
                mine = at(stage, chunk, own[stage])[...].astype(jnp.float32)
                total = held[stage + 1][chunk].astype(jnp.float32) + mine
                if stage < bits - 1:
                    held[stage + 1][chunk] = total.astype(jnp.bfloat16)
                    copy(stage + 1, chunk).start()
                else:
                    out_ref[:, pl.ds(pl.multiple_of(chunk * width, width), width)] = total

    @pl.loop(0, chunks)
    def _(chunk):
        for stage in range(bits):
            copy(stage, chunk).wait_send()


def ladder_sums(low, swapped, straight, mirrored, rows, width):
    count = low.shape[0] // rows
    bits = count.bit_length() - 1
    depth = low.shape[1]
    chunks = straight.shape[0] // width
    diag_chunks = mirrored.shape[0] // width
    held = [
        pltpu.VMEM((chunks,) + (2,) * (bits - stage) + (rows, width), jnp.bfloat16)
        for stage in range(bits + 1)
    ]
    return pl.pallas_call(
        functools.partial(ladder_kernel, bits, chunks, diag_chunks, width),
        out_shape=jax.ShapeDtypeStruct((rows, chunks * width), jnp.float32),
        in_specs=[pl.BlockSpec(memory_space=pltpu.VMEM)] * 2
        + [pl.BlockSpec(memory_space=pl.ANY)] * 2,
        out_specs=pl.BlockSpec(memory_space=pltpu.VMEM),
        scratch_shapes=[
            pltpu.VMEM((chunks, width, depth), jnp.bfloat16),
            pltpu.VMEM((diag_chunks, width, depth), jnp.bfloat16),
            *held,
            pltpu.SemaphoreType.DMA((chunks,)),
            pltpu.SemaphoreType.DMA((diag_chunks,)),
            pltpu.SemaphoreType.DMA((bits, chunks)),
            pltpu.SemaphoreType.DMA((bits, chunks)),
        ],
        compiler_params=pltpu.CompilerParams(
            collective_id=0, has_side_effects=True, vmem_limit_bytes=58 * 2**20
        ),
    )(low, swapped, straight, mirrored)


def iteration_kernel(
    bits, width, rows,
    state_ref, diagonal_ref, mask_ref, weight_ref, sums_ref, other_ref,
    low, straight, mirrored, outer, part, part_y, *rest,
):
    held = (part,) + rest[:bits]
    final, landed = rest[bits : bits + 2]
    (
        load_sem, self_sem, a_send, a_recv, b_send, b_recv,
        core_send, core_recv, y_send, y_recv, send_sem, recv_sem, last_send, last_recv,
    ) = rest[bits + 2 :]
    ab = lax.axis_index("ab")
    cd = lax.axis_index("cd")
    count = 1 << bits
    side = straight.shape[1]
    strips = weight_ref.shape[1] // side
    depth = weight_ref.shape[3]
    piece = depth // 2
    keeps = strips
    span = width // (side * side)
    diags = keeps + 1
    products = 3 * keeps + 1
    finals = diags + keeps
    own = [bit_of(cd, bit) for bit in range(bits)]
    partner = [(ab, flip_bit(cd, bit)) for bit in range(bits)]
    across = (1 - ab, cd)

    def remote(src, dst, send, recv, device):
        return pltpu.make_async_remote_copy(
            src_ref=src, dst_ref=dst, send_sem=send, recv_sem=recv,
            device_id=device, device_id_type=MESH,
        )

    def block_of(tile, x, y):
        return weight_ref.at[
            tile,
            pl.ds(pl.multiple_of(x * side, side), side),
            pl.ds(pl.multiple_of(y * side, side), side),
        ]

    def upper(p):
        starts = [sum(strips - r for r in range(s)) for s in range(strips)]
        x = sum((p >= start).astype(jnp.int32) for start in starts[1:])
        start = sum(
            jnp.where(x == s, starts[s], 0) for s in range(strips)
        )
        return x, p - start + x

    def kept_y(p, which):
        return span * lax.rem(p // (span * span) + which, 2) + lax.rem(p, span)

    @pl.loop(0, diags * span)
    def _(p):
        x, y = upper(p)
        pltpu.make_async_copy(block_of(ab, x, y), straight.at[p], load_sem.at[0]).start()
        pltpu.make_async_copy(block_of(ab, y, x), mirrored.at[p], load_sem.at[1]).start()

    @pl.loop(0, keeps * span)
    def _(p):
        pltpu.make_async_copy(
            block_of(1 - ab, p // span, kept_y(p, ab)), outer.at[0, p], load_sem.at[2]
        ).start()
        pltpu.make_async_copy(
            block_of(1 - ab, kept_y(p, 1 - ab), p // span), outer.at[1, p], load_sem.at[3]
        ).start()

    def masked(block, tile, x):
        pairs = side // 2
        mask = mask_ref[tile, pl.ds(pl.multiple_of(x * pairs, pairs), pairs)]
        value = block.reshape(pairs, 2, side, depth) * mask[:, None]
        return value.reshape(side * side, depth)

    area = side * side
    row_at = lax.broadcasted_iota(jnp.int32, (area, area), 0)
    col_at = lax.broadcasted_iota(jnp.int32, (area, area), 1)
    turn_rows = (row_at == lax.rem(col_at, side) * side + col_at // side).astype(jnp.bfloat16)

    def turned(value):
        product = jnp.dot(turn_rows, value, preferred_element_type=jnp.float32)
        return product.astype(jnp.bfloat16).reshape(side, side, depth)

    def prepare_diag(p):
        x, y = upper(p)
        straight[p] = masked(straight[p], ab, x).reshape(side, side, depth)
        mirrored[p] = turned(masked(mirrored[p], ab, y))

    def prepare_outer(p):
        outer[0, p] = masked(outer[0, p], 1 - ab, p // span).reshape(side, side, depth)
        outer[1, p] = turned(masked(outer[1, p], 1 - ab, kept_y(p, 1 - ab)))

    barrier = pltpu.get_barrier_semaphore()

    @pl.loop(1, count)
    def _(j):
        pl.semaphore_signal(
            barrier, inc=1, device_id=(ab, lax.rem(cd + j, count)), device_id_type=MESH
        )

    pl.semaphore_signal(barrier, inc=1, device_id=across, device_id_type=MESH)
    pl.semaphore_wait(barrier, count)

    def rows_of(source):
        return pl.ds(pl.multiple_of(source * rows, rows), rows)

    def cols_of(side):
        return pl.ds(pl.multiple_of(side * piece, piece), piece)

    def scatter(target, source):
        return remote(
            state_ref.at[:, pl.ds(pl.multiple_of(target * piece, piece), piece)],
            low.at[0, rows_of(source), cols_of(ab)],
            a_send.at[target], a_recv.at[source], (ab, target),
        )

    def forward(source, side):
        block = low.at[0, rows_of(source), cols_of(side)]
        return remote(block, block, b_send.at[source], b_recv.at[source], across)

    stay = pltpu.make_async_copy(
        state_ref.at[:, pl.ds(pl.multiple_of(cd * piece, piece), piece)],
        low.at[0, rows_of(cd), cols_of(ab)],
        self_sem,
    )
    stay.start()

    def other(j):
        return sum(
            lax.rem(own[bit] + bit_of(j, bit), 2) * (1 << bit) for bit in range(bits)
        )

    @pl.loop(1, count)
    def _(i):
        scatter(other(i), cd).start()

    stay.wait()
    forward(cd, ab).start()

    @pl.loop(0, count)
    def _(i):
        @pl.when(i != 0)
        def _():
            source = other(i)
            scatter(cd, source).wait_recv()
            forward(source, ab).start()

        @pl.when(i == 0)
        def _():
            pltpu.make_async_copy(straight, straight, load_sem.at[0]).wait()
            pltpu.make_async_copy(mirrored, mirrored, load_sem.at[1]).wait()

        @pl.when(i < diags * span)
        def _():
            prepare_diag(i)

        late = i - (count - keeps * span)

        @pl.when(late == 0)
        def _():
            pltpu.make_async_copy(outer.at[0], outer.at[0], load_sem.at[2]).wait()
            pltpu.make_async_copy(outer.at[1], outer.at[1], load_sem.at[3]).wait()

        @pl.when(late >= 0)
        def _():
            prepare_outer(late)

    @pl.loop(0, count)
    def _(i):
        forward(other(i), 1 - ab).wait_recv()

    odd = lax.rem(lax.broadcasted_iota(jnp.int32, (rows, 128), 0), 2) == 1

    @pl.loop(0, count)
    def _(source):
        at = rows_of(source)
        same = diagonal_ref[at, :] != 0
        for lane in range(0, depth, 128):
            value = low[0, at, lane : lane + 128].astype(jnp.float32)
            other = jnp.where(odd, pltpu.roll(value, 1, 0), pltpu.roll(value, rows - 1, 0))
            low[1, at, lane : lane + 128] = jnp.where(same, value, other).astype(jnp.bfloat16)

    def at(stage, index, which):
        lead = (slice(None),) * (bits - 1 - stage)
        return held[stage].at[(index,) + lead + (which,)]

    def place(q):
        turn = q // 2
        diag = jnp.where(turn == keeps, 3 * keeps, 3 * turn + 1)
        return jnp.where(lax.rem(q, 2) == 0, diag, 3 * turn + 2)

    def core_copy(u):
        return remote(
            at(0, u, 1 - own[0]), held[1].at[u], core_send.at[u], core_recv.at[u], partner[0]
        )

    def y_copy(j):
        return remote(held[1].at[3 * j], part_y.at[j], y_send.at[j], y_recv.at[j], across)

    def stage_copy(stage, q):
        source = at(1, place(q), 1 - own[1]) if stage == 1 else at(stage, q, 1 - own[stage])
        return remote(
            source, held[stage + 1].at[q],
            send_sem.at[stage - 1, q], recv_sem.at[stage - 1, q], partner[stage],
        )

    def last_copy(j):
        return remote(final.at[j], landed.at[j], last_send.at[j], last_recv.at[j], across)

    def put(u, product):
        value = product.astype(jnp.bfloat16)
        for block in range(count):
            index = tuple((block >> (bits - 1 - axis)) & 1 for axis in range(bits))
            part[(u,) + index] = value[block * rows : (block + 1) * rows]

    def rows_at(start):
        return pl.ds(pl.multiple_of(start, width), width)

    def blocks_at(turn):
        return pl.ds(turn * span, span)

    def dot(left, right):
        return lax.dot_general(left, right, NT, preferred_element_type=jnp.float32)

    y_lag = 7
    lags = [5 + 2 * s for s in range(bits - 1)]

    @pl.loop(0, 2 * (finals - 1) + lags[-1] + 1)
    def _(step):
        turn = step // 3
        kind = lax.rem(step, 3)
        is_diag = ((kind == 1) & (step < 3 * keeps)) | (step == 3 * keeps)

        @pl.when(is_diag)
        def _():
            total = dot(low[0], straight[blocks_at(turn)].reshape(width, depth))
            put(step, total + dot(low[1], mirrored[blocks_at(turn)].reshape(width, depth)))
            core_copy(step).start()

        @pl.when((kind != 1) & (step < 3 * keeps))
        def _():
            sent = 1 - kind // 2
            put(step, dot(low[sent], outer[sent, blocks_at(turn)].reshape(width, depth)))
            core_copy(step).start()

        u = step - 1

        @pl.when((u >= 0) & (u < products))
        def _():
            core_copy(u).wait_recv()
            held[1][u] = held[1][u] + at(0, u, own[0])[...]
            u_kind = lax.rem(u, 3)

            @pl.when((u_kind == 1) | (u == 3 * keeps))
            def _():
                stage_copy(1, 2 * (u // 3)).start()

            @pl.when((u_kind == 0) & (u < 3 * keeps))
            def _():
                y_copy(u // 3).start()

        v = step - y_lag

        @pl.when((v >= 0) & (lax.rem(v + 3, 3) == 0) & (v < 3 * keeps))
        def _():
            y_copy(v // 3).wait_recv()
            held[1][v + 2] = held[1][v + 2] + part_y[v // 3]
            stage_copy(1, 2 * (v // 3) + 1).start()

        for stage in range(1, bits):
            w = step - lags[stage - 1]
            q = w // 2

            @pl.when((w >= 0) & (lax.rem(w + 2, 2) == 0) & (q < finals))
            def _():
                stage_copy(stage, q).wait_recv()
                index = place(q) if stage == 1 else q
                mine = at(stage, index, own[stage])[...]
                if stage < bits - 1:
                    held[stage + 1][q] = held[stage + 1][q] + mine
                    stage_copy(stage + 1, q).start()
                else:
                    total = held[stage + 1][q].astype(jnp.float32) + mine.astype(jnp.float32)
                    kept = lax.rem(q, 2) == 1
                    start = jnp.where(kept, diags + q // 2, q // 2) * width
                    sums_ref[:, rows_at(start)] = total

                    @pl.when(kept)
                    def _():
                        final[q // 2] = total.astype(jnp.bfloat16)
                        last_copy(q // 2).start()

    for j in range(keeps):
        last_copy(j).wait_recv()
        other_ref[:, j * width : (j + 1) * width] = landed[j]

    @pl.loop(0, count)
    def _(i):
        @pl.when(i != cd)
        def _():
            scatter(i, cd).wait_send()

        forward(i, ab).wait_send()

    @pl.loop(0, products)
    def _(u):
        core_copy(u).wait_send()

    @pl.loop(0, keeps)
    def _(j):
        y_copy(j).wait_send()
        last_copy(j).wait_send()

    @pl.loop(0, finals)
    def _(q):
        for stage in range(1, bits):
            stage_copy(stage, q).wait_send()


def iteration_sums(state, diagonal, mask, weights, width):
    rows = state.shape[0]
    count = diagonal.shape[0] // rows
    bits = count.bit_length() - 1
    tile_width, depth = weights.shape[1], weights.shape[3]
    keeps = tile_width // STRIP
    diags = keeps + 1
    span = width // (STRIP * STRIP)
    products, finals = 3 * keeps + 1, 2 * keeps + 1
    dma = pltpu.SemaphoreType.DMA
    block = (rows, width)
    square = (STRIP, STRIP, depth)
    return pl.pallas_call(
        functools.partial(iteration_kernel, bits, width, rows),
        out_shape=(
            jax.ShapeDtypeStruct((rows, finals * width), jnp.float32),
            jax.ShapeDtypeStruct((rows, keeps * width), jnp.bfloat16),
        ),
        in_specs=[pl.BlockSpec(memory_space=pltpu.VMEM)] * 3
        + [pl.BlockSpec(memory_space=pl.ANY)],
        out_specs=[pl.BlockSpec(memory_space=pltpu.VMEM)] * 2,
        scratch_shapes=[
            pltpu.VMEM((2, count * rows, depth), jnp.bfloat16),
            pltpu.VMEM((diags * span,) + square, jnp.bfloat16),
            pltpu.VMEM((diags * span,) + square, jnp.bfloat16),
            pltpu.VMEM((2, keeps * span) + square, jnp.bfloat16),
            pltpu.VMEM((products,) + (2,) * bits + block, jnp.bfloat16),
            pltpu.VMEM((keeps,) + (2,) * (bits - 1) + block, jnp.bfloat16),
            pltpu.VMEM((products,) + (2,) * (bits - 1) + block, jnp.bfloat16),
            *[
                pltpu.VMEM((finals,) + (2,) * (bits - 1 - s) + block, jnp.bfloat16)
                for s in range(1, bits)
            ],
            pltpu.VMEM((keeps,) + block, jnp.bfloat16),
            pltpu.VMEM((keeps,) + block, jnp.bfloat16),
            dma((4,)), dma,
            dma((count,)), dma((count,)), dma((count,)), dma((count,)),
            dma((products,)), dma((products,)), dma((keeps,)), dma((keeps,)),
            dma((bits - 1, finals)), dma((bits - 1, finals)), dma((keeps,)), dma((keeps,)),
        ],
        compiler_params=pltpu.CompilerParams(
            collective_id=1, has_side_effects=True, vmem_limit_bytes=60 * 2**20
        ),
    )(state, diagonal, mask, weights)


def update_kernel(
    strips, side, span,
    sums_ref, other_ref, driver_ref, cols_ref, rows_ref, same_ref, next_ref,
):
    ab = lax.axis_index("ab")
    rows = driver_ref.shape[0]
    area = side * side
    wide = strips * area
    tile_area = strips * wide
    uppers = [(x, y) for x in range(strips) for y in range(x, strips)]

    def iotas(size):
        return (lax.broadcasted_iota(jnp.int32, (size, size), axis) for axis in (0, 1))

    start, end = iotas(area)
    turn = (start == lax.rem(end, side) * side + end // side).astype(jnp.bfloat16)
    start, end = iotas(wide)
    block, inner = lax.rem(end, strips * side) // side, lax.rem(end, side)
    ordered = start == block * area + end // (strips * side) * side + inner
    ordered = ordered.astype(jnp.bfloat16)
    odd = lax.rem(lax.broadcasted_iota(jnp.int32, (rows, area), 0), 2) == 1
    same = jnp.broadcast_to(same_ref[:, 0:1], (rows, area)) != 0

    def swap(value):
        return jnp.where(
            same, value, jnp.where(odd, pltpu.roll(value, 1, 0), pltpu.roll(value, rows - 1, 0))
        )

    def sums_of(index):
        return sums_ref[:, index * area : (index + 1) * area]

    def exact_dot(value, right):
        high = value.astype(jnp.bfloat16)
        rest = (value - high.astype(jnp.float32)).astype(jnp.bfloat16)
        return jnp.dot(high, right, preferred_element_type=jnp.float32) + jnp.dot(
            rest, right, preferred_element_type=jnp.float32
        )

    lower = [swap(sums_of(p)) for p, (x, y) in enumerate(uppers) if x < y]
    turned = exact_dot(jnp.concatenate(lower), turn)
    diag, taken = {}, 0
    for p, (x, y) in enumerate(uppers):
        diag[x, y] = sums_of(p)
        if x < y:
            diag[y, x] = turned[taken * rows : (taken + 1) * rows]
            taken += 1
    came = [
        swap(other_ref[:, p * area : (p + 1) * area].astype(jnp.float32))
        for p in range(strips * span)
    ]
    came = jnp.dot(
        jnp.concatenate(came).astype(jnp.bfloat16), turn, preferred_element_type=jnp.float32
    )
    even = ab == 0
    off = {}
    for x in range(strips):
        for y in range(strips):
            kept = sums_of(len(uppers) + x * span + y % span)
            p = y * span + x % span
            sent = came[p * rows : (p + 1) * rows]
            if x // span == y // span:
                off[x, y] = jnp.where(even, kept, sent)
            else:
                off[x, y] = jnp.where(even, sent, kept)
    for tile, blocks in ((ab, diag), (1 - ab, off)):
        for x in range(strips):
            line = jnp.concatenate([blocks[x, y] for y in range(strips)], axis=1)
            symmetric = exact_dot(line, ordered)
            at = pl.ds(pl.multiple_of(tile * tile_area + x * wide, wide), wide)
            below = cols_ref[:, at] - rows_ref[:, 0:1]
            next_ref[:, at] = ((driver_ref[:, at] + symmetric) / below).astype(next_ref.dtype)


def update(sums, other, driver, col_energy, row_energy, same, tile_width, width, dtype):
    strips = tile_width // STRIP
    span = width // (STRIP * STRIP)
    return pl.pallas_call(
        functools.partial(update_kernel, strips, STRIP, span),
        out_shape=jax.ShapeDtypeStruct(driver.shape, dtype),
        in_specs=[pl.BlockSpec(memory_space=pltpu.VMEM)] * 6,
        out_specs=pl.BlockSpec(memory_space=pltpu.VMEM),
        compiler_params=pltpu.CompilerParams(vmem_limit_bytes=48 * 2**20),
    )(sums, other, driver, col_energy, row_energy, same)


def body(amplitudes, driver, ladder, block_mask, pair_list, occ_energy, virt_energy):
    ab_count = lax.axis_size("ab")
    ab_index = lax.axis_index("ab")
    cd_index = lax.axis_index("cd")
    rows_dev, cols_dev = amplitudes.shape
    out_rows, in_cols = ladder.shape
    tile_width = NV // ab_count
    tile_area = tile_width * tile_width
    strip = min(STRIP, tile_width)
    strips = tile_width // strip
    diag_cols = sum(strip * (tile_width - s * strip) for s in range(strips))
    width = min(512, tile_area)

    paired = (
        ab_count == 2
        and tile_width % (2 * STRIP) == 0
        and width == 2 * STRIP * STRIP
        and diag_cols == (strips + 1) * width
        and lax.axis_size("cd") >= 2 * (strips + 1)
        and lax.axis_size("cd").bit_count() == 1
    )
    weights = ladder.reshape(out_rows // BLK, BLK, in_cols // BLK, BLK)
    weights = (weights * block_mask.astype(jnp.bfloat16)[:, None, :, None]).reshape(
        ab_count, tile_width, tile_width, in_cols
    )
    diag_tile = lax.dynamic_index_in_dim(weights, ab_index, 0, keepdims=False)

    def pack(tile):
        return jnp.concatenate(
            [
                tile[s * strip : (s + 1) * strip, s * strip :].reshape(-1, in_cols)
                for s in range(strips)
            ]
        )

    others = [
        lax.dynamic_index_in_dim(
            weights, lax.rem(ab_index + j, ab_count), 0, keepdims=False
        ).reshape(tile_area, in_cols)
        for j in range(1, ab_count)
    ]
    straight = jnp.concatenate([pack(diag_tile)] + others)
    mirrored = pack(jnp.swapaxes(diag_tile, 0, 1))

    pairs_local = ab_index * cols_dev + jnp.arange(cols_dev, dtype=jnp.int32)
    big_a = pairs_local // (tile_width * NV)
    big_b = pairs_local // tile_area % ab_count
    first = big_a * tile_width + pairs_local // tile_width % tile_width
    second = big_b * tile_width + pairs_local % tile_width
    virt_index = jnp.arange(NV, dtype=jnp.int32)
    picks = (first[:, None] == virt_index).astype(jnp.float32) + (
        second[:, None] == virt_index
    ).astype(jnp.float32)
    col_energy = jnp.dot(picks, virt_energy, precision=lax.Precision.HIGHEST)
    row_pairs = lax.dynamic_slice_in_dim(pair_list, cd_index * rows_dev, rows_dev)
    occ_index = jnp.arange(NOCC, dtype=jnp.int32)
    occ_picks = (row_pairs[:, None] // NOCC == occ_index).astype(jnp.float32)
    occ_picks = occ_picks + (row_pairs[:, None] % NOCC == occ_index).astype(jnp.float32)
    row_energy = jnp.dot(occ_picks, occ_energy, precision=lax.Precision.HIGHEST)
    denominator = col_energy[None, :] - row_energy[:, None]

    def swap_matrix(listed):
        diagonal = listed // NOCC == listed % NOCC
        index = jnp.arange(listed.shape[0], dtype=jnp.int32)
        mirror_row = jnp.where(diagonal, index, index ^ 1)
        return (mirror_row[:, None] == index).astype(jnp.bfloat16)

    row_swap = swap_matrix(row_pairs)
    all_swap = swap_matrix(pair_list)

    def spread(packed):
        pieces, start = [], 0
        for s in range(strips):
            wide = tile_width - s * strip
            piece = packed[:, start : start + strip * wide].reshape(rows_dev, strip, wide)
            start += strip * wide
            piece = jnp.concatenate([0.5 * piece[:, :, :strip], piece[:, :, strip:]], axis=2)
            pieces.append(jnp.pad(piece, ((0, 0), (0, 0), (s * strip, 0))))
        return jnp.concatenate(pieces, axis=1).reshape(rows_dev, tile_area)

    diag_rows = (pair_list // NOCC == pair_list % NOCC).astype(jnp.float32)
    diag_rows = jnp.broadcast_to(diag_rows[:, None], (pair_list.shape[0], 128))
    row_same = (row_pairs // NOCC == row_pairs % NOCC).astype(jnp.float32)

    def lanes(values):
        return jnp.broadcast_to(values[:, None], (values.shape[0], 128))

    if paired:
        masks = block_mask.astype(jnp.bfloat16).reshape(ab_count, tile_area // BLK, 1, -1, 1)
        masks = jnp.broadcast_to(
            masks, (ab_count, tile_area // BLK, STRIP, in_cols // BLK, BLK)
        ).reshape(ab_count, tile_area // BLK, STRIP, in_cols)
        tiles_in = ladder.reshape(ab_count, tile_width, tile_width, in_cols)
        first_energy = lax.dynamic_slice_in_dim(virt_energy, ab_index * tile_width, tile_width)
        tile_energy = (
            first_energy[None, :, None] + virt_energy.reshape(ab_count, 1, tile_width)
        ).reshape(1, cols_dev)
        state = amplitudes.astype(jnp.bfloat16)
        for step in range(ITERS):
            sums, other = iteration_sums(state, diag_rows, masks, tiles_in, width)
            state = update(
                sums, other, driver, tile_energy, lanes(row_energy), lanes(row_same),
                tile_width, width, jnp.bfloat16 if step < ITERS - 1 else jnp.float32,
            )
        return state

    state = amplitudes
    for step in range(ITERS):
        rounded = state.astype(jnp.bfloat16)
        regrouped = lax.all_to_all(rounded, "cd", split_axis=1, concat_axis=0, tiled=True)
        low = lax.all_gather(regrouped, "ab", axis=1, tiled=True)
        swapped_low = jnp.dot(all_swap, low, preferred_element_type=jnp.float32)
        sums = ladder_sums(
            low, swapped_low.astype(jnp.bfloat16), straight, mirrored, rows_dev, width
        )
        parts = [spread(sums[:, :diag_cols])]
        for j in range(1, ab_count):
            start = diag_cols + (j - 1) * tile_area
            parts.append(sums[:, start : start + tile_area])
        placed = jnp.concatenate(parts, axis=1)
        received = jnp.roll(placed.reshape(rows_dev, ab_count, tile_area), ab_index, axis=1)
        received = received.reshape(rows_dev, cols_dev)
        swapped = jnp.dot(
            row_swap, received.astype(jnp.bfloat16), preferred_element_type=jnp.float32
        )
        tiles = lax.all_to_all(
            swapped.astype(jnp.bfloat16).reshape(rows_dev, ab_count, tile_area),
            "ab",
            split_axis=1,
            concat_axis=1,
            tiled=True,
        )
        symmetric = received + flip_tiles(tiles, tile_width).astype(jnp.float32)
        state = (driver + symmetric) / denominator
    return state


def solution(mesh):
    placed = (P("cd", "ab"), P("cd", "ab"), P("ab", "cd"), P("ab", "cd"), P(), P(), P())
    return jax.shard_map(body, mesh=mesh, in_specs=placed, out_specs=P("cd", "ab"), check_vma=False)
```

```python
import functools

import jax
import jax.numpy as jnp
from jax import lax
from jax.experimental import pallas as pl
from jax.experimental.pallas import tpu as pltpu
from jax.sharding import PartitionSpec as P

NV = 128
NOCC = 32
BLK = 128
ITERS = 2
STRIP = 16
GROUP = 16
MESH = pl.DeviceIdType.MESH
NT = (((1,), (1,)), ((), ()))


def flip_tiles(tiles, tile_width):
    row_count, tile_count = tiles.shape[:2]
    turned = jnp.swapaxes(tiles.reshape(row_count, tile_count, tile_width, tile_width), 2, 3)
    return turned.reshape(row_count, tile_count * tile_width * tile_width)


def bit_of(index, bit):
    return lax.rem(index // (1 << bit), 2)


def flip_bit(index, bit):
    return index + (1 - 2 * bit_of(index, bit)) * (1 << bit)


def ladder_kernel(
    bits, chunks, diag_chunks, width,
    low_ref, swap_ref, straight_ref, mirrored_ref, out_ref,
    straight, mirrored, *rest,
):
    held = rest[: bits + 1]
    load_sem, mirror_sem, send_sem, recv_sem = rest[bits + 1 :]
    ab = lax.axis_index("ab")
    cd = lax.axis_index("cd")
    rows = out_ref.shape[0]
    own = [bit_of(cd, bit) for bit in range(bits)]
    partner = [(ab, flip_bit(cd, bit)) for bit in range(bits)]

    def at(stage, chunk, which):
        lead = (slice(None),) * (bits - 1 - stage)
        return held[stage].at[(chunk,) + lead + (which,)]

    def copy(stage, chunk):
        return pltpu.make_async_remote_copy(
            src_ref=at(stage, chunk, 1 - own[stage]),
            dst_ref=held[stage + 1].at[chunk],
            send_sem=send_sem.at[stage, chunk],
            recv_sem=recv_sem.at[stage, chunk],
            device_id=partner[stage],
            device_id_type=MESH,
        )

    def load_straight(chunk):
        start = pl.multiple_of(chunk * width, width)
        return pltpu.make_async_copy(
            straight_ref.at[pl.ds(start, width)], straight.at[chunk], load_sem.at[chunk]
        )

    def load_mirrored(chunk):
        start = pl.multiple_of(chunk * width, width)
        return pltpu.make_async_copy(
            mirrored_ref.at[pl.ds(start, width)], mirrored.at[chunk], mirror_sem.at[chunk]
        )

    @pl.loop(0, diag_chunks)
    def _(chunk):
        load_straight(chunk).start()
        load_mirrored(chunk).start()

    @pl.loop(diag_chunks, chunks)
    def _(chunk):
        load_straight(chunk).start()

    barrier = pltpu.get_barrier_semaphore()
    for device in partner:
        pl.semaphore_signal(barrier, inc=1, device_id=device, device_id_type=MESH)
    pl.semaphore_wait(barrier, bits)

    def put(chunk, product):
        value = product.astype(jnp.bfloat16)
        for block in range(1 << bits):
            index = tuple((block >> (bits - 1 - axis)) & 1 for axis in range(bits))
            held[0][(chunk,) + index] = value[block * rows : (block + 1) * rows]

    @pl.loop(0, chunks + 2 * bits)
    def _(step):
        @pl.when(step < diag_chunks)
        def _():
            load_straight(step).wait()
            load_mirrored(step).wait()
            total = lax.dot_general(
                low_ref[...], straight[step], NT, preferred_element_type=jnp.float32
            )
            total += lax.dot_general(
                swap_ref[...], mirrored[step], NT, preferred_element_type=jnp.float32
            )
            put(step, total)
            copy(0, step).start()

        @pl.when((step >= diag_chunks) & (step < chunks))
        def _():
            load_straight(step).wait()
            put(
                step,
                lax.dot_general(
                    low_ref[...], straight[step], NT, preferred_element_type=jnp.float32
                ),
            )
            copy(0, step).start()

        for stage in range(bits):
            chunk = step - (2 * stage + 1)

            @pl.when((chunk >= 0) & (chunk < chunks))
            def _():
                copy(stage, chunk).wait_recv()
                mine = at(stage, chunk, own[stage])[...].astype(jnp.float32)
                total = held[stage + 1][chunk].astype(jnp.float32) + mine
                if stage < bits - 1:
                    held[stage + 1][chunk] = total.astype(jnp.bfloat16)
                    copy(stage + 1, chunk).start()
                else:
                    out_ref[:, pl.ds(pl.multiple_of(chunk * width, width), width)] = total

    @pl.loop(0, chunks)
    def _(chunk):
        for stage in range(bits):
            copy(stage, chunk).wait_send()


def ladder_sums(low, swapped, straight, mirrored, rows, width):
    count = low.shape[0] // rows
    bits = count.bit_length() - 1
    depth = low.shape[1]
    chunks = straight.shape[0] // width
    diag_chunks = mirrored.shape[0] // width
    held = [
        pltpu.VMEM((chunks,) + (2,) * (bits - stage) + (rows, width), jnp.bfloat16)
        for stage in range(bits + 1)
    ]
    return pl.pallas_call(
        functools.partial(ladder_kernel, bits, chunks, diag_chunks, width),
        out_shape=jax.ShapeDtypeStruct((rows, chunks * width), jnp.float32),
        in_specs=[pl.BlockSpec(memory_space=pltpu.VMEM)] * 2
        + [pl.BlockSpec(memory_space=pl.ANY)] * 2,
        out_specs=pl.BlockSpec(memory_space=pltpu.VMEM),
        scratch_shapes=[
            pltpu.VMEM((chunks, width, depth), jnp.bfloat16),
            pltpu.VMEM((diag_chunks, width, depth), jnp.bfloat16),
            *held,
            pltpu.SemaphoreType.DMA((chunks,)),
            pltpu.SemaphoreType.DMA((diag_chunks,)),
            pltpu.SemaphoreType.DMA((bits, chunks)),
            pltpu.SemaphoreType.DMA((bits, chunks)),
        ],
        compiler_params=pltpu.CompilerParams(
            collective_id=0, has_side_effects=True, vmem_limit_bytes=58 * 2**20
        ),
    )(low, swapped, straight, mirrored)


def iteration_kernel(
    bits, width, rows, groups,
    state_ref, diagonal_ref, mask_ref, weight_ref, sums_ref, other_ref,
    low, straight, mirrored, outer, part, part_y, *rest,
):
    held = (part,) + rest[:bits]
    final, landed = rest[bits : bits + 2]
    (
        load_sem, self_sem, a_send, a_recv, b_send, b_recv,
        core_send, core_recv, y_send, y_recv, send_sem, recv_sem, last_send, last_recv,
    ) = rest[bits + 2 :]
    ab = lax.axis_index("ab")
    cd = lax.axis_index("cd")
    count = 1 << bits
    side = straight.shape[1]
    strips = weight_ref.shape[1] // side
    depth = weight_ref.shape[3]
    piece = depth // 2
    keeps = strips
    span = width // (side * side)
    diags = keeps + 1
    products = 3 * keeps + 1
    finals = diags + keeps
    own = [bit_of(cd, bit) for bit in range(bits)]
    partner = [(ab, flip_bit(cd, bit)) for bit in range(bits)]
    across = (1 - ab, cd)

    def remote(src, dst, send, recv, device):
        return pltpu.make_async_remote_copy(
            src_ref=src, dst_ref=dst, send_sem=send, recv_sem=recv,
            device_id=device, device_id_type=MESH,
        )

    def block_of(tile, x, y):
        return weight_ref.at[
            tile,
            pl.ds(pl.multiple_of(x * side, side), side),
            pl.ds(pl.multiple_of(y * side, side), side),
        ]

    def upper(p):
        starts = [sum(strips - r for r in range(s)) for s in range(strips)]
        x = sum((p >= start).astype(jnp.int32) for start in starts[1:])
        start = sum(
            jnp.where(x == s, starts[s], 0) for s in range(strips)
        )
        return x, p - start + x

    def kept_y(p, which):
        return span * lax.rem(p // (span * span) + which, 2) + lax.rem(p, span)

    @pl.loop(0, diags * span)
    def _(p):
        x, y = upper(p)
        pltpu.make_async_copy(block_of(ab, x, y), straight.at[p], load_sem.at[0]).start()
        pltpu.make_async_copy(block_of(ab, y, x), mirrored.at[p], load_sem.at[1]).start()

    @pl.loop(0, keeps * span)
    def _(p):
        pltpu.make_async_copy(
            block_of(1 - ab, p // span, kept_y(p, ab)), outer.at[0, p], load_sem.at[2]
        ).start()
        pltpu.make_async_copy(
            block_of(1 - ab, kept_y(p, 1 - ab), p // span), outer.at[1, p], load_sem.at[3]
        ).start()

    def masked(block, tile, x):
        pairs = side // 2
        mask = mask_ref[tile, pl.ds(pl.multiple_of(x * pairs, pairs), pairs)]
        value = block.reshape(pairs, 2, side, depth) * mask[:, None]
        return value.reshape(side * side, depth)

    area = side * side
    row_at = lax.broadcasted_iota(jnp.int32, (area, area), 0)
    col_at = lax.broadcasted_iota(jnp.int32, (area, area), 1)
    turn_rows = (row_at == lax.rem(col_at, side) * side + col_at // side).astype(jnp.bfloat16)

    def turned(value):
        product = jnp.dot(turn_rows, value, preferred_element_type=jnp.float32)
        return product.astype(jnp.bfloat16).reshape(side, side, depth)

    def prepare_diag(p):
        x, y = upper(p)
        straight[p] = masked(straight[p], ab, x).reshape(side, side, depth)
        mirrored[p] = turned(masked(mirrored[p], ab, y))

    def prepare_outer(p):
        outer[0, p] = masked(outer[0, p], 1 - ab, p // span).reshape(side, side, depth)
        outer[1, p] = turned(masked(outer[1, p], 1 - ab, kept_y(p, 1 - ab)))

    barrier = pltpu.get_barrier_semaphore()

    @pl.loop(1, count)
    def _(j):
        pl.semaphore_signal(
            barrier, inc=1, device_id=(ab, lax.rem(cd + j, count)), device_id_type=MESH
        )

    pl.semaphore_signal(barrier, inc=1, device_id=across, device_id_type=MESH)
    pl.semaphore_wait(barrier, count)

    def rows_of(source):
        return pl.ds(pl.multiple_of(source * rows, rows), rows)

    def cols_of(side):
        return pl.ds(pl.multiple_of(side * piece, piece), piece)

    def scatter(group, target, source):
        return remote(
            state_ref.at[rows_of(group), cols_of(target)],
            low.at[0, group, rows_of(source), cols_of(ab)],
            a_send.at[group, target], a_recv.at[group, source], (ab, target),
        )

    def stay(group):
        return pltpu.make_async_copy(
            state_ref.at[rows_of(group), cols_of(cd)],
            low.at[0, group, rows_of(cd), cols_of(ab)],
            self_sem.at[group],
        )

    def forward(group, source, side):
        block = low.at[0, group, rows_of(source), cols_of(side)]
        return remote(block, block, b_send.at[group, source], b_recv.at[group, source], across)

    def other(j):
        return sum(
            lax.rem(own[bit] + bit_of(j, bit), 2) * (1 << bit) for bit in range(bits)
        )

    odd = lax.rem(lax.broadcasted_iota(jnp.int32, (rows, 128), 0), 2) == 1

    def pass_on(group, i):
        @pl.when(i == 0)
        def _():
            stay(group).wait()
            forward(group, cd, ab).start()

        @pl.when(i != 0)
        def _():
            source = other(i)
            scatter(group, cd, source).wait_recv()
            forward(group, source, ab).start()

    def take_in(group, i):
        source = other(i)
        forward(group, source, 1 - ab).wait_recv()
        at = rows_of(source)
        same = diagonal_ref[group, at, :] != 0
        for lane in range(0, depth, 128):
            value = low[0, group, at, lane : lane + 128].astype(jnp.float32)
            mate = jnp.where(odd, pltpu.roll(value, 1, 0), pltpu.roll(value, rows - 1, 0))
            value = jnp.where(same, value, mate)
            low[1, group, at, lane : lane + 128] = value.astype(jnp.bfloat16)

    def send_group(group):
        stay(group).start()

        @pl.loop(1, count)
        def _(i):
            scatter(group, other(i), cd).start()

    send_group(0)

    @pl.loop(0, count)
    def _(i):
        pass_on(0, i)

        @pl.when(i == 0)
        def _():
            pltpu.make_async_copy(straight, straight, load_sem.at[0]).wait()
            pltpu.make_async_copy(mirrored, mirrored, load_sem.at[1]).wait()

        @pl.when(i < diags * span)
        def _():
            prepare_diag(i)

        late = i - (count - keeps * span)

        @pl.when(late == 0)
        def _():
            pltpu.make_async_copy(outer.at[0], outer.at[0], load_sem.at[2]).wait()
            pltpu.make_async_copy(outer.at[1], outer.at[1], load_sem.at[3]).wait()

        @pl.when(late >= 0)
        def _():
            prepare_outer(late)

    if groups > 1:
        send_group(1)

    @pl.loop(0, count)
    def _(i):
        take_in(0, i)

    def at(stage, index, which):
        lead = (slice(None),) * (bits - 1 - stage)
        return held[stage].at[(index,) + lead + (which,)]

    def place(q):
        inside = lax.rem(q, finals)
        turn = inside // 2
        diag = jnp.where(turn == keeps, 3 * keeps, 3 * turn + 1)
        return q // finals * products + jnp.where(lax.rem(inside, 2) == 0, diag, 3 * turn + 2)

    def core_copy(u):
        return remote(
            at(0, u, 1 - own[0]), held[1].at[u], core_send.at[u], core_recv.at[u], partner[0]
        )

    def y_copy(j):
        sent = j // keeps * products + 3 * lax.rem(j, keeps)
        return remote(held[1].at[sent], part_y.at[j], y_send.at[j], y_recv.at[j], across)

    def stage_copy(stage, q):
        source = at(1, place(q), 1 - own[1]) if stage == 1 else at(stage, q, 1 - own[stage])
        return remote(
            source, held[stage + 1].at[q],
            send_sem.at[stage - 1, q], recv_sem.at[stage - 1, q], partner[stage],
        )

    def last_copy(j):
        return remote(final.at[j], landed.at[j], last_send.at[j], last_recv.at[j], across)

    def put(u, product):
        value = product.astype(jnp.bfloat16)
        for block in range(count):
            index = tuple((block >> (bits - 1 - axis)) & 1 for axis in range(bits))
            part[(u,) + index] = value[block * rows : (block + 1) * rows]

    def rows_at(start):
        return pl.ds(pl.multiple_of(start, width), width)

    def blocks_at(turn):
        return pl.ds(turn * span, span)

    def dot(left, right):
        return lax.dot_general(left, right, NT, preferred_element_type=jnp.float32)

    y_lag = 8
    lags = [11 + 3 * stage for stage in range(bits - 1)]
    sources = count // 8

    @pl.loop(0, (products * (groups * finals - 1)) // finals + lags[-1] + 1)
    def _(step):
        group = step // products
        turn = lax.rem(step, products) // 3
        kind = lax.rem(lax.rem(step, products), 3)
        last = lax.rem(step, products) == 3 * keeps

        @pl.when((group < groups) & ((kind == 1) | last))
        def _():
            total = dot(low[0, group], straight[blocks_at(turn)].reshape(width, depth))
            total += dot(low[1, group], mirrored[blocks_at(turn)].reshape(width, depth))
            put(step, total)
            core_copy(step).start()

        @pl.when((group < groups) & (kind != 1) & ~last)
        def _():
            sent = 1 - kind // 2
            right = outer[sent, blocks_at(turn)].reshape(width, depth)
            put(step, dot(low[sent, group], right))
            core_copy(step).start()

        u = step - 1

        @pl.when((u >= 0) & (u < groups * products))
        def _():
            core_copy(u).wait_recv()
            held[1][u] = held[1][u] + at(0, u, own[0])[...]
            u_group = u // products
            u_step = lax.rem(u, products)
            u_kind = lax.rem(u_step, 3)

            @pl.when((u_kind == 1) | (u_step == 3 * keeps))
            def _():
                stage_copy(1, u_group * finals + 2 * (u_step // 3)).start()

            @pl.when((u_kind == 0) & (u_step < 3 * keeps))
            def _():
                y_copy(u_group * keeps + u_step // 3).start()

        arriving = lax.rem(step, products)

        @pl.when((group + 2 < groups) & (arriving == 9))
        def _():
            send_group(group + 2)

        @pl.when((group + 1 < groups) & (arriving >= 0) & (arriving < 8))
        def _():
            for i in range(sources):
                pass_on(group + 1, (arriving - 0) * sources + i)

        @pl.when((group + 1 < groups) & (arriving >= 9) & (arriving < 13))
        def _():
            for i in range(2 * sources):
                take_in(group + 1, (arriving - 9) * 2 * sources + i)

        v = step - y_lag
        v_step = lax.rem(v + products, products)

        @pl.when(
            (v >= 0) & (v < groups * products) & (lax.rem(v_step, 3) == 0) & (v_step < 3 * keeps)
        )
        def _():
            j = v_step // 3
            y_copy(v // products * keeps + j).wait_recv()
            held[1][v + 2] = held[1][v + 2] + part_y[v // products * keeps + j]
            stage_copy(1, v // products * finals + 2 * j + 1).start()

        for stage in range(1, bits):
            w = step - lags[stage - 1]
            q = (finals * w + products - 1) // products

            @pl.when((w >= 0) & ((products * q) // finals == w) & (q < groups * finals))
            def _():
                stage_copy(stage, q).wait_recv()
                index = place(q) if stage == 1 else q
                mine = at(stage, index, own[stage])[...]
                if stage < bits - 1:
                    held[stage + 1][q] = held[stage + 1][q] + mine
                    stage_copy(stage + 1, q).start()
                else:
                    total = held[stage + 1][q].astype(jnp.float32) + mine.astype(jnp.float32)
                    inside = lax.rem(q, finals)
                    kept = lax.rem(inside, 2) == 1
                    start = jnp.where(kept, diags + inside // 2, inside // 2) * width
                    sums_ref[rows_of(q // finals), rows_at(start)] = total

                    @pl.when(kept)
                    def _():
                        j = q // finals * keeps + inside // 2
                        final[j] = total.astype(jnp.bfloat16)
                        last_copy(j).start()

    @pl.loop(0, groups)
    def _(group):
        for j in range(keeps):
            last_copy(group * keeps + j).wait_recv()
            other_ref[rows_of(group), j * width : (j + 1) * width] = landed[group * keeps + j]

    @pl.loop(0, groups)
    def _(group):
        @pl.loop(0, count)
        def _(i):
            @pl.when(i != cd)
            def _():
                scatter(group, i, cd).wait_send()

            forward(group, i, ab).wait_send()

    @pl.loop(0, groups * products)
    def _(u):
        core_copy(u).wait_send()

    @pl.loop(0, groups * keeps)
    def _(j):
        y_copy(j).wait_send()
        last_copy(j).wait_send()

    @pl.loop(0, groups * finals)
    def _(q):
        for stage in range(1, bits):
            stage_copy(stage, q).wait_send()


def iteration_sums(state, diagonal, mask, weights, width):
    rows = state.shape[0]
    groups = rows // GROUP
    count = diagonal.shape[1] // GROUP
    bits = count.bit_length() - 1
    tile_width, depth = weights.shape[1], weights.shape[3]
    keeps = tile_width // STRIP
    diags = keeps + 1
    span = width // (STRIP * STRIP)
    products, finals = 3 * keeps + 1, 2 * keeps + 1
    dma = pltpu.SemaphoreType.DMA
    block = (GROUP, width)
    square = (STRIP, STRIP, depth)
    return pl.pallas_call(
        functools.partial(iteration_kernel, bits, width, GROUP, groups),
        out_shape=(
            jax.ShapeDtypeStruct((rows, finals * width), jnp.float32),
            jax.ShapeDtypeStruct((rows, keeps * width), jnp.bfloat16),
        ),
        in_specs=[pl.BlockSpec(memory_space=pltpu.VMEM)] * 3
        + [pl.BlockSpec(memory_space=pl.ANY)],
        out_specs=[pl.BlockSpec(memory_space=pltpu.VMEM)] * 2,
        scratch_shapes=[
            pltpu.VMEM((2, groups, count * GROUP, depth), jnp.bfloat16),
            pltpu.VMEM((diags * span,) + square, jnp.bfloat16),
            pltpu.VMEM((diags * span,) + square, jnp.bfloat16),
            pltpu.VMEM((2, keeps * span) + square, jnp.bfloat16),
            pltpu.VMEM((groups * products,) + (2,) * bits + block, jnp.bfloat16),
            pltpu.VMEM((groups * keeps,) + (2,) * (bits - 1) + block, jnp.bfloat16),
            pltpu.VMEM((groups * products,) + (2,) * (bits - 1) + block, jnp.bfloat16),
            *[
                pltpu.VMEM((groups * finals,) + (2,) * (bits - 1 - s) + block, jnp.bfloat16)
                for s in range(1, bits)
            ],
            pltpu.VMEM((groups * keeps,) + block, jnp.bfloat16),
            pltpu.VMEM((groups * keeps,) + block, jnp.bfloat16),
            dma((4,)), dma((groups,)),
            *[dma((groups, count))] * 4,
            *[dma((groups * products,))] * 2,
            *[dma((groups * keeps,))] * 2,
            *[dma((bits - 1, groups * finals))] * 2,
            *[dma((groups * keeps,))] * 2,
        ],
        compiler_params=pltpu.CompilerParams(
            collective_id=1, has_side_effects=True, vmem_limit_bytes=60 * 2**20
        ),
    )(state, diagonal, mask, weights)


def update_kernel(
    strips, side, span,
    sums_ref, other_ref, driver_ref, cols_ref, rows_ref, same_ref, next_ref,
):
    ab = lax.axis_index("ab")
    rows = driver_ref.shape[0]
    area = side * side
    wide = strips * area
    tile_area = strips * wide
    uppers = [(x, y) for x in range(strips) for y in range(x, strips)]

    def iotas(size):
        return (lax.broadcasted_iota(jnp.int32, (size, size), axis) for axis in (0, 1))

    start, end = iotas(area)
    turn = (start == lax.rem(end, side) * side + end // side).astype(jnp.bfloat16)
    start, end = iotas(wide)
    block, inner = lax.rem(end, strips * side) // side, lax.rem(end, side)
    ordered = start == block * area + end // (strips * side) * side + inner
    ordered = ordered.astype(jnp.bfloat16)
    odd = lax.rem(lax.broadcasted_iota(jnp.int32, (rows, area), 0), 2) == 1
    same = jnp.broadcast_to(same_ref[:, 0:1], (rows, area)) != 0

    def swap(value):
        return jnp.where(
            same, value, jnp.where(odd, pltpu.roll(value, 1, 0), pltpu.roll(value, rows - 1, 0))
        )

    def sums_of(index):
        return sums_ref[:, index * area : (index + 1) * area]

    def exact_dot(value, right):
        high = value.astype(jnp.bfloat16)
        rest = (value - high.astype(jnp.float32)).astype(jnp.bfloat16)
        return jnp.dot(high, right, preferred_element_type=jnp.float32) + jnp.dot(
            rest, right, preferred_element_type=jnp.float32
        )

    lower = [swap(sums_of(p)) for p, (x, y) in enumerate(uppers) if x < y]
    turned = exact_dot(jnp.concatenate(lower), turn)
    diag, taken = {}, 0
    for p, (x, y) in enumerate(uppers):
        diag[x, y] = sums_of(p)
        if x < y:
            diag[y, x] = turned[taken * rows : (taken + 1) * rows]
            taken += 1
    came = [
        swap(other_ref[:, p * area : (p + 1) * area].astype(jnp.float32))
        for p in range(strips * span)
    ]
    came = jnp.dot(
        jnp.concatenate(came).astype(jnp.bfloat16), turn, preferred_element_type=jnp.float32
    )
    even = ab == 0
    off = {}
    for x in range(strips):
        for y in range(strips):
            kept = sums_of(len(uppers) + x * span + y % span)
            p = y * span + x % span
            sent = came[p * rows : (p + 1) * rows]
            if x // span == y // span:
                off[x, y] = jnp.where(even, kept, sent)
            else:
                off[x, y] = jnp.where(even, sent, kept)
    for tile, blocks in ((ab, diag), (1 - ab, off)):
        for x in range(strips):
            line = jnp.concatenate([blocks[x, y] for y in range(strips)], axis=1)
            symmetric = exact_dot(line, ordered)
            at = pl.ds(pl.multiple_of(tile * tile_area + x * wide, wide), wide)
            below = cols_ref[:, at] - rows_ref[:, 0:1]
            next_ref[:, at] = ((driver_ref[:, at] + symmetric) / below).astype(next_ref.dtype)


def update(sums, other, driver, col_energy, row_energy, same, tile_width, width, dtype):
    strips = tile_width // STRIP
    span = width // (STRIP * STRIP)
    return pl.pallas_call(
        functools.partial(update_kernel, strips, STRIP, span),
        out_shape=jax.ShapeDtypeStruct(driver.shape, dtype),
        in_specs=[pl.BlockSpec(memory_space=pltpu.VMEM)] * 6,
        out_specs=pl.BlockSpec(memory_space=pltpu.VMEM),
        compiler_params=pltpu.CompilerParams(vmem_limit_bytes=48 * 2**20),
    )(sums, other, driver, col_energy, row_energy, same)


def body(amplitudes, driver, ladder, block_mask, pair_list, occ_energy, virt_energy):
    ab_count = lax.axis_size("ab")
    ab_index = lax.axis_index("ab")
    cd_index = lax.axis_index("cd")
    rows_dev, cols_dev = amplitudes.shape
    out_rows, in_cols = ladder.shape
    tile_width = NV // ab_count
    tile_area = tile_width * tile_width
    strip = min(STRIP, tile_width)
    strips = tile_width // strip
    diag_cols = sum(strip * (tile_width - s * strip) for s in range(strips))
    width = min(512, tile_area)

    paired = (
        ab_count == 2
        and tile_width % (2 * STRIP) == 0
        and width == 2 * STRIP * STRIP
        and diag_cols == (strips + 1) * width
        and rows_dev % GROUP == 0
        and lax.axis_size("cd") >= 2 * (strips + 1)
        and lax.axis_size("cd") % 8 == 0
        and lax.axis_size("cd").bit_count() == 1
    )
    weights = ladder.reshape(out_rows // BLK, BLK, in_cols // BLK, BLK)
    weights = (weights * block_mask.astype(jnp.bfloat16)[:, None, :, None]).reshape(
        ab_count, tile_width, tile_width, in_cols
    )
    diag_tile = lax.dynamic_index_in_dim(weights, ab_index, 0, keepdims=False)

    def pack(tile):
        return jnp.concatenate(
            [
                tile[s * strip : (s + 1) * strip, s * strip :].reshape(-1, in_cols)
                for s in range(strips)
            ]
        )

    others = [
        lax.dynamic_index_in_dim(
            weights, lax.rem(ab_index + j, ab_count), 0, keepdims=False
        ).reshape(tile_area, in_cols)
        for j in range(1, ab_count)
    ]
    straight = jnp.concatenate([pack(diag_tile)] + others)
    mirrored = pack(jnp.swapaxes(diag_tile, 0, 1))

    pairs_local = ab_index * cols_dev + jnp.arange(cols_dev, dtype=jnp.int32)
    big_a = pairs_local // (tile_width * NV)
    big_b = pairs_local // tile_area % ab_count
    first = big_a * tile_width + pairs_local // tile_width % tile_width
    second = big_b * tile_width + pairs_local % tile_width
    virt_index = jnp.arange(NV, dtype=jnp.int32)
    picks = (first[:, None] == virt_index).astype(jnp.float32) + (
        second[:, None] == virt_index
    ).astype(jnp.float32)
    col_energy = jnp.dot(picks, virt_energy, precision=lax.Precision.HIGHEST)
    row_pairs = lax.dynamic_slice_in_dim(pair_list, cd_index * rows_dev, rows_dev)
    occ_index = jnp.arange(NOCC, dtype=jnp.int32)
    occ_picks = (row_pairs[:, None] // NOCC == occ_index).astype(jnp.float32)
    occ_picks = occ_picks + (row_pairs[:, None] % NOCC == occ_index).astype(jnp.float32)
    row_energy = jnp.dot(occ_picks, occ_energy, precision=lax.Precision.HIGHEST)
    denominator = col_energy[None, :] - row_energy[:, None]

    def swap_matrix(listed):
        diagonal = listed // NOCC == listed % NOCC
        index = jnp.arange(listed.shape[0], dtype=jnp.int32)
        mirror_row = jnp.where(diagonal, index, index ^ 1)
        return (mirror_row[:, None] == index).astype(jnp.bfloat16)

    row_swap = swap_matrix(row_pairs)
    all_swap = swap_matrix(pair_list)

    def spread(packed):
        pieces, start = [], 0
        for s in range(strips):
            wide = tile_width - s * strip
            piece = packed[:, start : start + strip * wide].reshape(rows_dev, strip, wide)
            start += strip * wide
            piece = jnp.concatenate([0.5 * piece[:, :, :strip], piece[:, :, strip:]], axis=2)
            pieces.append(jnp.pad(piece, ((0, 0), (0, 0), (s * strip, 0))))
        return jnp.concatenate(pieces, axis=1).reshape(rows_dev, tile_area)

    diag_rows = (pair_list // NOCC == pair_list % NOCC).astype(jnp.float32)
    diag_rows = jnp.broadcast_to(diag_rows[:, None], (pair_list.shape[0], 128))
    row_same = (row_pairs // NOCC == row_pairs % NOCC).astype(jnp.float32)

    def lanes(values):
        return jnp.broadcast_to(values[:, None], (values.shape[0], 128))

    if paired:
        masks = block_mask.astype(jnp.bfloat16).reshape(ab_count, tile_area // BLK, 1, -1, 1)
        masks = jnp.broadcast_to(
            masks, (ab_count, tile_area // BLK, STRIP, in_cols // BLK, BLK)
        ).reshape(ab_count, tile_area // BLK, STRIP, in_cols)
        tiles_in = ladder.reshape(ab_count, tile_width, tile_width, in_cols)
        first_energy = lax.dynamic_slice_in_dim(virt_energy, ab_index * tile_width, tile_width)
        tile_energy = (
            first_energy[None, :, None] + virt_energy.reshape(ab_count, 1, tile_width)
        ).reshape(1, cols_dev)
        diag_rows = diag_rows.reshape(-1, rows_dev // GROUP, GROUP, 128)
        diag_rows = jnp.swapaxes(diag_rows, 0, 1).reshape(rows_dev // GROUP, -1, 128)
        state = amplitudes.astype(jnp.bfloat16)
        for step in range(ITERS):
            sums, other = iteration_sums(state, diag_rows, masks, tiles_in, width)
            state = update(
                sums, other, driver, tile_energy, lanes(row_energy), lanes(row_same),
                tile_width, width, jnp.bfloat16 if step < ITERS - 1 else jnp.float32,
            )
        return state

    state = amplitudes
    for step in range(ITERS):
        rounded = state.astype(jnp.bfloat16)
        regrouped = lax.all_to_all(rounded, "cd", split_axis=1, concat_axis=0, tiled=True)
        low = lax.all_gather(regrouped, "ab", axis=1, tiled=True)
        swapped_low = jnp.dot(all_swap, low, preferred_element_type=jnp.float32)
        sums = ladder_sums(
            low, swapped_low.astype(jnp.bfloat16), straight, mirrored, rows_dev, width
        )
        parts = [spread(sums[:, :diag_cols])]
        for j in range(1, ab_count):
            start = diag_cols + (j - 1) * tile_area
            parts.append(sums[:, start : start + tile_area])
        placed = jnp.concatenate(parts, axis=1)
        received = jnp.roll(placed.reshape(rows_dev, ab_count, tile_area), ab_index, axis=1)
        received = received.reshape(rows_dev, cols_dev)
        swapped = jnp.dot(
            row_swap, received.astype(jnp.bfloat16), preferred_element_type=jnp.float32
        )
        tiles = lax.all_to_all(
            swapped.astype(jnp.bfloat16).reshape(rows_dev, ab_count, tile_area),
            "ab",
            split_axis=1,
            concat_axis=1,
            tiled=True,
        )
        symmetric = received + flip_tiles(tiles, tile_width).astype(jnp.float32)
        state = (driver + symmetric) / denominator
    return state


def solution(mesh):
    placed = (P("cd", "ab"), P("cd", "ab"), P("ab", "cd"), P("ab", "cd"), P(), P(), P())
    return jax.shard_map(body, mesh=mesh, in_specs=placed, out_specs=P("cd", "ab"), check_vma=False)
```

```python
import functools

import jax
import jax.numpy as jnp
from jax import lax
from jax.experimental import pallas as pl
from jax.experimental.pallas import tpu as pltpu
from jax.sharding import PartitionSpec as P

NV = 128
NOCC = 32
BLK = 128
ITERS = 2
STRIP = 16
GROUP = 16
MESH = pl.DeviceIdType.MESH
NT = (((1,), (1,)), ((), ()))


def flip_tiles(tiles, tile_width):
    row_count, tile_count = tiles.shape[:2]
    turned = jnp.swapaxes(tiles.reshape(row_count, tile_count, tile_width, tile_width), 2, 3)
    return turned.reshape(row_count, tile_count * tile_width * tile_width)


def bit_of(index, bit):
    return lax.rem(index // (1 << bit), 2)


def flip_bit(index, bit):
    return index + (1 - 2 * bit_of(index, bit)) * (1 << bit)


def ladder_kernel(
    bits, chunks, diag_chunks, width,
    low_ref, swap_ref, straight_ref, mirrored_ref, out_ref,
    straight, mirrored, *rest,
):
    held = rest[: bits + 1]
    load_sem, mirror_sem, send_sem, recv_sem = rest[bits + 1 :]
    ab = lax.axis_index("ab")
    cd = lax.axis_index("cd")
    rows = out_ref.shape[0]
    own = [bit_of(cd, bit) for bit in range(bits)]
    partner = [(ab, flip_bit(cd, bit)) for bit in range(bits)]

    def at(stage, chunk, which):
        lead = (slice(None),) * (bits - 1 - stage)
        return held[stage].at[(chunk,) + lead + (which,)]

    def copy(stage, chunk):
        return pltpu.make_async_remote_copy(
            src_ref=at(stage, chunk, 1 - own[stage]),
            dst_ref=held[stage + 1].at[chunk],
            send_sem=send_sem.at[stage, chunk],
            recv_sem=recv_sem.at[stage, chunk],
            device_id=partner[stage],
            device_id_type=MESH,
        )

    def load_straight(chunk):
        start = pl.multiple_of(chunk * width, width)
        return pltpu.make_async_copy(
            straight_ref.at[pl.ds(start, width)], straight.at[chunk], load_sem.at[chunk]
        )

    def load_mirrored(chunk):
        start = pl.multiple_of(chunk * width, width)
        return pltpu.make_async_copy(
            mirrored_ref.at[pl.ds(start, width)], mirrored.at[chunk], mirror_sem.at[chunk]
        )

    @pl.loop(0, diag_chunks)
    def _(chunk):
        load_straight(chunk).start()
        load_mirrored(chunk).start()

    @pl.loop(diag_chunks, chunks)
    def _(chunk):
        load_straight(chunk).start()

    barrier = pltpu.get_barrier_semaphore()
    for device in partner:
        pl.semaphore_signal(barrier, inc=1, device_id=device, device_id_type=MESH)
    pl.semaphore_wait(barrier, bits)

    def put(chunk, product):
        value = product.astype(jnp.bfloat16)
        for block in range(1 << bits):
            index = tuple((block >> (bits - 1 - axis)) & 1 for axis in range(bits))
            held[0][(chunk,) + index] = value[block * rows : (block + 1) * rows]

    @pl.loop(0, chunks + 2 * bits)
    def _(step):
        @pl.when(step < diag_chunks)
        def _():
            load_straight(step).wait()
            load_mirrored(step).wait()
            total = lax.dot_general(
                low_ref[...], straight[step], NT, preferred_element_type=jnp.float32
            )
            total += lax.dot_general(
                swap_ref[...], mirrored[step], NT, preferred_element_type=jnp.float32
            )
            put(step, total)
            copy(0, step).start()

        @pl.when((step >= diag_chunks) & (step < chunks))
        def _():
            load_straight(step).wait()
            put(
                step,
                lax.dot_general(
                    low_ref[...], straight[step], NT, preferred_element_type=jnp.float32
                ),
            )
            copy(0, step).start()

        for stage in range(bits):
            chunk = step - (2 * stage + 1)

            @pl.when((chunk >= 0) & (chunk < chunks))
            def _():
                copy(stage, chunk).wait_recv()
                mine = at(stage, chunk, own[stage])[...].astype(jnp.float32)
                total = held[stage + 1][chunk].astype(jnp.float32) + mine
                if stage < bits - 1:
                    held[stage + 1][chunk] = total.astype(jnp.bfloat16)
                    copy(stage + 1, chunk).start()
                else:
                    out_ref[:, pl.ds(pl.multiple_of(chunk * width, width), width)] = total

    @pl.loop(0, chunks)
    def _(chunk):
        for stage in range(bits):
            copy(stage, chunk).wait_send()


def ladder_sums(low, swapped, straight, mirrored, rows, width):
    count = low.shape[0] // rows
    bits = count.bit_length() - 1
    depth = low.shape[1]
    chunks = straight.shape[0] // width
    diag_chunks = mirrored.shape[0] // width
    held = [
        pltpu.VMEM((chunks,) + (2,) * (bits - stage) + (rows, width), jnp.bfloat16)
        for stage in range(bits + 1)
    ]
    return pl.pallas_call(
        functools.partial(ladder_kernel, bits, chunks, diag_chunks, width),
        out_shape=jax.ShapeDtypeStruct((rows, chunks * width), jnp.float32),
        in_specs=[pl.BlockSpec(memory_space=pltpu.VMEM)] * 2
        + [pl.BlockSpec(memory_space=pl.ANY)] * 2,
        out_specs=pl.BlockSpec(memory_space=pltpu.VMEM),
        scratch_shapes=[
            pltpu.VMEM((chunks, width, depth), jnp.bfloat16),
            pltpu.VMEM((diag_chunks, width, depth), jnp.bfloat16),
            *held,
            pltpu.SemaphoreType.DMA((chunks,)),
            pltpu.SemaphoreType.DMA((diag_chunks,)),
            pltpu.SemaphoreType.DMA((bits, chunks)),
            pltpu.SemaphoreType.DMA((bits, chunks)),
        ],
        compiler_params=pltpu.CompilerParams(
            collective_id=0, has_side_effects=True, vmem_limit_bytes=58 * 2**20
        ),
    )(low, swapped, straight, mirrored)


def iteration_kernel(
    bits, width, rows, groups,
    state_ref, diagonal_ref, mask_ref, weight_ref, sums_ref, other_ref,
    state, low, straight, mirrored, outer, part, part_y, *rest,
):
    held = (part,) + rest[:bits]
    final, landed = rest[bits : bits + 2]
    (
        load_sem, self_sem, a_send, a_recv, b_send, b_recv,
        core_send, core_recv, y_send, y_recv, send_sem, recv_sem, last_send, last_recv,
    ) = rest[bits + 2 :]
    ab = lax.axis_index("ab")
    cd = lax.axis_index("cd")
    count = 1 << bits
    side = straight.shape[1]
    strips = weight_ref.shape[1] // side
    depth = weight_ref.shape[3]
    piece = depth // 2
    keeps = strips
    span = width // (side * side)
    diags = keeps + 1
    products = 3 * keeps + 1
    finals = diags + keeps
    own = [bit_of(cd, bit) for bit in range(bits)]
    partner = [(ab, flip_bit(cd, bit)) for bit in range(bits)]
    across = (1 - ab, cd)

    def remote(src, dst, send, recv, device):
        return pltpu.make_async_remote_copy(
            src_ref=src, dst_ref=dst, send_sem=send, recv_sem=recv,
            device_id=device, device_id_type=MESH,
        )

    def block_of(tile, x, y):
        return weight_ref.at[
            tile,
            pl.ds(pl.multiple_of(x * side, side), side),
            pl.ds(pl.multiple_of(y * side, side), side),
        ]

    def upper(p):
        starts = [sum(strips - r for r in range(s)) for s in range(strips)]
        x = sum((p >= start).astype(jnp.int32) for start in starts[1:])
        start = sum(
            jnp.where(x == s, starts[s], 0) for s in range(strips)
        )
        return x, p - start + x

    def kept_y(p, which):
        return span * lax.rem(p // (span * span) + which, 2) + lax.rem(p, span)

    @pl.loop(0, diags * span)
    def _(p):
        x, y = upper(p)
        pltpu.make_async_copy(block_of(ab, x, y), straight.at[p], load_sem.at[0]).start()
        pltpu.make_async_copy(block_of(ab, y, x), mirrored.at[p], load_sem.at[1]).start()

    @pl.loop(0, keeps * span)
    def _(p):
        pltpu.make_async_copy(
            block_of(1 - ab, p // span, kept_y(p, ab)), outer.at[0, p], load_sem.at[2]
        ).start()
        pltpu.make_async_copy(
            block_of(1 - ab, kept_y(p, 1 - ab), p // span), outer.at[1, p], load_sem.at[3]
        ).start()

    def masked(block, tile, x):
        pairs = side // 2
        mask = mask_ref[tile, pl.ds(pl.multiple_of(x * pairs, pairs), pairs)]
        value = block.reshape(pairs, 2, side, depth) * mask[:, None]
        return value.reshape(side * side, depth)

    area = side * side
    row_at = lax.broadcasted_iota(jnp.int32, (area, area), 0)
    col_at = lax.broadcasted_iota(jnp.int32, (area, area), 1)
    turn_rows = (row_at == lax.rem(col_at, side) * side + col_at // side).astype(jnp.bfloat16)

    def turned(value):
        product = jnp.dot(turn_rows, value, preferred_element_type=jnp.float32)
        return product.astype(jnp.bfloat16).reshape(side, side, depth)

    def prepare_diag(p):
        x, y = upper(p)
        straight[p] = masked(straight[p], ab, x).reshape(side, side, depth)
        mirrored[p] = turned(masked(mirrored[p], ab, y))

    def prepare_outer(p):
        outer[0, p] = masked(outer[0, p], 1 - ab, p // span).reshape(side, side, depth)
        outer[1, p] = turned(masked(outer[1, p], 1 - ab, kept_y(p, 1 - ab)))

    state[...] = state_ref[...].astype(jnp.bfloat16)
    barrier = pltpu.get_barrier_semaphore()

    @pl.loop(1, count)
    def _(j):
        pl.semaphore_signal(
            barrier, inc=1, device_id=(ab, lax.rem(cd + j, count)), device_id_type=MESH
        )

    pl.semaphore_signal(barrier, inc=1, device_id=across, device_id_type=MESH)
    pl.semaphore_wait(barrier, count)

    def rows_of(source):
        return pl.ds(pl.multiple_of(source * rows, rows), rows)

    def cols_of(side):
        return pl.ds(pl.multiple_of(side * piece, piece), piece)

    def scatter(group, target, source):
        return remote(
            state.at[rows_of(group), cols_of(target)],
            low.at[0, group, rows_of(source), cols_of(ab)],
            a_send.at[group, target], a_recv.at[group, source], (ab, target),
        )

    def stay(group):
        return pltpu.make_async_copy(
            state.at[rows_of(group), cols_of(cd)],
            low.at[0, group, rows_of(cd), cols_of(ab)],
            self_sem.at[group],
        )

    def forward(group, source, side):
        block = low.at[0, group, rows_of(source), cols_of(side)]
        return remote(block, block, b_send.at[group, source], b_recv.at[group, source], across)

    def other(j):
        return sum(
            lax.rem(own[bit] + bit_of(j, bit), 2) * (1 << bit) for bit in range(bits)
        )

    odd = lax.rem(lax.broadcasted_iota(jnp.int32, (rows, 128), 0), 2) == 1

    def pass_on(group, i):
        @pl.when(i == 0)
        def _():
            stay(group).wait()
            forward(group, cd, ab).start()

        @pl.when(i != 0)
        def _():
            source = other(i)
            scatter(group, cd, source).wait_recv()
            forward(group, source, ab).start()

    def take_in(group, i):
        source = other(i)
        forward(group, source, 1 - ab).wait_recv()
        at = rows_of(source)
        same = diagonal_ref[group, at, :] != 0
        for lane in range(0, depth, 128):
            value = low[0, group, at, lane : lane + 128].astype(jnp.float32)
            mate = jnp.where(odd, pltpu.roll(value, 1, 0), pltpu.roll(value, rows - 1, 0))
            value = jnp.where(same, value, mate)
            low[1, group, at, lane : lane + 128] = value.astype(jnp.bfloat16)

    def send_group(group):
        stay(group).start()

        @pl.loop(1, count)
        def _(i):
            scatter(group, other(i), cd).start()

    send_group(0)

    @pl.loop(0, count)
    def _(i):
        pass_on(0, i)

        @pl.when(i == 0)
        def _():
            pltpu.make_async_copy(straight, straight, load_sem.at[0]).wait()
            pltpu.make_async_copy(mirrored, mirrored, load_sem.at[1]).wait()

        @pl.when(i < diags * span)
        def _():
            prepare_diag(i)

        late = i - (count - keeps * span)

        @pl.when(late == 0)
        def _():
            pltpu.make_async_copy(outer.at[0], outer.at[0], load_sem.at[2]).wait()
            pltpu.make_async_copy(outer.at[1], outer.at[1], load_sem.at[3]).wait()

        @pl.when(late >= 0)
        def _():
            prepare_outer(late)

    if groups > 1:
        send_group(1)

    @pl.loop(0, count)
    def _(i):
        take_in(0, i)

    def at(stage, index, which):
        lead = (slice(None),) * (bits - 1 - stage)
        return held[stage].at[(index,) + lead + (which,)]

    def place(q):
        inside = lax.rem(q, finals)
        turn = inside // 2
        diag = jnp.where(turn == keeps, 3 * keeps, 3 * turn + 1)
        return q // finals * products + jnp.where(lax.rem(inside, 2) == 0, diag, 3 * turn + 2)

    def core_copy(u):
        return remote(
            at(0, u, 1 - own[0]), held[1].at[u], core_send.at[u], core_recv.at[u], partner[0]
        )

    def y_copy(j):
        sent = j // keeps * products + 3 * lax.rem(j, keeps)
        return remote(held[1].at[sent], part_y.at[j], y_send.at[j], y_recv.at[j], across)

    def stage_copy(stage, q):
        source = at(1, place(q), 1 - own[1]) if stage == 1 else at(stage, q, 1 - own[stage])
        return remote(
            source, held[stage + 1].at[q],
            send_sem.at[stage - 1, q], recv_sem.at[stage - 1, q], partner[stage],
        )

    def last_copy(j):
        return remote(final.at[j], landed.at[j], last_send.at[j], last_recv.at[j], across)

    def put(u, product):
        value = product.astype(jnp.bfloat16)
        for block in range(count):
            index = tuple((block >> (bits - 1 - axis)) & 1 for axis in range(bits))
            part[(u,) + index] = value[block * rows : (block + 1) * rows]

    def rows_at(start):
        return pl.ds(pl.multiple_of(start, width), width)

    def blocks_at(turn):
        return pl.ds(turn * span, span)

    def dot(left, right):
        return lax.dot_general(left, right, NT, preferred_element_type=jnp.float32)

    y_lag = 7
    lags = [10 + 3 * stage for stage in range(bits - 1)]
    sources = count // 8

    @pl.loop(0, (products * (groups * finals - 1)) // finals + lags[-1] + 1)
    def _(step):
        group = step // products
        turn = lax.rem(step, products) // 3
        kind = lax.rem(lax.rem(step, products), 3)
        last = lax.rem(step, products) == 3 * keeps

        @pl.when((group < groups) & ((kind == 1) | last))
        def _():
            total = dot(low[0, group], straight[blocks_at(turn)].reshape(width, depth))
            total += dot(low[1, group], mirrored[blocks_at(turn)].reshape(width, depth))
            put(step, total)
            core_copy(step).start()

        @pl.when((group < groups) & (kind != 1) & ~last)
        def _():
            sent = 1 - kind // 2
            right = outer[sent, blocks_at(turn)].reshape(width, depth)
            put(step, dot(low[sent, group], right))
            core_copy(step).start()

        u = step - 1

        @pl.when((u >= 0) & (u < groups * products))
        def _():
            core_copy(u).wait_recv()
            held[1][u] = held[1][u] + at(0, u, own[0])[...]
            u_group = u // products
            u_step = lax.rem(u, products)
            u_kind = lax.rem(u_step, 3)

            @pl.when((u_kind == 1) | (u_step == 3 * keeps))
            def _():
                stage_copy(1, u_group * finals + 2 * (u_step // 3)).start()

            @pl.when((u_kind == 0) & (u_step < 3 * keeps))
            def _():
                y_copy(u_group * keeps + u_step // 3).start()

        arriving = lax.rem(step, products)

        @pl.when((group + 2 < groups) & (arriving == 9))
        def _():
            send_group(group + 2)

        @pl.when((group + 1 < groups) & (arriving >= 0) & (arriving < 8))
        def _():
            for i in range(sources):
                pass_on(group + 1, (arriving - 0) * sources + i)

        @pl.when((group + 1 < groups) & (arriving >= 9) & (arriving < 13))
        def _():
            for i in range(2 * sources):
                take_in(group + 1, (arriving - 9) * 2 * sources + i)

        v = step - y_lag
        v_step = lax.rem(v + products, products)

        @pl.when(
            (v >= 0) & (v < groups * products) & (lax.rem(v_step, 3) == 0) & (v_step < 3 * keeps)
        )
        def _():
            j = v_step // 3
            y_copy(v // products * keeps + j).wait_recv()
            held[1][v + 2] = held[1][v + 2] + part_y[v // products * keeps + j]
            stage_copy(1, v // products * finals + 2 * j + 1).start()

        for stage in range(1, bits):
            w = step - lags[stage - 1]
            q = (finals * w + products - 1) // products

            @pl.when((w >= 0) & ((products * q) // finals == w) & (q < groups * finals))
            def _():
                stage_copy(stage, q).wait_recv()
                index = place(q) if stage == 1 else q
                mine = at(stage, index, own[stage])[...]
                if stage < bits - 1:
                    held[stage + 1][q] = held[stage + 1][q] + mine
                    stage_copy(stage + 1, q).start()
                else:
                    total = held[stage + 1][q].astype(jnp.float32) + mine.astype(jnp.float32)
                    inside = lax.rem(q, finals)
                    kept = lax.rem(inside, 2) == 1
                    start = jnp.where(kept, diags + inside // 2, inside // 2) * width
                    sums_ref[rows_of(q // finals), rows_at(start)] = total

                    @pl.when(kept)
                    def _():
                        j = q // finals * keeps + inside // 2
                        final[j] = total.astype(jnp.bfloat16)
                        last_copy(j).start()

    @pl.loop(0, groups)
    def _(group):
        for j in range(keeps):
            last_copy(group * keeps + j).wait_recv()
            other_ref[rows_of(group), j * width : (j + 1) * width] = landed[group * keeps + j]

    @pl.loop(0, groups)
    def _(group):
        @pl.loop(0, count)
        def _(i):
            @pl.when(i != cd)
            def _():
                scatter(group, i, cd).wait_send()

            forward(group, i, ab).wait_send()

    @pl.loop(0, groups * products)
    def _(u):
        core_copy(u).wait_send()

    @pl.loop(0, groups * keeps)
    def _(j):
        y_copy(j).wait_send()
        last_copy(j).wait_send()

    @pl.loop(0, groups * finals)
    def _(q):
        for stage in range(1, bits):
            stage_copy(stage, q).wait_send()


def iteration_sums(state, diagonal, mask, weights, width):
    rows = state.shape[0]
    groups = rows // GROUP
    count = diagonal.shape[1] // GROUP
    bits = count.bit_length() - 1
    tile_width, depth = weights.shape[1], weights.shape[3]
    keeps = tile_width // STRIP
    diags = keeps + 1
    span = width // (STRIP * STRIP)
    products, finals = 3 * keeps + 1, 2 * keeps + 1
    dma = pltpu.SemaphoreType.DMA
    block = (GROUP, width)
    square = (STRIP, STRIP, depth)
    return pl.pallas_call(
        functools.partial(iteration_kernel, bits, width, GROUP, groups),
        out_shape=(
            jax.ShapeDtypeStruct((rows, finals * width), jnp.float32),
            jax.ShapeDtypeStruct((rows, keeps * width), jnp.bfloat16),
        ),
        in_specs=[pl.BlockSpec(memory_space=pltpu.VMEM)] * 3
        + [pl.BlockSpec(memory_space=pl.ANY)],
        out_specs=[pl.BlockSpec(memory_space=pltpu.VMEM)] * 2,
        scratch_shapes=[
            pltpu.VMEM(state.shape, jnp.bfloat16),
            pltpu.VMEM((2, groups, count * GROUP, depth), jnp.bfloat16),
            pltpu.VMEM((diags * span,) + square, jnp.bfloat16),
            pltpu.VMEM((diags * span,) + square, jnp.bfloat16),
            pltpu.VMEM((2, keeps * span) + square, jnp.bfloat16),
            pltpu.VMEM((groups * products,) + (2,) * bits + block, jnp.bfloat16),
            pltpu.VMEM((groups * keeps,) + (2,) * (bits - 1) + block, jnp.bfloat16),
            pltpu.VMEM((groups * products,) + (2,) * (bits - 1) + block, jnp.bfloat16),
            *[
                pltpu.VMEM((groups * finals,) + (2,) * (bits - 1 - s) + block, jnp.bfloat16)
                for s in range(1, bits)
            ],
            pltpu.VMEM((groups * keeps,) + block, jnp.bfloat16),
            pltpu.VMEM((groups * keeps,) + block, jnp.bfloat16),
            dma((4,)), dma((groups,)),
            *[dma((groups, count))] * 4,
            *[dma((groups * products,))] * 2,
            *[dma((groups * keeps,))] * 2,
            *[dma((bits - 1, groups * finals))] * 2,
            *[dma((groups * keeps,))] * 2,
        ],
        compiler_params=pltpu.CompilerParams(
            collective_id=1 if state.dtype == jnp.bfloat16 else 2,
            has_side_effects=True,
            vmem_limit_bytes=60 * 2**20,
        ),
    )(state, diagonal, mask, weights)


def update_kernel(
    strips, side, span,
    sums_ref, other_ref, driver_ref, cols_ref, rows_ref, same_ref, next_ref,
):
    ab = lax.axis_index("ab")
    rows = driver_ref.shape[0]
    area = side * side
    wide = strips * area
    tile_area = strips * wide
    uppers = [(x, y) for x in range(strips) for y in range(x, strips)]

    def iotas(size):
        return (lax.broadcasted_iota(jnp.int32, (size, size), axis) for axis in (0, 1))

    start, end = iotas(area)
    turn = (start == lax.rem(end, side) * side + end // side).astype(jnp.bfloat16)
    start, end = iotas(wide)
    block, inner = lax.rem(end, strips * side) // side, lax.rem(end, side)
    ordered = start == block * area + end // (strips * side) * side + inner
    ordered = ordered.astype(jnp.bfloat16)
    odd = lax.rem(lax.broadcasted_iota(jnp.int32, (rows, area), 0), 2) == 1
    same = jnp.broadcast_to(same_ref[:, 0:1], (rows, area)) != 0

    def swap(value):
        return jnp.where(
            same, value, jnp.where(odd, pltpu.roll(value, 1, 0), pltpu.roll(value, rows - 1, 0))
        )

    def sums_of(index):
        return sums_ref[:, index * area : (index + 1) * area]

    def exact_dot(value, right):
        high = value.astype(jnp.bfloat16)
        rest = (value - high.astype(jnp.float32)).astype(jnp.bfloat16)
        return jnp.dot(high, right, preferred_element_type=jnp.float32) + jnp.dot(
            rest, right, preferred_element_type=jnp.float32
        )

    lower = [swap(sums_of(p)) for p, (x, y) in enumerate(uppers) if x < y]
    turned = exact_dot(jnp.concatenate(lower), turn)
    diag, taken = {}, 0
    for p, (x, y) in enumerate(uppers):
        diag[x, y] = sums_of(p)
        if x < y:
            diag[y, x] = turned[taken * rows : (taken + 1) * rows]
            taken += 1
    came = [
        swap(other_ref[:, p * area : (p + 1) * area].astype(jnp.float32))
        for p in range(strips * span)
    ]
    came = jnp.dot(
        jnp.concatenate(came).astype(jnp.bfloat16), turn, preferred_element_type=jnp.float32
    )
    even = ab == 0
    off = {}
    for x in range(strips):
        for y in range(strips):
            kept = sums_of(len(uppers) + x * span + y % span)
            p = y * span + x % span
            sent = came[p * rows : (p + 1) * rows]
            if x // span == y // span:
                off[x, y] = jnp.where(even, kept, sent)
            else:
                off[x, y] = jnp.where(even, sent, kept)
    for tile, blocks in ((ab, diag), (1 - ab, off)):
        for x in range(strips):
            line = jnp.concatenate([blocks[x, y] for y in range(strips)], axis=1)
            symmetric = exact_dot(line, ordered)
            at = pl.ds(pl.multiple_of(tile * tile_area + x * wide, wide), wide)
            below = cols_ref[:, at] - rows_ref[:, 0:1]
            next_ref[:, at] = ((driver_ref[:, at] + symmetric) / below).astype(next_ref.dtype)


def update(sums, other, driver, col_energy, row_energy, same, tile_width, width, dtype):
    strips = tile_width // STRIP
    span = width // (STRIP * STRIP)
    return pl.pallas_call(
        functools.partial(update_kernel, strips, STRIP, span),
        out_shape=jax.ShapeDtypeStruct(driver.shape, dtype),
        in_specs=[pl.BlockSpec(memory_space=pltpu.VMEM)] * 6,
        out_specs=pl.BlockSpec(memory_space=pltpu.VMEM),
        compiler_params=pltpu.CompilerParams(vmem_limit_bytes=48 * 2**20),
    )(sums, other, driver, col_energy, row_energy, same)


def body(amplitudes, driver, ladder, block_mask, pair_list, occ_energy, virt_energy):
    ab_count = lax.axis_size("ab")
    ab_index = lax.axis_index("ab")
    cd_index = lax.axis_index("cd")
    rows_dev, cols_dev = amplitudes.shape
    out_rows, in_cols = ladder.shape
    tile_width = NV // ab_count
    tile_area = tile_width * tile_width
    strip = min(STRIP, tile_width)
    strips = tile_width // strip
    diag_cols = sum(strip * (tile_width - s * strip) for s in range(strips))
    width = min(512, tile_area)

    paired = (
        ab_count == 2
        and tile_width % (2 * STRIP) == 0
        and width == 2 * STRIP * STRIP
        and diag_cols == (strips + 1) * width
        and rows_dev % GROUP == 0
        and lax.axis_size("cd") >= 2 * (strips + 1)
        and lax.axis_size("cd") % 8 == 0
        and lax.axis_size("cd").bit_count() == 1
    )
    weights = ladder.reshape(out_rows // BLK, BLK, in_cols // BLK, BLK)
    weights = (weights * block_mask.astype(jnp.bfloat16)[:, None, :, None]).reshape(
        ab_count, tile_width, tile_width, in_cols
    )
    diag_tile = lax.dynamic_index_in_dim(weights, ab_index, 0, keepdims=False)

    def pack(tile):
        return jnp.concatenate(
            [
                tile[s * strip : (s + 1) * strip, s * strip :].reshape(-1, in_cols)
                for s in range(strips)
            ]
        )

    others = [
        lax.dynamic_index_in_dim(
            weights, lax.rem(ab_index + j, ab_count), 0, keepdims=False
        ).reshape(tile_area, in_cols)
        for j in range(1, ab_count)
    ]
    straight = jnp.concatenate([pack(diag_tile)] + others)
    mirrored = pack(jnp.swapaxes(diag_tile, 0, 1))

    pairs_local = ab_index * cols_dev + jnp.arange(cols_dev, dtype=jnp.int32)
    big_a = pairs_local // (tile_width * NV)
    big_b = pairs_local // tile_area % ab_count
    first = big_a * tile_width + pairs_local // tile_width % tile_width
    second = big_b * tile_width + pairs_local % tile_width
    virt_index = jnp.arange(NV, dtype=jnp.int32)
    picks = (first[:, None] == virt_index).astype(jnp.float32) + (
        second[:, None] == virt_index
    ).astype(jnp.float32)
    col_energy = jnp.dot(picks, virt_energy, precision=lax.Precision.HIGHEST)
    row_pairs = lax.dynamic_slice_in_dim(pair_list, cd_index * rows_dev, rows_dev)
    occ_index = jnp.arange(NOCC, dtype=jnp.int32)
    occ_picks = (row_pairs[:, None] // NOCC == occ_index).astype(jnp.float32)
    occ_picks = occ_picks + (row_pairs[:, None] % NOCC == occ_index).astype(jnp.float32)
    row_energy = jnp.dot(occ_picks, occ_energy, precision=lax.Precision.HIGHEST)
    denominator = col_energy[None, :] - row_energy[:, None]

    def swap_matrix(listed):
        diagonal = listed // NOCC == listed % NOCC
        index = jnp.arange(listed.shape[0], dtype=jnp.int32)
        mirror_row = jnp.where(diagonal, index, index ^ 1)
        return (mirror_row[:, None] == index).astype(jnp.bfloat16)

    row_swap = swap_matrix(row_pairs)
    all_swap = swap_matrix(pair_list)

    def spread(packed):
        pieces, start = [], 0
        for s in range(strips):
            wide = tile_width - s * strip
            piece = packed[:, start : start + strip * wide].reshape(rows_dev, strip, wide)
            start += strip * wide
            piece = jnp.concatenate([0.5 * piece[:, :, :strip], piece[:, :, strip:]], axis=2)
            pieces.append(jnp.pad(piece, ((0, 0), (0, 0), (s * strip, 0))))
        return jnp.concatenate(pieces, axis=1).reshape(rows_dev, tile_area)

    diag_rows = (pair_list // NOCC == pair_list % NOCC).astype(jnp.float32)
    diag_rows = jnp.broadcast_to(diag_rows[:, None], (pair_list.shape[0], 128))
    row_same = (row_pairs // NOCC == row_pairs % NOCC).astype(jnp.float32)

    def lanes(values):
        return jnp.broadcast_to(values[:, None], (values.shape[0], 128))

    if paired:
        masks = block_mask.astype(jnp.bfloat16).reshape(ab_count, tile_area // BLK, 1, -1, 1)
        masks = jnp.broadcast_to(
            masks, (ab_count, tile_area // BLK, STRIP, in_cols // BLK, BLK)
        ).reshape(ab_count, tile_area // BLK, STRIP, in_cols)
        tiles_in = ladder.reshape(ab_count, tile_width, tile_width, in_cols)
        first_energy = lax.dynamic_slice_in_dim(virt_energy, ab_index * tile_width, tile_width)
        tile_energy = (
            first_energy[None, :, None] + virt_energy.reshape(ab_count, 1, tile_width)
        ).reshape(1, cols_dev)
        diag_rows = diag_rows.reshape(-1, rows_dev // GROUP, GROUP, 128)
        diag_rows = jnp.swapaxes(diag_rows, 0, 1).reshape(rows_dev // GROUP, -1, 128)
        state = amplitudes
        for step in range(ITERS):
            sums, other = iteration_sums(state, diag_rows, masks, tiles_in, width)
            state = update(
                sums, other, driver, tile_energy, lanes(row_energy), lanes(row_same),
                tile_width, width, jnp.bfloat16 if step < ITERS - 1 else jnp.float32,
            )
        return state

    state = amplitudes
    for step in range(ITERS):
        rounded = state.astype(jnp.bfloat16)
        regrouped = lax.all_to_all(rounded, "cd", split_axis=1, concat_axis=0, tiled=True)
        low = lax.all_gather(regrouped, "ab", axis=1, tiled=True)
        swapped_low = jnp.dot(all_swap, low, preferred_element_type=jnp.float32)
        sums = ladder_sums(
            low, swapped_low.astype(jnp.bfloat16), straight, mirrored, rows_dev, width
        )
        parts = [spread(sums[:, :diag_cols])]
        for j in range(1, ab_count):
            start = diag_cols + (j - 1) * tile_area
            parts.append(sums[:, start : start + tile_area])
        placed = jnp.concatenate(parts, axis=1)
        received = jnp.roll(placed.reshape(rows_dev, ab_count, tile_area), ab_index, axis=1)
        received = received.reshape(rows_dev, cols_dev)
        swapped = jnp.dot(
            row_swap, received.astype(jnp.bfloat16), preferred_element_type=jnp.float32
        )
        tiles = lax.all_to_all(
            swapped.astype(jnp.bfloat16).reshape(rows_dev, ab_count, tile_area),
            "ab",
            split_axis=1,
            concat_axis=1,
            tiled=True,
        )
        symmetric = received + flip_tiles(tiles, tile_width).astype(jnp.float32)
        state = (driver + symmetric) / denominator
    return state


def solution(mesh):
    placed = (P("cd", "ab"), P("cd", "ab"), P("ab", "cd"), P("ab", "cd"), P(), P(), P())
    return jax.shard_map(body, mesh=mesh, in_specs=placed, out_specs=P("cd", "ab"), check_vma=False)
```

```python
import functools

import jax
import jax.numpy as jnp
from jax import lax
from jax.experimental import pallas as pl
from jax.experimental.pallas import tpu as pltpu
from jax.sharding import PartitionSpec as P

NV = 128
NOCC = 32
BLK = 128
ITERS = 2
STRIP = 16
GROUP = 16
MESH = pl.DeviceIdType.MESH
NT = (((1,), (1,)), ((), ()))


def flip_tiles(tiles, tile_width):
    row_count, tile_count = tiles.shape[:2]
    turned = jnp.swapaxes(tiles.reshape(row_count, tile_count, tile_width, tile_width), 2, 3)
    return turned.reshape(row_count, tile_count * tile_width * tile_width)


def bit_of(index, bit):
    return lax.rem(index // (1 << bit), 2)


def flip_bit(index, bit):
    return index + (1 - 2 * bit_of(index, bit)) * (1 << bit)


def ladder_kernel(
    bits, chunks, diag_chunks, width,
    low_ref, swap_ref, straight_ref, mirrored_ref, out_ref,
    straight, mirrored, *rest,
):
    held = rest[: bits + 1]
    load_sem, mirror_sem, send_sem, recv_sem = rest[bits + 1 :]
    ab = lax.axis_index("ab")
    cd = lax.axis_index("cd")
    rows = out_ref.shape[0]
    own = [bit_of(cd, bit) for bit in range(bits)]
    partner = [(ab, flip_bit(cd, bit)) for bit in range(bits)]

    def at(stage, chunk, which):
        lead = (slice(None),) * (bits - 1 - stage)
        return held[stage].at[(chunk,) + lead + (which,)]

    def copy(stage, chunk):
        return pltpu.make_async_remote_copy(
            src_ref=at(stage, chunk, 1 - own[stage]),
            dst_ref=held[stage + 1].at[chunk],
            send_sem=send_sem.at[stage, chunk],
            recv_sem=recv_sem.at[stage, chunk],
            device_id=partner[stage],
            device_id_type=MESH,
        )

    def load_straight(chunk):
        start = pl.multiple_of(chunk * width, width)
        return pltpu.make_async_copy(
            straight_ref.at[pl.ds(start, width)], straight.at[chunk], load_sem.at[chunk]
        )

    def load_mirrored(chunk):
        start = pl.multiple_of(chunk * width, width)
        return pltpu.make_async_copy(
            mirrored_ref.at[pl.ds(start, width)], mirrored.at[chunk], mirror_sem.at[chunk]
        )

    @pl.loop(0, diag_chunks)
    def _(chunk):
        load_straight(chunk).start()
        load_mirrored(chunk).start()

    @pl.loop(diag_chunks, chunks)
    def _(chunk):
        load_straight(chunk).start()

    barrier = pltpu.get_barrier_semaphore()
    for device in partner:
        pl.semaphore_signal(barrier, inc=1, device_id=device, device_id_type=MESH)
    pl.semaphore_wait(barrier, bits)

    def put(chunk, product):
        value = product.astype(jnp.bfloat16)
        for block in range(1 << bits):
            index = tuple((block >> (bits - 1 - axis)) & 1 for axis in range(bits))
            held[0][(chunk,) + index] = value[block * rows : (block + 1) * rows]

    @pl.loop(0, chunks + 2 * bits)
    def _(step):
        @pl.when(step < diag_chunks)
        def _():
            load_straight(step).wait()
            load_mirrored(step).wait()
            total = lax.dot_general(
                low_ref[...], straight[step], NT, preferred_element_type=jnp.float32
            )
            total += lax.dot_general(
                swap_ref[...], mirrored[step], NT, preferred_element_type=jnp.float32
            )
            put(step, total)
            copy(0, step).start()

        @pl.when((step >= diag_chunks) & (step < chunks))
        def _():
            load_straight(step).wait()
            put(
                step,
                lax.dot_general(
                    low_ref[...], straight[step], NT, preferred_element_type=jnp.float32
                ),
            )
            copy(0, step).start()

        for stage in range(bits):
            chunk = step - (2 * stage + 1)

            @pl.when((chunk >= 0) & (chunk < chunks))
            def _():
                copy(stage, chunk).wait_recv()
                mine = at(stage, chunk, own[stage])[...].astype(jnp.float32)
                total = held[stage + 1][chunk].astype(jnp.float32) + mine
                if stage < bits - 1:
                    held[stage + 1][chunk] = total.astype(jnp.bfloat16)
                    copy(stage + 1, chunk).start()
                else:
                    out_ref[:, pl.ds(pl.multiple_of(chunk * width, width), width)] = total

    @pl.loop(0, chunks)
    def _(chunk):
        for stage in range(bits):
            copy(stage, chunk).wait_send()


def ladder_sums(low, swapped, straight, mirrored, rows, width):
    count = low.shape[0] // rows
    bits = count.bit_length() - 1
    depth = low.shape[1]
    chunks = straight.shape[0] // width
    diag_chunks = mirrored.shape[0] // width
    held = [
        pltpu.VMEM((chunks,) + (2,) * (bits - stage) + (rows, width), jnp.bfloat16)
        for stage in range(bits + 1)
    ]
    return pl.pallas_call(
        functools.partial(ladder_kernel, bits, chunks, diag_chunks, width),
        out_shape=jax.ShapeDtypeStruct((rows, chunks * width), jnp.float32),
        in_specs=[pl.BlockSpec(memory_space=pltpu.VMEM)] * 2
        + [pl.BlockSpec(memory_space=pl.ANY)] * 2,
        out_specs=pl.BlockSpec(memory_space=pltpu.VMEM),
        scratch_shapes=[
            pltpu.VMEM((chunks, width, depth), jnp.bfloat16),
            pltpu.VMEM((diag_chunks, width, depth), jnp.bfloat16),
            *held,
            pltpu.SemaphoreType.DMA((chunks,)),
            pltpu.SemaphoreType.DMA((diag_chunks,)),
            pltpu.SemaphoreType.DMA((bits, chunks)),
            pltpu.SemaphoreType.DMA((bits, chunks)),
        ],
        compiler_params=pltpu.CompilerParams(
            collective_id=0, has_side_effects=True, vmem_limit_bytes=58 * 2**20
        ),
    )(low, swapped, straight, mirrored)


def iteration_kernel(
    bits, width, rows, groups,
    state_ref, diagonal_ref, mask_ref, weight_ref, sums_ref, other_ref,
    state, low, straight, mirrored, outer, part, part_y, *rest,
):
    held = (part,) + rest[:bits]
    final, landed = rest[bits : bits + 2]
    (
        load_sem, self_sem, a_send, a_recv, b_send, b_recv,
        core_send, core_recv, y_send, y_recv, send_sem, recv_sem, last_send, last_recv,
    ) = rest[bits + 2 :]
    ab = lax.axis_index("ab")
    cd = lax.axis_index("cd")
    count = 1 << bits
    side = straight.shape[1]
    strips = weight_ref.shape[1] // side
    depth = weight_ref.shape[3]
    piece = depth // 2
    keeps = strips
    span = width // (side * side)
    diags = keeps + 1
    products = 3 * keeps + 1
    finals = diags + keeps
    own = [bit_of(cd, bit) for bit in range(bits)]
    partner = [(ab, flip_bit(cd, bit)) for bit in range(bits)]
    across = (1 - ab, cd)

    def remote(src, dst, send, recv, device):
        return pltpu.make_async_remote_copy(
            src_ref=src, dst_ref=dst, send_sem=send, recv_sem=recv,
            device_id=device, device_id_type=MESH,
        )

    def block_of(tile, x, y):
        return weight_ref.at[
            tile,
            pl.ds(pl.multiple_of(x * side, side), side),
            pl.ds(pl.multiple_of(y * side, side), side),
        ]

    def upper(p):
        starts = [sum(strips - r for r in range(s)) for s in range(strips)]
        x = sum((p >= start).astype(jnp.int32) for start in starts[1:])
        start = sum(
            jnp.where(x == s, starts[s], 0) for s in range(strips)
        )
        return x, p - start + x

    def kept_y(p, which):
        return span * lax.rem(p // (span * span) + which, 2) + lax.rem(p, span)

    @pl.loop(0, diags * span)
    def _(p):
        x, y = upper(p)
        pltpu.make_async_copy(block_of(ab, x, y), straight.at[p], load_sem.at[0]).start()
        pltpu.make_async_copy(block_of(ab, y, x), mirrored.at[p], load_sem.at[1]).start()

    @pl.loop(0, keeps * span)
    def _(p):
        pltpu.make_async_copy(
            block_of(1 - ab, p // span, kept_y(p, ab)), outer.at[0, p], load_sem.at[2]
        ).start()
        pltpu.make_async_copy(
            block_of(1 - ab, kept_y(p, 1 - ab), p // span), outer.at[1, p], load_sem.at[3]
        ).start()

    def masked(block, tile, x):
        pairs = side // 2
        mask = mask_ref[tile, pl.ds(pl.multiple_of(x * pairs, pairs), pairs)]
        value = block.reshape(pairs, 2, side, depth) * mask[:, None]
        return value.reshape(side * side, depth)

    area = side * side
    row_at = lax.broadcasted_iota(jnp.int32, (area, area), 0)
    col_at = lax.broadcasted_iota(jnp.int32, (area, area), 1)
    turn_rows = (row_at == lax.rem(col_at, side) * side + col_at // side).astype(jnp.bfloat16)

    def turned(value):
        product = jnp.dot(turn_rows, value, preferred_element_type=jnp.float32)
        return product.astype(jnp.bfloat16).reshape(side, side, depth)

    def prepare_diag(p):
        x, y = upper(p)
        straight[p] = masked(straight[p], ab, x).reshape(side, side, depth)
        mirrored[p] = turned(masked(mirrored[p], ab, y))

    def prepare_outer(p):
        outer[0, p] = masked(outer[0, p], 1 - ab, p // span).reshape(side, side, depth)
        outer[1, p] = turned(masked(outer[1, p], 1 - ab, kept_y(p, 1 - ab)))

    state[...] = state_ref[...].astype(jnp.bfloat16)
    barrier = pltpu.get_barrier_semaphore()

    @pl.loop(1, count)
    def _(j):
        pl.semaphore_signal(
            barrier, inc=1, device_id=(ab, lax.rem(cd + j, count)), device_id_type=MESH
        )

    pl.semaphore_signal(barrier, inc=1, device_id=across, device_id_type=MESH)
    pl.semaphore_wait(barrier, count)

    def rows_of(source):
        return pl.ds(pl.multiple_of(source * rows, rows), rows)

    def cols_of(side):
        return pl.ds(pl.multiple_of(side * piece, piece), piece)

    def scatter(group, target, source):
        return remote(
            state.at[rows_of(group), cols_of(target)],
            low.at[0, group, rows_of(source), cols_of(ab)],
            a_send.at[group, target], a_recv.at[group, source], (ab, target),
        )

    def stay(group):
        return pltpu.make_async_copy(
            state.at[rows_of(group), cols_of(cd)],
            low.at[0, group, rows_of(cd), cols_of(ab)],
            self_sem.at[group],
        )

    def forward(group, source, side):
        block = low.at[0, group, rows_of(source), cols_of(side)]
        return remote(block, block, b_send.at[group, source], b_recv.at[group, source], across)

    def other(j):
        return sum(
            lax.rem(own[bit] + bit_of(j, bit), 2) * (1 << bit) for bit in range(bits)
        )

    odd = lax.rem(lax.broadcasted_iota(jnp.int32, (rows, 128), 0), 2) == 1

    def pass_on(group, i):
        @pl.when(i == 0)
        def _():
            stay(group).wait()
            forward(group, cd, ab).start()

        @pl.when(i != 0)
        def _():
            source = other(i)
            scatter(group, cd, source).wait_recv()
            forward(group, source, ab).start()

    def take_in(group, i):
        source = other(i)
        forward(group, source, 1 - ab).wait_recv()
        at = rows_of(source)
        same = diagonal_ref[group, at, :] != 0
        for lane in range(0, depth, 128):
            value = low[0, group, at, lane : lane + 128].astype(jnp.float32)
            mate = jnp.where(odd, pltpu.roll(value, 1, 0), pltpu.roll(value, rows - 1, 0))
            value = jnp.where(same, value, mate)
            low[1, group, at, lane : lane + 128] = value.astype(jnp.bfloat16)

    def send_group(group):
        stay(group).start()

        @pl.loop(1, count)
        def _(i):
            scatter(group, other(i), cd).start()

    send_group(0)

    @pl.loop(0, count)
    def _(i):
        pass_on(0, i)

        if groups > 1:
            @pl.when(i == count - 4)
            def _():
                send_group(1)

        @pl.when(i == 0)
        def _():
            pltpu.make_async_copy(straight, straight, load_sem.at[0]).wait()
            pltpu.make_async_copy(mirrored, mirrored, load_sem.at[1]).wait()

        @pl.when(i < diags * span)
        def _():
            prepare_diag(i)

        late = i - (count - keeps * span)

        @pl.when(late == 0)
        def _():
            pltpu.make_async_copy(outer.at[0], outer.at[0], load_sem.at[2]).wait()
            pltpu.make_async_copy(outer.at[1], outer.at[1], load_sem.at[3]).wait()

        @pl.when(late >= 0)
        def _():
            prepare_outer(late)

    @pl.loop(0, count)
    def _(i):
        take_in(0, i)

    def at(stage, index, which):
        lead = (slice(None),) * (bits - 1 - stage)
        return held[stage].at[(index,) + lead + (which,)]

    def place(q):
        inside = lax.rem(q, finals)
        turn = inside // 2
        diag = jnp.where(turn == keeps, 3 * keeps, 3 * turn + 1)
        return q // finals * products + jnp.where(lax.rem(inside, 2) == 0, diag, 3 * turn + 2)

    def core_copy(u):
        return remote(
            at(0, u, 1 - own[0]), held[1].at[u], core_send.at[u], core_recv.at[u], partner[0]
        )

    def y_copy(j):
        sent = j // keeps * products + 3 * lax.rem(j, keeps)
        return remote(held[1].at[sent], part_y.at[j], y_send.at[j], y_recv.at[j], across)

    def stage_copy(stage, q):
        source = at(1, place(q), 1 - own[1]) if stage == 1 else at(stage, q, 1 - own[stage])
        return remote(
            source, held[stage + 1].at[q],
            send_sem.at[stage - 1, q], recv_sem.at[stage - 1, q], partner[stage],
        )

    def last_copy(j):
        return remote(final.at[j], landed.at[j], last_send.at[j], last_recv.at[j], across)

    def put(u, product):
        value = product.astype(jnp.bfloat16)
        for block in range(count):
            index = tuple((block >> (bits - 1 - axis)) & 1 for axis in range(bits))
            part[(u,) + index] = value[block * rows : (block + 1) * rows]

    def rows_at(start):
        return pl.ds(pl.multiple_of(start, width), width)

    def blocks_at(turn):
        return pl.ds(turn * span, span)

    def dot(left, right):
        return lax.dot_general(left, right, NT, preferred_element_type=jnp.float32)

    y_lag = 7
    lags = [10 + 3 * stage for stage in range(bits - 1)]
    sources = count // 8

    @pl.loop(0, (products * (groups * finals - 1)) // finals + lags[-1] + 1)
    def _(step):
        group = step // products
        turn = lax.rem(step, products) // 3
        kind = lax.rem(lax.rem(step, products), 3)
        last = lax.rem(step, products) == 3 * keeps

        @pl.when((group < groups) & ((kind == 1) | last))
        def _():
            total = dot(low[0, group], straight[blocks_at(turn)].reshape(width, depth))
            total += dot(low[1, group], mirrored[blocks_at(turn)].reshape(width, depth))
            put(step, total)
            core_copy(step).start()

        @pl.when((group < groups) & (kind != 1) & ~last)
        def _():
            sent = 1 - kind // 2
            right = outer[sent, blocks_at(turn)].reshape(width, depth)
            put(step, dot(low[sent, group], right))
            core_copy(step).start()

        u = step - 1

        @pl.when((u >= 0) & (u < groups * products))
        def _():
            core_copy(u).wait_recv()
            held[1][u] = held[1][u] + at(0, u, own[0])[...]
            u_group = u // products
            u_step = lax.rem(u, products)
            u_kind = lax.rem(u_step, 3)

            @pl.when((u_kind == 1) | (u_step == 3 * keeps))
            def _():
                stage_copy(1, u_group * finals + 2 * (u_step // 3)).start()

            @pl.when((u_kind == 0) & (u_step < 3 * keeps))
            def _():
                y_copy(u_group * keeps + u_step // 3).start()

        arriving = lax.rem(step, products)

        @pl.when((group + 2 < groups) & (arriving == 9))
        def _():
            send_group(group + 2)

        @pl.when((group + 1 < groups) & (arriving >= 0) & (arriving < 8))
        def _():
            for i in range(sources):
                pass_on(group + 1, (arriving - 0) * sources + i)

        @pl.when((group + 1 < groups) & (arriving >= 9) & (arriving < 13))
        def _():
            for i in range(2 * sources):
                take_in(group + 1, (arriving - 9) * 2 * sources + i)

        v = step - y_lag
        v_step = lax.rem(v + products, products)

        @pl.when(
            (v >= 0) & (v < groups * products) & (lax.rem(v_step, 3) == 0) & (v_step < 3 * keeps)
        )
        def _():
            j = v_step // 3
            y_copy(v // products * keeps + j).wait_recv()
            held[1][v + 2] = held[1][v + 2] + part_y[v // products * keeps + j]
            stage_copy(1, v // products * finals + 2 * j + 1).start()

        for stage in range(1, bits):
            w = step - lags[stage - 1]
            q = (finals * w + products - 1) // products

            @pl.when((w >= 0) & ((products * q) // finals == w) & (q < groups * finals))
            def _():
                stage_copy(stage, q).wait_recv()
                index = place(q) if stage == 1 else q
                mine = at(stage, index, own[stage])[...]
                if stage < bits - 1:
                    held[stage + 1][q] = held[stage + 1][q] + mine
                    stage_copy(stage + 1, q).start()
                else:
                    total = held[stage + 1][q].astype(jnp.float32) + mine.astype(jnp.float32)
                    inside = lax.rem(q, finals)
                    kept = lax.rem(inside, 2) == 1
                    start = jnp.where(kept, diags + inside // 2, inside // 2) * width
                    sums_ref[rows_of(q // finals), rows_at(start)] = total

                    @pl.when(kept)
                    def _():
                        j = q // finals * keeps + inside // 2
                        final[j] = total.astype(jnp.bfloat16)
                        last_copy(j).start()

    @pl.loop(0, groups)
    def _(group):
        for j in range(keeps):
            last_copy(group * keeps + j).wait_recv()
            other_ref[rows_of(group), j * width : (j + 1) * width] = landed[group * keeps + j]

    @pl.loop(0, groups)
    def _(group):
        @pl.loop(0, count)
        def _(i):
            @pl.when(i != cd)
            def _():
                scatter(group, i, cd).wait_send()

            forward(group, i, ab).wait_send()

    @pl.loop(0, groups * products)
    def _(u):
        core_copy(u).wait_send()

    @pl.loop(0, groups * keeps)
    def _(j):
        y_copy(j).wait_send()
        last_copy(j).wait_send()

    @pl.loop(0, groups * finals)
    def _(q):
        for stage in range(1, bits):
            stage_copy(stage, q).wait_send()


def iteration_sums(state, diagonal, mask, weights, width):
    rows = state.shape[0]
    groups = rows // GROUP
    count = diagonal.shape[1] // GROUP
    bits = count.bit_length() - 1
    tile_width, depth = weights.shape[1], weights.shape[3]
    keeps = tile_width // STRIP
    diags = keeps + 1
    span = width // (STRIP * STRIP)
    products, finals = 3 * keeps + 1, 2 * keeps + 1
    dma = pltpu.SemaphoreType.DMA
    block = (GROUP, width)
    square = (STRIP, STRIP, depth)
    return pl.pallas_call(
        functools.partial(iteration_kernel, bits, width, GROUP, groups),
        out_shape=(
            jax.ShapeDtypeStruct((rows, finals * width), jnp.float32),
            jax.ShapeDtypeStruct((rows, keeps * width), jnp.bfloat16),
        ),
        in_specs=[pl.BlockSpec(memory_space=pltpu.VMEM)] * 3
        + [pl.BlockSpec(memory_space=pl.ANY)],
        out_specs=[pl.BlockSpec(memory_space=pltpu.VMEM)] * 2,
        scratch_shapes=[
            pltpu.VMEM(state.shape, jnp.bfloat16),
            pltpu.VMEM((2, groups, count * GROUP, depth), jnp.bfloat16),
            pltpu.VMEM((diags * span,) + square, jnp.bfloat16),
            pltpu.VMEM((diags * span,) + square, jnp.bfloat16),
            pltpu.VMEM((2, keeps * span) + square, jnp.bfloat16),
            pltpu.VMEM((groups * products,) + (2,) * bits + block, jnp.bfloat16),
            pltpu.VMEM((groups * keeps,) + (2,) * (bits - 1) + block, jnp.bfloat16),
            pltpu.VMEM((groups * products,) + (2,) * (bits - 1) + block, jnp.bfloat16),
            *[
                pltpu.VMEM((groups * finals,) + (2,) * (bits - 1 - s) + block, jnp.bfloat16)
                for s in range(1, bits)
            ],
            pltpu.VMEM((groups * keeps,) + block, jnp.bfloat16),
            pltpu.VMEM((groups * keeps,) + block, jnp.bfloat16),
            dma((4,)), dma((groups,)),
            *[dma((groups, count))] * 4,
            *[dma((groups * products,))] * 2,
            *[dma((groups * keeps,))] * 2,
            *[dma((bits - 1, groups * finals))] * 2,
            *[dma((groups * keeps,))] * 2,
        ],
        compiler_params=pltpu.CompilerParams(
            collective_id=1 if state.dtype == jnp.bfloat16 else 2,
            has_side_effects=True,
            vmem_limit_bytes=60 * 2**20,
        ),
    )(state, diagonal, mask, weights)


def update_kernel(
    strips, side, span,
    sums_ref, other_ref, driver_ref, cols_ref, rows_ref, same_ref, next_ref,
):
    ab = lax.axis_index("ab")
    rows = driver_ref.shape[0]
    area = side * side
    wide = strips * area
    tile_area = strips * wide
    uppers = [(x, y) for x in range(strips) for y in range(x, strips)]

    def iotas(size):
        return (lax.broadcasted_iota(jnp.int32, (size, size), axis) for axis in (0, 1))

    start, end = iotas(area)
    turn = (start == lax.rem(end, side) * side + end // side).astype(jnp.bfloat16)
    start, end = iotas(wide)
    block, inner = lax.rem(end, strips * side) // side, lax.rem(end, side)
    ordered = start == block * area + end // (strips * side) * side + inner
    ordered = ordered.astype(jnp.bfloat16)
    odd = lax.rem(lax.broadcasted_iota(jnp.int32, (rows, area), 0), 2) == 1
    same = jnp.broadcast_to(same_ref[:, 0:1], (rows, area)) != 0

    def swap(value):
        return jnp.where(
            same, value, jnp.where(odd, pltpu.roll(value, 1, 0), pltpu.roll(value, rows - 1, 0))
        )

    def sums_of(index):
        return sums_ref[:, index * area : (index + 1) * area]

    def exact_dot(value, right):
        high = value.astype(jnp.bfloat16)
        rest = (value - high.astype(jnp.float32)).astype(jnp.bfloat16)
        return jnp.dot(high, right, preferred_element_type=jnp.float32) + jnp.dot(
            rest, right, preferred_element_type=jnp.float32
        )

    lower = [swap(sums_of(p)) for p, (x, y) in enumerate(uppers) if x < y]
    turned = exact_dot(jnp.concatenate(lower), turn)
    diag, taken = {}, 0
    for p, (x, y) in enumerate(uppers):
        diag[x, y] = sums_of(p)
        if x < y:
            diag[y, x] = turned[taken * rows : (taken + 1) * rows]
            taken += 1
    came = [
        swap(other_ref[:, p * area : (p + 1) * area].astype(jnp.float32))
        for p in range(strips * span)
    ]
    came = jnp.dot(
        jnp.concatenate(came).astype(jnp.bfloat16), turn, preferred_element_type=jnp.float32
    )
    even = ab == 0
    off = {}
    for x in range(strips):
        for y in range(strips):
            kept = sums_of(len(uppers) + x * span + y % span)
            p = y * span + x % span
            sent = came[p * rows : (p + 1) * rows]
            if x // span == y // span:
                off[x, y] = jnp.where(even, kept, sent)
            else:
                off[x, y] = jnp.where(even, sent, kept)
    for tile, blocks in ((ab, diag), (1 - ab, off)):
        for x in range(strips):
            line = jnp.concatenate([blocks[x, y] for y in range(strips)], axis=1)
            symmetric = exact_dot(line, ordered)
            at = pl.ds(pl.multiple_of(tile * tile_area + x * wide, wide), wide)
            below = cols_ref[:, at] - rows_ref[:, 0:1]
            next_ref[:, at] = ((driver_ref[:, at] + symmetric) / below).astype(next_ref.dtype)


def update(sums, other, driver, col_energy, row_energy, same, tile_width, width, dtype):
    strips = tile_width // STRIP
    span = width // (STRIP * STRIP)
    return pl.pallas_call(
        functools.partial(update_kernel, strips, STRIP, span),
        out_shape=jax.ShapeDtypeStruct(driver.shape, dtype),
        in_specs=[pl.BlockSpec(memory_space=pltpu.VMEM)] * 6,
        out_specs=pl.BlockSpec(memory_space=pltpu.VMEM),
        compiler_params=pltpu.CompilerParams(vmem_limit_bytes=48 * 2**20),
    )(sums, other, driver, col_energy, row_energy, same)


def body(amplitudes, driver, ladder, block_mask, pair_list, occ_energy, virt_energy):
    ab_count = lax.axis_size("ab")
    ab_index = lax.axis_index("ab")
    cd_index = lax.axis_index("cd")
    rows_dev, cols_dev = amplitudes.shape
    out_rows, in_cols = ladder.shape
    tile_width = NV // ab_count
    tile_area = tile_width * tile_width
    strip = min(STRIP, tile_width)
    strips = tile_width // strip
    diag_cols = sum(strip * (tile_width - s * strip) for s in range(strips))
    width = min(512, tile_area)

    paired = (
        ab_count == 2
        and tile_width % (2 * STRIP) == 0
        and width == 2 * STRIP * STRIP
        and diag_cols == (strips + 1) * width
        and rows_dev % GROUP == 0
        and lax.axis_size("cd") >= 2 * (strips + 1)
        and lax.axis_size("cd") % 8 == 0
        and lax.axis_size("cd").bit_count() == 1
    )
    weights = ladder.reshape(out_rows // BLK, BLK, in_cols // BLK, BLK)
    weights = (weights * block_mask.astype(jnp.bfloat16)[:, None, :, None]).reshape(
        ab_count, tile_width, tile_width, in_cols
    )
    diag_tile = lax.dynamic_index_in_dim(weights, ab_index, 0, keepdims=False)

    def pack(tile):
        return jnp.concatenate(
            [
                tile[s * strip : (s + 1) * strip, s * strip :].reshape(-1, in_cols)
                for s in range(strips)
            ]
        )

    others = [
        lax.dynamic_index_in_dim(
            weights, lax.rem(ab_index + j, ab_count), 0, keepdims=False
        ).reshape(tile_area, in_cols)
        for j in range(1, ab_count)
    ]
    straight = jnp.concatenate([pack(diag_tile)] + others)
    mirrored = pack(jnp.swapaxes(diag_tile, 0, 1))

    pairs_local = ab_index * cols_dev + jnp.arange(cols_dev, dtype=jnp.int32)
    big_a = pairs_local // (tile_width * NV)
    big_b = pairs_local // tile_area % ab_count
    first = big_a * tile_width + pairs_local // tile_width % tile_width
    second = big_b * tile_width + pairs_local % tile_width
    virt_index = jnp.arange(NV, dtype=jnp.int32)
    picks = (first[:, None] == virt_index).astype(jnp.float32) + (
        second[:, None] == virt_index
    ).astype(jnp.float32)
    col_energy = jnp.dot(picks, virt_energy, precision=lax.Precision.HIGHEST)
    row_pairs = lax.dynamic_slice_in_dim(pair_list, cd_index * rows_dev, rows_dev)
    occ_index = jnp.arange(NOCC, dtype=jnp.int32)
    occ_picks = (row_pairs[:, None] // NOCC == occ_index).astype(jnp.float32)
    occ_picks = occ_picks + (row_pairs[:, None] % NOCC == occ_index).astype(jnp.float32)
    row_energy = jnp.dot(occ_picks, occ_energy, precision=lax.Precision.HIGHEST)
    denominator = col_energy[None, :] - row_energy[:, None]

    def swap_matrix(listed):
        diagonal = listed // NOCC == listed % NOCC
        index = jnp.arange(listed.shape[0], dtype=jnp.int32)
        mirror_row = jnp.where(diagonal, index, index ^ 1)
        return (mirror_row[:, None] == index).astype(jnp.bfloat16)

    row_swap = swap_matrix(row_pairs)
    all_swap = swap_matrix(pair_list)

    def spread(packed):
        pieces, start = [], 0
        for s in range(strips):
            wide = tile_width - s * strip
            piece = packed[:, start : start + strip * wide].reshape(rows_dev, strip, wide)
            start += strip * wide
            piece = jnp.concatenate([0.5 * piece[:, :, :strip], piece[:, :, strip:]], axis=2)
            pieces.append(jnp.pad(piece, ((0, 0), (0, 0), (s * strip, 0))))
        return jnp.concatenate(pieces, axis=1).reshape(rows_dev, tile_area)

    diag_rows = (pair_list // NOCC == pair_list % NOCC).astype(jnp.float32)
    diag_rows = jnp.broadcast_to(diag_rows[:, None], (pair_list.shape[0], 128))
    row_same = (row_pairs // NOCC == row_pairs % NOCC).astype(jnp.float32)

    def lanes(values):
        return jnp.broadcast_to(values[:, None], (values.shape[0], 128))

    if paired:
        masks = block_mask.astype(jnp.bfloat16).reshape(ab_count, tile_area // BLK, 1, -1, 1)
        masks = jnp.broadcast_to(
            masks, (ab_count, tile_area // BLK, STRIP, in_cols // BLK, BLK)
        ).reshape(ab_count, tile_area // BLK, STRIP, in_cols)
        tiles_in = ladder.reshape(ab_count, tile_width, tile_width, in_cols)
        first_energy = lax.dynamic_slice_in_dim(virt_energy, ab_index * tile_width, tile_width)
        tile_energy = (
            first_energy[None, :, None] + virt_energy.reshape(ab_count, 1, tile_width)
        ).reshape(1, cols_dev)
        diag_rows = diag_rows.reshape(-1, rows_dev // GROUP, GROUP, 128)
        diag_rows = jnp.swapaxes(diag_rows, 0, 1).reshape(rows_dev // GROUP, -1, 128)
        state = amplitudes
        for step in range(ITERS):
            sums, other = iteration_sums(state, diag_rows, masks, tiles_in, width)
            state = update(
                sums, other, driver, tile_energy, lanes(row_energy), lanes(row_same),
                tile_width, width, jnp.bfloat16 if step < ITERS - 1 else jnp.float32,
            )
        return state

    state = amplitudes
    for step in range(ITERS):
        rounded = state.astype(jnp.bfloat16)
        regrouped = lax.all_to_all(rounded, "cd", split_axis=1, concat_axis=0, tiled=True)
        low = lax.all_gather(regrouped, "ab", axis=1, tiled=True)
        swapped_low = jnp.dot(all_swap, low, preferred_element_type=jnp.float32)
        sums = ladder_sums(
            low, swapped_low.astype(jnp.bfloat16), straight, mirrored, rows_dev, width
        )
        parts = [spread(sums[:, :diag_cols])]
        for j in range(1, ab_count):
            start = diag_cols + (j - 1) * tile_area
            parts.append(sums[:, start : start + tile_area])
        placed = jnp.concatenate(parts, axis=1)
        received = jnp.roll(placed.reshape(rows_dev, ab_count, tile_area), ab_index, axis=1)
        received = received.reshape(rows_dev, cols_dev)
        swapped = jnp.dot(
            row_swap, received.astype(jnp.bfloat16), preferred_element_type=jnp.float32
        )
        tiles = lax.all_to_all(
            swapped.astype(jnp.bfloat16).reshape(rows_dev, ab_count, tile_area),
            "ab",
            split_axis=1,
            concat_axis=1,
            tiled=True,
        )
        symmetric = received + flip_tiles(tiles, tile_width).astype(jnp.float32)
        state = (driver + symmetric) / denominator
    return state


def solution(mesh):
    placed = (P("cd", "ab"), P("cd", "ab"), P("ab", "cd"), P("ab", "cd"), P(), P(), P())
    return jax.shard_map(body, mesh=mesh, in_specs=placed, out_specs=P("cd", "ab"), check_vma=False)
```
